128 devices in a mesh: shard: 16 (over z, x), context: 4 (over y), tensor: 2 (over core).
Axes of the slice: x: 4, y: 4, z: 4, core: 2. Of those that a mesh axis runs over, the one named last changes fastest.
Arguments:
- inputs: float32 [32, 512, 768], P('shard', 'context'), may hold values from -6 to 6
- segment_ids: int32 [32, 512], P('shard', 'context'), may hold values from 0 to 3, never falling along the last dimension, each value on 1 to 256 neighbouring positions
- projection: bfloat16 [2, 3, 768, 768], P(None, None, 'shard', 'tensor'), may hold values from -1 to 1
- head_bias: bfloat16 [2, 2, 12, 64], P(None, None, 'tensor', 'shard'), may hold values from -3 to 3
- mixing: bfloat16 [2, 768, 768], P(None, 'tensor', 'shard'), may hold values from -0.875 to 0.875
- expansion: bfloat16 [2, 768, 3072], P(None, 'shard', 'tensor'), may hold values from -0.21875 to 0.21875
- hidden_bias: bfloat16 [2, 48, 64], P(None, 'tensor', 'shard'), may hold values from -3 to 3
- contraction: bfloat16 [2, 3072, 768], P(None, 'tensor', 'shard'), may hold values from -0.109375 to 0.109375
- norm_gains: bfloat16 [2, 2, 768], P(None, None, 'shard'), may hold values from 0.3984375 to 1.59375
- offsets: bfloat16 [2, 4, 768], P(None, None, 'shard'), may hold values from -2 to 2
- cotangent: float32 [32, 512, 768], P('shard', 'context'), may hold values from -6 to 6
Outputs:
- outputs: float32 [32, 512, 768], P('shard', 'context')
- input_grad: float32 [32, 512, 768], P('shard', 'context')
- grad_projection: float32 [2, 3, 768, 768], P(None, None, 'shard', 'tensor')
- head_grad: float32 [2, 2, 12, 64], P(None, None, 'tensor', 'shard')
- grad_mixing: float32 [2, 768, 768], P(None, 'tensor', 'shard')
- grad_expansion: float32 [2, 768, 3072], P(None, 'shard', 'tensor')
- hidden_grad: float32 [2, 48, 64], P(None, 'tensor', 'shard')
- grad_contraction: float32 [2, 3072, 768], P(None, 'tensor', 'shard')
- gains_grad: float32 [2, 2, 768], P(None, None, 'shard')
- grad_offsets: float32 [2, 4, 768], P(None, None, 'shard')
The draws below stay inside these ranges and needn't reach their ends.
Inputs may be any that keep to these rules, and one draw needn't show every extreme that they name: `segment_ids`: within a row ids never fall; every document holds 1 to 256 positions and in every row some document holds exactly 256.
All inputs are finite; a program needn't handle non-finite values.
Results may differ from the reference program's by a relative error of at most 0.033.
Values may be sent and summed in bfloat16 or wider, within the bound.
No kernel may reach another device: no remote copies, remote signals or barrier semaphores. Data moves between devices by JAX's collectives and lax.ppermute only.
A program may use at most 128 MiB of HBM per device.

```python
import math
import jax
import jax.numpy as jnp
import numpy as np
from jax import lax

D = 768
HEADS = 12
HEAD = 64
FF = 3072
LAYERS = 2
ROW_TOK = 512
ROWS = 32
MAX_DOC = 256
SEGS = 4


def draw_projection(key, part):
    scale_base = 1.0 / math.sqrt(D)
    first_key = jax.random.fold_in(key, 0)
    drawn = scale_base * jnp.clip(jax.random.normal(first_key, (LAYERS, 3, D, D), jnp.float32), -6.0, 6.0)
    return jnp.clip(drawn, -1.0, 1.0).astype(jnp.bfloat16)


def level_of(own_key, extent, pieces, least, top_value):
    loudness, own = 1.0, jax.random.fold_in(own_key, 6)
    for dim, shards_of in pieces:
        draws = jnp.exp(jax.random.uniform(jax.random.fold_in(own, dim), (shards_of,), jnp.float32, least / len(pieces), top_value / len(pieces)))
        loudness = loudness * jnp.repeat(draws, extent[dim] // shards_of).reshape([-1 if axis == dim else 1 for axis in range(len(extent))])
    return loudness


def split_up(number_of, total, most, slope):
    weights = [(1 << 20) // math.isqrt(grade ** slope) + 1 for grade in range(2, number_of + 1)]
    rest, holding = total - most - (number_of - 1), [1] * (number_of - 1)
    while rest > 0:
        movable = [i for i in range(number_of - 1) if holding[i] < most]
        pool, budget = sum([weights[i] for i in movable]), rest
        for i in movable:
            addition = min(most - holding[i], max(1, budget * weights[i] // pool), rest)
            holding[i] = holding[i] + addition
            rest = rest - addition
    return np.array([most] + holding)


def ragged(own_key, amount, total, most, slope):
    if amount == 2:
        one = jax.random.randint(own_key, (), max(1, total - most), min(most, total - 1) + 1)
        return jnp.stack([one, total - one])
    tallies = jnp.asarray(split_up(amount, total, most, slope), jnp.int32)
    couples = (amount - 1) // 2
    source_of, receiver = tallies[1:1 + 2 * couples:2], tallies[2:2 + 2 * couples:2]
    margin = jnp.minimum(source_of - 1, most - receiver)
    shifted = jax.random.randint(jax.random.fold_in(own_key, 1), (couples,), 0, 1 << 20) % (margin + 1)
    tallies = tallies.at[1:1 + 2 * couples:2].set(source_of - shifted).at[2:2 + 2 * couples:2].set(receiver + shifted)
    return tallies[jax.random.permutation(jax.random.fold_in(own_key, 2), amount)]


def normal_values(rng, shape, scale, most, cuts=(), held_as=jnp.bfloat16):
    entries = scale * jax.random.normal(rng, shape, jnp.float32)
    if cuts:
        entries = entries * level_of(rng, shape, cuts, -0.22, 0.18)
    return jnp.clip(entries, -most, most).astype(held_as)


def setup_inputs(seed: int = 0) -> dict:
    seeds = jax.random.split(jax.random.key(seed), 12)
    inputs = normal_values(seeds[0], (ROWS, ROW_TOK, D), 1.0, 6.0, ((0, 16), (1, 4)), jnp.float32)
    segment_ids = jax.vmap(lambda own: jnp.searchsorted(jnp.cumsum(ragged(own, SEGS, ROW_TOK, MAX_DOC, 1)), jnp.arange(ROW_TOK), side="right"))(jax.random.split(seeds[1], ROWS)).reshape((ROWS, ROW_TOK)).astype(jnp.int32)
    projection = draw_projection(jax.random.fold_in(seeds[11], 71), 0)
    head_bias = normal_values(seeds[3], (LAYERS, 2, HEADS, HEAD), 0.5, 3.0, ((2, 2), (3, 16)))
    mixing = normal_values(seeds[4], (LAYERS, D, D), (D // 16) ** -0.5, 0.875, ((1, 2), (2, 16)))
    expansion = normal_values(seeds[5], (LAYERS, D, FF), D ** -0.5, 0.21875, ((1, 16), (2, 2)))
    hidden_bias = normal_values(seeds[6], (LAYERS, FF // HEAD, HEAD), 0.5, 3.0, ((1, 2), (2, 16)))
    contraction = normal_values(seeds[7], (LAYERS, FF, D), FF ** -0.5, 0.109375, ((1, 2), (2, 16)))
    norm_gains = jnp.clip(1.0 + 0.12 * jax.random.normal(seeds[8], (LAYERS, 2, D), jnp.float32), 0.3984375, 1.59375).astype(jnp.bfloat16)
    offsets = normal_values(seeds[9], (LAYERS, 4, D), 0.3, 2.0, ((2, 16),))
    cotangent = normal_values(seeds[10], (ROWS, ROW_TOK, D), 1.0, 6.0, ((0, 16), (1, 4)), jnp.float32)
    return {"inputs": inputs, "segment_ids": segment_ids, "projection": projection, "head_bias": head_bias, "mixing": mixing, "expansion": expansion, "hidden_bias": hidden_bias, "contraction": contraction, "norm_gains": norm_gains, "offsets": offsets, "cotangent": cotangent}


EPS = 1e-05
GELU_COEF = 0.7978845608028654
GELU_CUBE = 0.044715
MASKED = -1e+30

def gelu_value(preact):
    inner_arg = GELU_COEF * (preact + GELU_CUBE * preact * preact * preact)
    return 0.5 * preact * (1.0 + jnp.tanh(inner_arg))

def gelu_slope(preact):
    inner_arg = GELU_COEF * (preact + GELU_CUBE * preact * preact * preact)
    tanh_value = jnp.tanh(inner_arg)
    return 0.5 * (1.0 + tanh_value) + 0.5 * preact * (1.0 - tanh_value * tanh_value) * GELU_COEF * (1.0 + 3.0 * GELU_CUBE * preact * preact)

def norm_forward(stream):
    center = stream - lax.optimization_barrier(jnp.mean(stream, axis=-1, keepdims=True))
    spread = lax.rsqrt(lax.optimization_barrier(jnp.mean(center * center, axis=-1, keepdims=True)) + EPS)
    return (center * spread, spread)

def norm_backward(upstream, normed, spread, gain_row):
    scaled = upstream * gain_row
    first_mean = lax.optimization_barrier(jnp.mean(scaled, axis=-1, keepdims=True))
    second_mean = lax.optimization_barrier(jnp.mean(scaled * normed, axis=-1, keepdims=True))
    return spread * (scaled - first_mean - normed * second_mean)

def widened(values):
    return lax.optimization_barrier(values).astype(jnp.float32)

def reference(inputs, segment_ids, projection, head_bias, mixing, expansion, hidden_bias, contraction, norm_gains, offsets, cotangent):
    gain_table = norm_gains.astype(jnp.float32)
    offset_table = offsets.astype(jnp.float32)
    head_table = head_bias.astype(jnp.float32).reshape(LAYERS, 2, D)
    hidden_table = hidden_bias.astype(jnp.float32).reshape(LAYERS, FF)
    head_scale = HEAD ** (-0.5)
    positions = jnp.arange(ROW_TOK, dtype=jnp.int32)

    def one_row(totals, row_data):
        row_input, row_segments, row_cotangent = row_data
        visible = (row_segments[None, :] == row_segments[:, None]) & (positions[None, :] <= positions[:, None])
        stream = row_input
        kept_state = []
        for layer_index in range(LAYERS):
            normed_one, spread_one = norm_forward(stream)
            attend_input = (normed_one * gain_table[layer_index, 0] + offset_table[layer_index, 0]).astype(jnp.bfloat16)
            projected = [jnp.dot(attend_input, projection[layer_index, slot], preferred_element_type=jnp.float32) for slot in range(3)]
            query_rows = (projected[0] + head_table[layer_index, 0]).astype(jnp.bfloat16)
            key_rows = projected[1].astype(jnp.bfloat16)
            value_rows = (projected[2] + head_table[layer_index, 1]).astype(jnp.bfloat16)
            query_heads = widened(query_rows).reshape(ROW_TOK, HEADS, HEAD)
            key_heads = widened(key_rows).reshape(ROW_TOK, HEADS, HEAD)
            value_heads = widened(value_rows).reshape(ROW_TOK, HEADS, HEAD)
            masked = jnp.where(visible[None], jnp.einsum('qhe,khe->hqk', query_heads, key_heads) * head_scale, MASKED)
            row_top = lax.optimization_barrier(jnp.max(masked, axis=-1, keepdims=True))
            log_total = row_top + jnp.log(lax.optimization_barrier(jnp.sum(jnp.exp(masked - row_top), axis=-1, keepdims=True)))
            soft_half = jnp.exp(masked - log_total).astype(jnp.bfloat16)
            attended = jnp.einsum('hqk,khe->qhe', widened(soft_half), value_heads).astype(jnp.bfloat16).reshape(ROW_TOK, D)
            middle = stream + jnp.dot(attended, mixing[layer_index], preferred_element_type=jnp.float32) + offset_table[layer_index, 2]
            normed_two, spread_two = norm_forward(middle)
            feed_input = (normed_two * gain_table[layer_index, 1] + offset_table[layer_index, 1]).astype(jnp.bfloat16)
            preact = jnp.dot(feed_input, expansion[layer_index], preferred_element_type=jnp.float32) + hidden_table[layer_index]
            activation = gelu_value(preact).astype(jnp.bfloat16)
            stream = middle + jnp.dot(activation, contraction[layer_index], preferred_element_type=jnp.float32) + offset_table[layer_index, 3]
            kept_state.append((normed_one, spread_one, attend_input, query_heads, key_heads, value_heads, log_total, attended, normed_two, spread_two, feed_input, preact, activation))
        row_output = stream
        upstream = row_cotangent
        running_totals = list(totals)
        for layer_index in reversed(range(LAYERS)):
            normed_one, spread_one, attend_input, query_heads, key_heads, value_heads, log_total, attended, normed_two, spread_two, feed_input, preact, activation = kept_state[layer_index]
            upstream_half = upstream.astype(jnp.bfloat16)
            contraction_part = jnp.dot(activation.T, upstream_half, preferred_element_type=jnp.float32)
            offset_down = lax.optimization_barrier(jnp.sum(upstream, axis=0))
            hidden_back = jnp.dot(upstream_half, contraction[layer_index].T, preferred_element_type=jnp.float32) * gelu_slope(preact)
            hidden_half = hidden_back.astype(jnp.bfloat16)
            hidden_part = lax.optimization_barrier(jnp.sum(hidden_back, axis=0)).reshape(FF // HEAD, HEAD)
            expansion_part = jnp.dot(feed_input.T, hidden_half, preferred_element_type=jnp.float32)
            feed_back = jnp.dot(hidden_half, expansion[layer_index].T, preferred_element_type=jnp.float32)
            gain_two = lax.optimization_barrier(jnp.sum(feed_back * normed_two, axis=0))
            offset_two = lax.optimization_barrier(jnp.sum(feed_back, axis=0))
            middle_back = upstream + norm_backward(feed_back, normed_two, spread_two, gain_table[layer_index, 1])
            middle_half = middle_back.astype(jnp.bfloat16)
            mixing_part = jnp.dot(attended.T, middle_half, preferred_element_type=jnp.float32)
            offset_mix = lax.optimization_barrier(jnp.sum(middle_back, axis=0))
            attended_back = jnp.dot(middle_half, mixing[layer_index].T, preferred_element_type=jnp.float32).astype(jnp.bfloat16)
            back_heads = widened(attended_back).reshape(ROW_TOK, HEADS, HEAD)
            row_delta = lax.optimization_barrier(jnp.sum(back_heads * attended.astype(jnp.float32).reshape(ROW_TOK, HEADS, HEAD), axis=-1))
            masked = jnp.where(visible[None], jnp.einsum('qhe,khe->hqk', query_heads, key_heads) * head_scale, MASKED)
            soft = jnp.exp(masked - log_total)
            soft_half = soft.astype(jnp.bfloat16)
            prob_back = jnp.einsum('qhe,khe->hqk', back_heads, value_heads)
            score_back = widened((soft * (prob_back - row_delta.T[:, :, None]) * head_scale).astype(jnp.bfloat16))
            query_back = jnp.einsum('hqk,khe->qhe', score_back, key_heads).reshape(ROW_TOK, D)
            key_back = jnp.einsum('hqk,qhe->khe', score_back, query_heads).reshape(ROW_TOK, D)
            value_back = jnp.einsum('hqk,qhe->khe', widened(soft_half), back_heads).reshape(ROW_TOK, D)
            head_part = jnp.stack([lax.optimization_barrier(jnp.sum(query_back, axis=0)), lax.optimization_barrier(jnp.sum(value_back, axis=0))]).reshape(2, HEADS, HEAD)
            project_back = [query_back.astype(jnp.bfloat16), key_back.astype(jnp.bfloat16), value_back.astype(jnp.bfloat16)]
            projection_part = jnp.stack([jnp.dot(attend_input.T, project_back[slot], preferred_element_type=jnp.float32) for slot in range(3)])
            input_back = jnp.dot(project_back[0], projection[layer_index, 0].T, preferred_element_type=jnp.float32)
            input_back = input_back + jnp.dot(project_back[1], projection[layer_index, 1].T, preferred_element_type=jnp.float32)
            input_back = input_back + jnp.dot(project_back[2], projection[layer_index, 2].T, preferred_element_type=jnp.float32)
            gain_one = lax.optimization_barrier(jnp.sum(input_back * normed_one, axis=0))
            offset_one = lax.optimization_barrier(jnp.sum(input_back, axis=0))
            upstream = middle_back + norm_backward(input_back, normed_one, spread_one, gain_table[layer_index, 0])
            grad_parts = (projection_part, head_part, mixing_part, expansion_part, hidden_part, contraction_part, jnp.stack([gain_one, gain_two]), jnp.stack([offset_one, offset_two, offset_mix, offset_down]))
            running_totals = [running.at[layer_index].add(addend) for running, addend in zip(running_totals, grad_parts)]
        return (tuple(running_totals), (row_output, upstream))
    zeros_start = (jnp.zeros((LAYERS, 3, D, D), jnp.float32), jnp.zeros((LAYERS, 2, HEADS, HEAD), jnp.float32), jnp.zeros((LAYERS, D, D), jnp.float32), jnp.zeros((LAYERS, D, FF), jnp.float32), jnp.zeros((LAYERS, FF // HEAD, HEAD), jnp.float32), jnp.zeros((LAYERS, FF, D), jnp.float32), jnp.zeros((LAYERS, 2, D), jnp.float32), jnp.zeros((LAYERS, 4, D), jnp.float32))
    totals, (outputs, input_grad) = lax.scan(one_row, zeros_start, (inputs, segment_ids, cotangent))
    return (outputs, input_grad, totals[0], totals[1], totals[2], totals[3], totals[4], totals[5], totals[6], totals[7])
```

```python
import jax
import jax.numpy as jnp
from jax import lax
from jax.sharding import PartitionSpec as P

HEAD = 64

EPS = 1e-05
GELU_COEF = 0.7978845608028654
GELU_CUBE = 0.044715
MASKED = -1e30
HALF = jnp.bfloat16
FULL = jnp.float32


def gelu_value(preact):
    inner_arg = GELU_COEF * (preact + GELU_CUBE * preact * preact * preact)
    return 0.5 * preact * (1.0 + jnp.tanh(inner_arg))


def gelu_slope(preact):
    inner_arg = GELU_COEF * (preact + GELU_CUBE * preact * preact * preact)
    tanh_value = jnp.tanh(inner_arg)
    return 0.5 * (1.0 + tanh_value) + 0.5 * preact * (1.0 - tanh_value * tanh_value) * GELU_COEF * (
        1.0 + 3.0 * GELU_CUBE * preact * preact
    )


def norm_forward(stream):
    center = stream - jnp.mean(stream, axis=-1, keepdims=True)
    spread = lax.rsqrt(jnp.mean(center * center, axis=-1, keepdims=True) + EPS)
    return (center * spread, spread)


def norm_backward(upstream, normed, spread, gain_row):
    scaled = upstream * gain_row
    first_mean = jnp.mean(scaled, axis=-1, keepdims=True)
    second_mean = jnp.mean(scaled * normed, axis=-1, keepdims=True)
    return spread * (scaled - first_mean - normed * second_mean)


def dot(left, right, left_dim, right_dim):
    return lax.dot_general(
        left, right, (((left_dim,), (right_dim,)), ((), ())), preferred_element_type=FULL
    )


def pair_sum(part):
    size = lax.axis_size("tensor")
    other = lax.ppermute(part, "tensor", [(i, (i + 1) % size) for i in range(size)])
    return part.astype(FULL) + other.astype(FULL)


def from_before(block, steps):
    size = lax.axis_size("context")
    return lax.ppermute(block, "context", [(i, i + steps) for i in range(size - steps)])


def from_after(block, steps):
    size = lax.axis_size("context")
    return lax.ppermute(block, "context", [(i + steps, i) for i in range(size - steps)])


def context_sum(part):
    size = lax.axis_size("context")
    total = part.astype(FULL)
    for steps in range(1, size):
        moved = lax.ppermute(part, "context", [(i, (i + steps) % size) for i in range(size)])
        total = total + moved.astype(FULL)
    return total


def masked_scores(query_block, key_block, visible, head_scale):
    scores = (
        jnp.einsum("rqhe,rkhe->rhqk", query_block, key_block, preferred_element_type=FULL)
        * head_scale
    )
    return jnp.where(visible, scores, MASKED)


def per_device(
    inputs,
    segment_ids,
    projection,
    head_bias,
    mixing,
    expansion,
    hidden_bias,
    contraction,
    norm_gains,
    offsets,
    cotangent,
):
    layers = projection.shape[0]
    rows, block, width = inputs.shape
    shards = lax.axis_size("shard")
    contexts = lax.axis_size("context")
    own = projection.shape[2]
    heads = head_bias.shape[2]
    head_cols = projection.shape[3]
    hidden = expansion.shape[2]
    tokens = rows * block
    head_scale = HEAD ** (-0.5)
    back_steps = 2

    gathered = []
    for layer in range(layers):
        packed = jnp.concatenate(
            [projection[layer, 0], projection[layer, 1], projection[layer, 2], mixing[layer].T,
             expansion[layer], contraction[layer].T], axis=1)
        gathered.append(lax.all_gather(packed, "shard", axis=0, tiled=True))
    small_parts = [norm_gains, offsets, head_bias, hidden_bias]
    small_sizes = [part.size for part in small_parts]
    small_total = sum(small_sizes)
    small_padded = -(-small_total // 1024) * 1024
    small = jnp.concatenate([part.reshape(-1) for part in small_parts] + [jnp.zeros((small_padded - small_total,), HALF)])
    small = jnp.broadcast_to(small.reshape(1, -1, 128), (shards, small_padded // 128, 128))
    small = lax.all_to_all(small, "shard", 0, 0).reshape(shards, small_padded)

    def widen(index):
        start = sum(small_sizes[:index])
        shape = small_parts[index].shape
        piece = small[:, start:start + small_sizes[index]].astype(FULL).reshape((shards,) + shape)
        piece = jnp.moveaxis(piece, 0, -2)
        return piece.reshape(shape[:-1] + (shards * shape[-1],))

    gains_all, offsets_all = widen(0), widen(1)
    head_all = widen(2).reshape(layers, 2, head_cols)
    hidden_all = widen(3).reshape(layers, hidden)

    seg_before = [from_before(segment_ids, steps) for steps in range(back_steps, 0, -1)]
    segments_all = jnp.concatenate(seg_before + [segment_ids], axis=1)
    query_pos = jnp.arange(block, dtype=jnp.int32) + back_steps * block
    key_pos = jnp.arange((back_steps + 1) * block, dtype=jnp.int32)
    first_key = (back_steps - lax.axis_index("context")) * block
    visible = (segments_all[:, None, :] == segment_ids[:, :, None]) & (
        key_pos[None, None, :] <= query_pos[None, :, None]
    ) & (key_pos >= first_key)[None, None, :]
    visible = visible[:, None]

    def split_weights(weights):
        ends = [3 * head_cols, 4 * head_cols, 4 * head_cols + hidden, 4 * head_cols + 2 * hidden]
        return (weights[:, :ends[0]], weights[:, ends[0]:ends[1]], weights[:, ends[1]:ends[2]], weights[:, ends[2]:ends[3]])

    stream = inputs.reshape(tokens, width)
    kept = []
    for layer in range(layers):
        qkv_weight, out_weight, up_weight, down_weight = split_weights(gathered[layer])
        gain, offset = gains_all[layer], offsets_all[layer]
        normed_one, spread_one = norm_forward(stream)
        attend_input = (normed_one * gain[0] + offset[0]).astype(HALF)
        zero_bias = jnp.zeros((head_cols,), FULL)
        bias = jnp.concatenate([head_all[layer, 0], zero_bias, head_all[layer, 1]])
        projected = (dot(attend_input, qkv_weight, 1, 0) + bias).astype(HALF)
        query_rows = projected[:, :head_cols]
        key_value = projected[:, head_cols:].reshape(rows, block, 2 * head_cols)
        before = [from_before(key_value, steps) for steps in range(back_steps, 0, -1)]
        key_value_all = jnp.concatenate(before + [key_value], axis=1)
        query_block = query_rows.reshape(rows, block, heads, HEAD)
        key_block = key_value_all[:, :, :head_cols].reshape(rows, -1, heads, HEAD)
        value_block = key_value_all[:, :, head_cols:].reshape(rows, -1, heads, HEAD)
        masked = masked_scores(query_block, key_block, visible, head_scale)
        row_top = jnp.max(masked, axis=-1, keepdims=True)
        log_total = row_top + jnp.log(jnp.sum(jnp.exp(masked - row_top), axis=-1, keepdims=True))
        soft_half = jnp.exp(masked - log_total).astype(HALF)
        attended = (
            jnp.einsum("rhqk,rkhe->rqhe", soft_half, value_block, preferred_element_type=FULL)
            .astype(HALF)
            .reshape(tokens, head_cols)
        )
        middle = stream + pair_sum(dot(attended, out_weight, 1, 1)) + offset[2]
        normed_two, spread_two = norm_forward(middle)
        feed_input = (normed_two * gain[1] + offset[1]).astype(HALF)
        preact = dot(feed_input, up_weight, 1, 0) + hidden_all[layer]
        activation = gelu_value(preact).astype(HALF)
        stream = middle + pair_sum(dot(activation, down_weight, 1, 1)) + offset[3]
        kept.append((normed_one, spread_one, attend_input, query_block, key_block, value_block,
                     log_total, attended, normed_two, spread_two, feed_input, preact, activation))

    def scatter(parts):
        packed = jnp.concatenate([part.astype(HALF) for part in parts], axis=1)
        return lax.psum_scatter(packed, "shard", scatter_dimension=0, tiled=True)

    upstream = cotangent.reshape(tokens, width)
    feed_shares, attend_shares, vectors = [None] * layers, [None] * layers, [None] * layers
    for layer in reversed(range(layers)):
        (normed_one, spread_one, attend_input, query_block, key_block, value_block,
         log_total, attended, normed_two, spread_two, feed_input, preact, activation) = kept[layer]
        qkv_weight, out_weight, up_weight, down_weight = split_weights(gathered[layer])
        gain = gains_all[layer]
        upstream_half = upstream.astype(HALF)
        contraction_part = dot(upstream_half, activation, 0, 0)
        offset_down = jnp.sum(upstream, axis=0)
        hidden_back = dot(upstream_half, down_weight, 1, 0) * gelu_slope(preact)
        hidden_half = hidden_back.astype(HALF)
        hidden_part = jnp.sum(hidden_back, axis=0)
        expansion_part = dot(feed_input, hidden_half, 0, 0)
        feed_shares[layer] = scatter([expansion_part, contraction_part])
        feed_back = pair_sum(dot(hidden_half, up_weight, 1, 1).astype(HALF))
        gain_two = jnp.sum(feed_back * normed_two, axis=0)
        offset_two = jnp.sum(feed_back, axis=0)
        middle_back = upstream + norm_backward(feed_back, normed_two, spread_two, gain[1])
        middle_half = middle_back.astype(HALF)
        mixing_part = dot(middle_half, attended, 0, 0)
        offset_mix = jnp.sum(middle_back, axis=0)
        attended_back = dot(middle_half, out_weight, 1, 0).astype(HALF)
        back_heads = attended_back.reshape(rows, block, heads, HEAD)
        attended_heads = attended.reshape(rows, block, heads, HEAD)
        row_delta = jnp.sum(back_heads.astype(FULL) * attended_heads.astype(FULL), axis=-1)
        masked = masked_scores(query_block, key_block, visible, head_scale)
        soft = jnp.exp(masked - log_total)
        soft_half = soft.astype(HALF)
        prob_back = jnp.einsum("rqhe,rkhe->rhqk", back_heads, value_block, preferred_element_type=FULL)
        score_back = (
            soft * (prob_back - jnp.transpose(row_delta, (0, 2, 1))[..., None]) * head_scale
        ).astype(HALF)
        query_back = jnp.einsum(
            "rhqk,rkhe->rqhe", score_back, key_block, preferred_element_type=FULL
        ).reshape(tokens, head_cols)
        key_full = jnp.einsum(
            "rhqk,rqhe->rkhe", score_back, query_block, preferred_element_type=FULL
        ).reshape(rows, -1, head_cols)
        value_full = jnp.einsum(
            "rhqk,rqhe->rkhe", soft_half, back_heads, preferred_element_type=FULL
        ).reshape(rows, -1, head_cols)
        both_full = jnp.concatenate([key_full, value_full], axis=2)
        both_back = both_full[:, back_steps * block:]
        for steps in range(1, back_steps + 1):
            start = (back_steps - steps) * block
            both_back = both_back + from_after(both_full[:, start:start + block].astype(HALF), steps).astype(FULL)
        both_back = both_back.reshape(tokens, 2 * head_cols)
        head_part = jnp.concatenate([jnp.sum(query_back, axis=0), jnp.sum(both_back[:, head_cols:], axis=0)])
        project_back = jnp.concatenate([query_back, both_back], axis=1).astype(HALF)
        projection_part = dot(attend_input, project_back, 0, 0)
        attend_shares[layer] = scatter([projection_part, mixing_part])
        input_back = pair_sum(dot(project_back, qkv_weight, 1, 1).astype(HALF))
        gain_one = jnp.sum(input_back * normed_one, axis=0)
        offset_one = jnp.sum(input_back, axis=0)
        upstream = middle_back + norm_backward(input_back, normed_one, spread_one, gain[0])
        vectors[layer] = ([gain_one, gain_two], [offset_one, offset_two, offset_mix, offset_down], head_part, hidden_part)

    def spread_out(values, shape):
        lead = shape[:-1]
        values = values.reshape(lead + (shards, shape[-1]))
        return jnp.moveaxis(values, -2, 0).reshape(shards, -1)

    gain_sums = jnp.stack([jnp.stack(entry[0]) for entry in vectors])
    offset_sums = jnp.stack([jnp.stack(entry[1]) for entry in vectors])
    head_sums = jnp.stack([entry[2] for entry in vectors])
    hidden_sums = jnp.stack([entry[3] for entry in vectors])
    vector_pack = jnp.concatenate(
        [spread_out(values, part.shape) for values, part in zip((gain_sums, offset_sums, head_sums, hidden_sums), small_parts)]
        + [jnp.zeros((shards, small_padded - small_total), FULL)], axis=1)
    vector_pack = lax.all_to_all(vector_pack.reshape(shards, -1, 128), "shard", 0, 0)
    vector_own = context_sum(jnp.sum(vector_pack, axis=0)).reshape(-1)
    vector_out = []
    for index, part in enumerate(small_parts):
        start = sum(small_sizes[:index])
        vector_out.append(vector_own[start:start + small_sizes[index]].reshape(part.shape))
    gains_grad, offsets_grad, head_grad, hidden_grad = vector_out

    feed_own = [context_sum(share) for share in feed_shares]
    attend_own = [context_sum(share) for share in attend_shares]
    projection_grad = jnp.stack(
        [jnp.stack([share[:, k * head_cols:(k + 1) * head_cols] for k in range(3)]) for share in attend_own])
    mixing_grad = jnp.stack([share[:, 3 * head_cols:].T for share in attend_own])
    expansion_grad = jnp.stack([share[:, :hidden] for share in feed_own])
    contraction_grad = jnp.stack([share[:, hidden:].T for share in feed_own])
    return (
        stream.reshape(rows, block, width),
        upstream.reshape(rows, block, width),
        projection_grad,
        head_grad,
        mixing_grad,
        expansion_grad,
        hidden_grad,
        contraction_grad,
        gains_grad,
        offsets_grad,
    )


def solution(mesh):
    in_specs = (
        P("shard", "context", None),
        P("shard", "context"),
        P(None, None, "shard", "tensor"),
        P(None, None, "tensor", "shard"),
        P(None, "tensor", "shard"),
        P(None, "shard", "tensor"),
        P(None, "tensor", "shard"),
        P(None, "tensor", "shard"),
        P(None, None, "shard"),
        P(None, None, "shard"),
        P("shard", "context", None),
    )
    out_specs = (
        P("shard", "context", None),
        P("shard", "context", None),
        P(None, None, "shard", "tensor"),
        P(None, None, "tensor", "shard"),
        P(None, "tensor", "shard"),
        P(None, "shard", "tensor"),
        P(None, "tensor", "shard"),
        P(None, "tensor", "shard"),
        P(None, None, "shard"),
        P(None, None, "shard"),
    )
    return jax.shard_map(
        per_device, mesh=mesh, in_specs=in_specs, out_specs=out_specs, check_vma=False
    )
```

```python
import jax
import jax.numpy as jnp
from jax import lax
from jax.sharding import PartitionSpec as P

HEAD = 64

EPS = 1e-05
GELU_COEF = 0.7978845608028654
GELU_CUBE = 0.044715
MASKED = -1e30
SIDE = 4
HALF = jnp.bfloat16
FULL = jnp.float32


def gelu_value(preact):
    inner_arg = GELU_COEF * (preact + GELU_CUBE * preact * preact * preact)
    return 0.5 * preact * (1.0 + jnp.tanh(inner_arg))


def gelu_slope(preact):
    inner_arg = GELU_COEF * (preact + GELU_CUBE * preact * preact * preact)
    tanh_value = jnp.tanh(inner_arg)
    return 0.5 * (1.0 + tanh_value) + 0.5 * preact * (1.0 - tanh_value * tanh_value) * GELU_COEF * (
        1.0 + 3.0 * GELU_CUBE * preact * preact
    )


def norm_forward(stream):
    center = stream - jnp.mean(stream, axis=-1, keepdims=True)
    spread = lax.rsqrt(jnp.mean(center * center, axis=-1, keepdims=True) + EPS)
    return (center * spread, spread)


def norm_backward(upstream, normed, spread, gain_row):
    scaled = upstream * gain_row
    first_mean = jnp.mean(scaled, axis=-1, keepdims=True)
    second_mean = jnp.mean(scaled * normed, axis=-1, keepdims=True)
    return spread * (scaled - first_mean - normed * second_mean)


def dot(left, right, left_dim, right_dim):
    return lax.dot_general(
        left, right, (((left_dim,), (right_dim,)), ((), ())), preferred_element_type=FULL
    )


def pair_sum(part):
    size = lax.axis_size("tensor")
    other = lax.ppermute(part, "tensor", [(i, (i + 1) % size) for i in range(size)])
    return part.astype(FULL) + other.astype(FULL)


def from_before(block, steps):
    size = lax.axis_size("context")
    return lax.ppermute(block, "context", [(i, i + steps) for i in range(size - steps)])


def from_after(block, steps):
    size = lax.axis_size("context")
    return lax.ppermute(block, "context", [(i + steps, i) for i in range(size - steps)])


def context_sum(part):
    size = lax.axis_size("context")
    total = part.astype(FULL)
    for steps in range(1, size):
        moved = lax.ppermute(part, "context", [(i, (i + steps) % size) for i in range(size)])
        total = total + moved.astype(FULL)
    return total


def pair_other(part):
    size = lax.axis_size("tensor")
    return lax.ppermute(part, "tensor", [(i, (i + 1) % size) for i in range(size)])


def own_half(values, other=False):
    cols = values.shape[-1] // 2
    which = lax.axis_index("tensor")
    start = (1 - which if other else which) * cols
    return lax.dynamic_slice_in_dim(values, start, cols, axis=values.ndim - 1)


def join_halves(mine, other):
    first = lax.axis_index("tensor") == 0
    return jnp.concatenate([jnp.where(first, mine, other), jnp.where(first, other, mine)], axis=-1)


def shard_moves(axis, steps):
    moves = []
    for slow in range(SIDE):
        for fast in range(SIDE):
            target = (slow, (fast + steps) % SIDE) if axis else ((slow + steps) % SIDE, fast)
            moves.append((slow * SIDE + fast, target[0] * SIDE + target[1]))
    return moves


def scatter_axis(values, axis, dim):
    place = lax.axis_index("shard")
    place = place % SIDE if axis else place // SIDE
    sent = values.astype(HALF)
    total = lax.dynamic_index_in_dim(values, place, dim, keepdims=False).astype(FULL)
    for steps in (1, 3, 2):
        piece = lax.dynamic_index_in_dim(sent, (place + steps) % SIDE, dim, keepdims=False)
        total = total + lax.ppermute(piece, "shard", shard_moves(axis, steps)).astype(FULL)
    return total


def scatter_two(values):
    count = values.shape[1] // 2
    grid = values.reshape(SIDE, SIDE, -1, values.shape[1])
    first = scatter_axis(scatter_axis(grid[..., :count], 1, 1), 0, 0)
    second = scatter_axis(scatter_axis(grid[..., count:], 0, 0), 1, 0)
    return jnp.concatenate([first, second], axis=1)


def masked_scores(query_block, key_block, visible, head_scale):
    scores = (
        jnp.einsum("rqhe,rkhe->rhqk", query_block, key_block, preferred_element_type=FULL)
        * head_scale
    )
    return jnp.where(visible, scores, MASKED)


def per_device(
    inputs,
    segment_ids,
    projection,
    head_bias,
    mixing,
    expansion,
    hidden_bias,
    contraction,
    norm_gains,
    offsets,
    cotangent,
):
    layers = projection.shape[0]
    rows, block, width = inputs.shape
    shards = lax.axis_size("shard")
    contexts = lax.axis_size("context")
    own = projection.shape[2]
    heads = head_bias.shape[2]
    head_cols = projection.shape[3]
    hidden = expansion.shape[2]
    tokens = rows * block
    head_scale = HEAD ** (-0.5)
    back_steps = 2

    gathered = []
    for layer in range(layers):
        packed = jnp.concatenate(
            [projection[layer, 0], projection[layer, 1], projection[layer, 2], mixing[layer].T,
             expansion[layer], contraction[layer].T], axis=1)
        gathered.append(lax.all_gather(packed, "shard", axis=0, tiled=True))
    small_parts = [norm_gains, offsets, head_bias, hidden_bias]
    small_sizes = [part.size for part in small_parts]
    small_total = sum(small_sizes)
    small_padded = -(-small_total // 1024) * 1024
    small = jnp.concatenate([part.reshape(-1) for part in small_parts] + [jnp.zeros((small_padded - small_total,), HALF)])
    small = jnp.broadcast_to(small.reshape(1, -1, 128), (shards, small_padded // 128, 128))
    small = lax.all_to_all(small, "shard", 0, 0).reshape(shards, small_padded)

    def widen(index):
        start = sum(small_sizes[:index])
        shape = small_parts[index].shape
        piece = small[:, start:start + small_sizes[index]].astype(FULL).reshape((shards,) + shape)
        piece = jnp.moveaxis(piece, 0, -2)
        return piece.reshape(shape[:-1] + (shards * shape[-1],))

    gains_all, offsets_all = widen(0), widen(1)
    head_all = widen(2).reshape(layers, 2, head_cols)
    hidden_all = widen(3).reshape(layers, hidden)

    seg_before = [from_before(segment_ids, steps) for steps in range(back_steps, 0, -1)]
    segments_all = jnp.concatenate(seg_before + [segment_ids], axis=1)
    query_pos = jnp.arange(block, dtype=jnp.int32) + back_steps * block
    key_pos = jnp.arange((back_steps + 1) * block, dtype=jnp.int32)
    first_key = (back_steps - lax.axis_index("context")) * block
    visible = (segments_all[:, None, :] == segment_ids[:, :, None]) & (
        key_pos[None, None, :] <= query_pos[None, :, None]
    ) & (key_pos >= first_key)[None, None, :]
    visible = visible[:, None]

    def split_weights(weights):
        ends = [3 * head_cols, 4 * head_cols, 4 * head_cols + hidden, 4 * head_cols + 2 * hidden]
        return (weights[:, :ends[0]], weights[:, ends[0]:ends[1]], weights[:, ends[1]:ends[2]], weights[:, ends[2]:ends[3]])

    stream = inputs.reshape(tokens, width)
    kept = []
    for layer in range(layers):
        qkv_weight, out_weight, up_weight, down_weight = split_weights(gathered[layer])
        gain, offset = gains_all[layer], offsets_all[layer]
        normed_one, spread_one = norm_forward(stream)
        attend_input = (normed_one * gain[0] + offset[0]).astype(HALF)
        half_input = own_half(attend_input).reshape(rows, block, width // 2)
        halo = jnp.concatenate([from_before(half_input, steps) for steps in range(back_steps, 0, -1)], axis=1)
        halo = join_halves(halo, pair_other(halo))
        wide_input = jnp.concatenate([halo, attend_input.reshape(rows, block, width)], axis=1).reshape(-1, width)
        query_rows = (dot(attend_input, qkv_weight[:, :head_cols], 1, 0) + head_all[layer, 0]).astype(HALF)
        key_rows = dot(wide_input, qkv_weight[:, head_cols:2 * head_cols], 1, 0).astype(HALF)
        value_rows = (dot(wide_input, qkv_weight[:, 2 * head_cols:], 1, 0) + head_all[layer, 1]).astype(HALF)
        query_block = query_rows.reshape(rows, block, heads, HEAD)
        key_block = key_rows.reshape(rows, -1, heads, HEAD)
        value_block = value_rows.reshape(rows, -1, heads, HEAD)
        masked = masked_scores(query_block, key_block, visible, head_scale)
        row_top = jnp.max(masked, axis=-1, keepdims=True)
        log_total = row_top + jnp.log(jnp.sum(jnp.exp(masked - row_top), axis=-1, keepdims=True))
        soft_half = jnp.exp(masked - log_total).astype(HALF)
        attended = (
            jnp.einsum("rhqk,rkhe->rqhe", soft_half, value_block, preferred_element_type=FULL)
            .astype(HALF)
            .reshape(tokens, head_cols)
        )
        middle = stream + pair_sum(dot(attended, out_weight, 1, 1)) + offset[2]
        normed_two, spread_two = norm_forward(middle)
        feed_input = (normed_two * gain[1] + offset[1]).astype(HALF)
        preact = dot(feed_input, up_weight, 1, 0) + hidden_all[layer]
        activation = gelu_value(preact).astype(HALF)
        stream = middle + pair_sum(dot(activation, down_weight, 1, 1)) + offset[3]
        kept.append((normed_one, spread_one, attend_input, wide_input, query_block, key_block, value_block,
                     log_total, attended, normed_two, spread_two, feed_input, preact, activation))

    def scatter(parts):
        packed = jnp.concatenate([part.astype(HALF) for part in parts], axis=1)
        return lax.psum_scatter(packed, "shard", scatter_dimension=0, tiled=True)

    upstream = cotangent.reshape(tokens, width)
    feed_shares, attend_shares, vectors = [None] * layers, [None] * layers, [None] * layers
    for layer in reversed(range(layers)):
        (normed_one, spread_one, attend_input, wide_input, query_block, key_block, value_block,
         log_total, attended, normed_two, spread_two, feed_input, preact, activation) = kept[layer]
        qkv_weight, out_weight, up_weight, down_weight = split_weights(gathered[layer])
        gain = gains_all[layer]
        upstream_half = upstream.astype(HALF)
        contraction_part = dot(upstream_half, activation, 0, 0)
        offset_down = jnp.sum(upstream, axis=0)
        hidden_back = dot(upstream_half, down_weight, 1, 0) * gelu_slope(preact)
        hidden_half = hidden_back.astype(HALF)
        hidden_part = jnp.sum(hidden_back, axis=0)
        expansion_part = dot(feed_input, hidden_half, 0, 0)
        if layer == 0:
            feed_shares[layer] = [scatter_two(jnp.concatenate([expansion_part, contraction_part], axis=1))]
        feed_back = pair_sum(dot(hidden_half, up_weight, 1, 1).astype(HALF))
        gain_two = jnp.sum(feed_back * normed_two, axis=0)
        offset_two = jnp.sum(feed_back, axis=0)
        middle_back = upstream + norm_backward(feed_back, normed_two, spread_two, gain[1])
        middle_half = middle_back.astype(HALF)
        mixing_part = dot(middle_half, attended, 0, 0)
        offset_mix = jnp.sum(middle_back, axis=0)
        attended_back = dot(middle_half, out_weight, 1, 0).astype(HALF)
        back_heads = attended_back.reshape(rows, block, heads, HEAD)
        attended_heads = attended.reshape(rows, block, heads, HEAD)
        row_delta = jnp.sum(back_heads.astype(FULL) * attended_heads.astype(FULL), axis=-1)
        masked = masked_scores(query_block, key_block, visible, head_scale)
        soft = jnp.exp(masked - log_total)
        soft_half = soft.astype(HALF)
        prob_back = jnp.einsum("rqhe,rkhe->rhqk", back_heads, value_block, preferred_element_type=FULL)
        score_back = (
            soft * (prob_back - jnp.transpose(row_delta, (0, 2, 1))[..., None]) * head_scale
        ).astype(HALF)
        query_back = jnp.einsum(
            "rhqk,rkhe->rqhe", score_back, key_block, preferred_element_type=FULL
        ).reshape(tokens, head_cols)
        key_full = jnp.einsum(
            "rhqk,rqhe->rkhe", score_back, query_block, preferred_element_type=FULL
        ).reshape(rows, -1, head_cols)
        value_full = jnp.einsum(
            "rhqk,rqhe->rkhe", soft_half, back_heads, preferred_element_type=FULL
        ).reshape(rows, -1, head_cols)
        head_part = jnp.concatenate([jnp.sum(query_back, axis=0), jnp.sum(value_full, axis=(0, 1))])
        query_half = query_back.astype(HALF)
        both_half = jnp.concatenate([key_full, value_full], axis=2).astype(HALF).reshape(-1, 2 * head_cols)
        query_part = dot(attend_input, query_half, 0, 0)
        both_part = dot(wide_input, both_half, 0, 0)
        if layer == 0:
            attend_shares[layer] = scatter_two(jnp.concatenate([query_part, both_part, mixing_part], axis=1))
        else:
            attend_shares[layer] = scatter([query_part, both_part, mixing_part, expansion_part, contraction_part])
        query_input = dot(query_half, qkv_weight[:, :head_cols], 1, 1).reshape(rows, block, width)
        wide_back = dot(both_half, qkv_weight[:, head_cols:], 1, 1).reshape(rows, -1, width)
        wide_back = jnp.concatenate(
            [wide_back[:, :back_steps * block], wide_back[:, back_steps * block:] + query_input], axis=1)
        wide_back = own_half(wide_back) + pair_other(own_half(wide_back, other=True).astype(HALF)).astype(FULL)
        half_back = wide_back[:, back_steps * block:]
        for steps in range(1, back_steps + 1):
            start = (back_steps - steps) * block
            half_back = half_back + from_after(wide_back[:, start:start + block].astype(HALF), steps).astype(FULL)
        input_back = join_halves(half_back, pair_other(half_back)).reshape(tokens, width)
        gain_one = jnp.sum(input_back * normed_one, axis=0)
        offset_one = jnp.sum(input_back, axis=0)
        upstream = middle_back + norm_backward(input_back, normed_one, spread_one, gain[0])
        vectors[layer] = ([gain_one, gain_two], [offset_one, offset_two, offset_mix, offset_down], head_part, hidden_part)

    def spread_out(values, shape):
        lead = shape[:-1]
        values = values.reshape(lead + (shards, shape[-1]))
        return jnp.moveaxis(values, -2, 0).reshape(shards, -1)

    gain_sums = jnp.stack([jnp.stack(entry[0]) for entry in vectors])
    offset_sums = jnp.stack([jnp.stack(entry[1]) for entry in vectors])
    head_sums = jnp.stack([entry[2] for entry in vectors])
    hidden_sums = jnp.stack([entry[3] for entry in vectors])
    vector_pack = jnp.concatenate(
        [spread_out(values, part.shape) for values, part in zip((gain_sums, offset_sums, head_sums, hidden_sums), small_parts)]
        + [jnp.zeros((shards, small_padded - small_total), FULL)], axis=1)
    vector_pack = lax.all_to_all(vector_pack.reshape(shards, -1, 128), "shard", 0, 0)
    vector_own = context_sum(jnp.sum(vector_pack, axis=0)).reshape(-1)
    vector_out = []
    for index, part in enumerate(small_parts):
        start = sum(small_sizes[:index])
        vector_out.append(vector_own[start:start + small_sizes[index]].reshape(part.shape))
    gains_grad, offsets_grad, head_grad, hidden_grad = vector_out

    later = context_sum(attend_shares[1])
    qkv_end, out_end = 3 * head_cols, 4 * head_cols
    attend_own = [context_sum(attend_shares[0].astype(HALF)), later[:, :out_end]]
    feed_own = [context_sum(feed_shares[0][0].astype(HALF)), later[:, out_end:]]
    projection_grad = jnp.stack(
        [jnp.stack([share[:, k * head_cols:(k + 1) * head_cols] for k in range(3)]) for share in attend_own])
    mixing_grad = jnp.stack([share[:, qkv_end:].T for share in attend_own])
    expansion_grad = jnp.stack([share[:, :hidden] for share in feed_own])
    contraction_grad = jnp.stack([share[:, hidden:].T for share in feed_own])
    return (
        stream.reshape(rows, block, width),
        upstream.reshape(rows, block, width),
        projection_grad,
        head_grad,
        mixing_grad,
        expansion_grad,
        hidden_grad,
        contraction_grad,
        gains_grad,
        offsets_grad,
    )


def solution(mesh):
    in_specs = (
        P("shard", "context", None),
        P("shard", "context"),
        P(None, None, "shard", "tensor"),
        P(None, None, "tensor", "shard"),
        P(None, "tensor", "shard"),
        P(None, "shard", "tensor"),
        P(None, "tensor", "shard"),
        P(None, "tensor", "shard"),
        P(None, None, "shard"),
        P(None, None, "shard"),
        P("shard", "context", None),
    )
    out_specs = (
        P("shard", "context", None),
        P("shard", "context", None),
        P(None, None, "shard", "tensor"),
        P(None, None, "tensor", "shard"),
        P(None, "tensor", "shard"),
        P(None, "shard", "tensor"),
        P(None, "tensor", "shard"),
        P(None, "tensor", "shard"),
        P(None, None, "shard"),
        P(None, None, "shard"),
    )
    return jax.shard_map(
        per_device, mesh=mesh, in_specs=in_specs, out_specs=out_specs, check_vma=False
    )
```

```python
import functools

import jax
import jax.numpy as jnp
from jax import lax
from jax.experimental import pallas as pl
from jax.experimental.pallas import tpu as pltpu
from jax.sharding import PartitionSpec as P

HEAD = 64

EPS = 1e-05
GELU_COEF = 0.7978845608028654
GELU_CUBE = 0.044715
MASKED = -1e30
HALF = jnp.bfloat16
FULL = jnp.float32


def gelu_value(preact):
    inner_arg = GELU_COEF * (preact + GELU_CUBE * preact * preact * preact)
    return 0.5 * preact * (1.0 + jnp.tanh(inner_arg))


def norm_backward(upstream, normed, spread, gain_row):
    scaled = upstream * gain_row
    first_mean = jnp.mean(scaled, axis=-1, keepdims=True)
    second_mean = jnp.mean(scaled * normed, axis=-1, keepdims=True)
    return spread * (scaled - first_mean - normed * second_mean)


def dot(left, right, left_dim, right_dim):
    return lax.dot_general(
        left, right, (((left_dim,), (right_dim,)), ((), ())), preferred_element_type=FULL
    )


def from_before(block, steps):
    size = lax.axis_size("context")
    return lax.ppermute(block, "context", [(i, i + steps) for i in range(size - steps)])


def from_after(block, steps):
    size = lax.axis_size("context")
    return lax.ppermute(block, "context", [(i + steps, i) for i in range(size - steps)])


def context_sum(part):
    size = lax.axis_size("context")
    total = part.astype(FULL)
    for steps in range(1, size):
        moved = lax.ppermute(part, "context", [(i, (i + steps) % size) for i in range(size)])
        total = total + moved.astype(FULL)
    return total


def pair_other(part):
    size = lax.axis_size("tensor")
    return lax.ppermute(part, "tensor", [(i, (i + 1) % size) for i in range(size)])


def call(body, outs, ins, scratch=(), aliases=None, in_specs=None, out_specs=None, name=None):
    return pl.pallas_call(
        body,
        out_shape=outs,
        grid=(1,),
        in_specs=in_specs,
        out_specs=out_specs,
        scratch_shapes=list(scratch),
        input_output_aliases=aliases or {},
        compiler_params=pltpu.CompilerParams(vmem_limit_bytes=58 * 2**20),
        name=name,
    )(*ins)


def whole():
    return pl.BlockSpec(memory_space=pltpu.VMEM)


def scalars():
    return pl.BlockSpec(memory_space=pltpu.SMEM)


def shape(dims, dtype):
    return jax.ShapeDtypeStruct(dims, dtype)


def weight_spec(depth, cols, index):
    return pl.BlockSpec((depth, cols), lambda *_: (0, index))


def norm_stats(stream):
    center = stream - jnp.mean(stream, axis=-1, keepdims=True)
    spread = lax.rsqrt(jnp.mean(center * center, axis=-1, keepdims=True) + EPS)
    return center * spread, spread


def enter_kernel(has_parts, place, *refs):
    if has_parts:
        middle, mine, other, offset_last, gain, offset, stream_out, attend_out, half_out = refs
        stream = middle[...] + (mine[...] + other[...]) + offset_last[...]
        stream_out[...] = stream
    else:
        stream_in, gain, offset, attend_out, half_out = refs
        stream = stream_in[...]
    normed, _ = norm_stats(stream)
    attend = (normed * gain[...] + offset[...]).astype(HALF)
    attend_out[...] = attend
    cols = half_out.shape[1]
    half_out[...] = jnp.where(place[0] == 0, attend[:, :cols], attend[:, cols:])


def attend_kernel(place, own, far_mine, near_mine, far_other, near_other, weights, bias, visible,
                  query_out, key_out, value_out, attended_out, log_out, wide_out, part_out):
    tokens, width = own.shape
    rows, block, keys = visible.shape
    cols = query_out.shape[1]
    half = far_mine.shape[2]
    wide_out[:, keys - block:, :] = own[...].reshape(rows, block, width)

    def put(first, mine, other):
        mine, other = mine[...], other[...]
        low = place[0] == 0
        wide_out[:, first:first + block, :half] = jnp.where(low, mine, other)
        wide_out[:, first:first + block, half:] = jnp.where(low, other, mine)

    put(0, far_mine, far_other)
    put(block, near_mine, near_other)
    query_out[...] = (dot(own[...], weights[:, :cols], 1, 0) + bias[0:1, :]).astype(HALF)
    wide = wide_out[...].reshape(rows * keys, width)
    key_out[...] = dot(wide, weights[:, cols:2 * cols], 1, 0).astype(HALF).reshape(rows, keys, cols)
    value_out[...] = (dot(wide, weights[:, 2 * cols:3 * cols], 1, 0) + bias[1:2, :]).astype(HALF).reshape(rows, keys, cols)
    scale = HEAD ** (-0.5)
    pairs = cols // 128
    low_lane = lax.broadcasted_iota(jnp.int32, (block, 128), 1) < HEAD
    lane = lax.broadcasted_iota(jnp.int32, (block, 128), 1)
    log_out[...] = jnp.zeros(log_out.shape, FULL)

    def one(step, carry):
        row, pair = step // pairs, step % pairs
        at_rows = pl.ds(pl.multiple_of(row * block, block), block)
        at_cols = pl.ds(pl.multiple_of(pair * 128, 128), 128)
        query = query_out[at_rows, at_cols]
        key = key_out[row, :, at_cols]
        value = value_out[row, :, at_cols]
        shown = visible[row] > 0
        outs = []
        logs = log_out[at_rows, :]
        for which in range(2):
            picked = jnp.where(low_lane if which == 0 else ~low_lane, query, jnp.zeros_like(query))
            scores = jnp.where(shown, dot(picked, key, 1, 1) * scale, MASKED)
            top = jnp.max(scores, axis=-1, keepdims=True)
            grown = jnp.exp(scores - top)
            total = jnp.sum(grown, axis=-1, keepdims=True)
            logs = jnp.where(lane == 2 * pair + which, top + jnp.log(total), logs)
            soft = (grown * (1.0 / total)).astype(HALF)
            outs.append(dot(soft, value, 1, 0))
        log_out[at_rows, :] = logs
        attended_out[at_rows, at_cols] = jnp.where(low_lane, outs[0], outs[1]).astype(HALF)
        return carry

    lax.fori_loop(0, rows * pairs, one, 0)
    part_out[...] = dot(attended_out[...], weights[:, 3 * cols:4 * cols], 1, 1)


def feed_kernel(stream, mine, other, offset_mid, gain, offset, up, hidden_bias, down,
                middle_out, preact_out, part_out, active):
    middle = stream[...] + (mine[...] + other[...]) + offset_mid[...]
    middle_out[...] = middle
    normed, _ = norm_stats(middle)
    feed = (normed * gain[...] + offset[...]).astype(HALF)
    preact_out[...] = dot(feed, up[...], 1, 0) + hidden_bias[...]
    step_rows = 32

    def one(step, carry):
        at = pl.ds(pl.multiple_of(step * step_rows, step_rows), step_rows)
        active[at, :] = gelu_value(preact_out[at, :]).astype(HALF)
        return carry

    lax.fori_loop(0, preact_out.shape[0] // step_rows, one, 0)
    part_out[...] = dot(active[...], down[...], 1, 1)


def leave_norm(place, middle_back, stream, mine, other, gain):
    low = place[0] == 0
    mine, other = mine[...], other[...]
    back = jnp.concatenate([jnp.where(low, mine, other), jnp.where(low, other, mine)], axis=1)
    normed, spread = norm_stats(stream[...])
    upstream = middle_back[...] + norm_backward(back, normed, spread, gain[...])
    sums = jnp.concatenate(
        [jnp.sum(back * normed, axis=0, keepdims=True), jnp.sum(back, axis=0, keepdims=True)], axis=0)
    return upstream, sums


def leave_kernel(place, middle_back, stream, mine, other, gain, upstream_out, sums_out):
    upstream, sums = leave_norm(place, middle_back, stream, mine, other, gain)
    upstream_out[...] = upstream
    sums_out[...] = sums


def feed_back_kernel(has_leave, spread_pack, *refs):
    if has_leave:
        place, middle_back, stream, mine, other, gain_one = refs[:6]
        middle, preact, gain, offset, up, down = refs[6:12]
        upstream_out, sums_out, pack, hidden_sum, down_sum, part_out, active, hidden_half = refs[12:]
        upstream, sums = leave_norm(place, middle_back, stream, mine, other, gain_one)
        upstream_out[...] = upstream
        sums_out[...] = sums
    else:
        upstream_in, middle, preact, gain, offset, up, down = refs[:7]
        pack, hidden_sum, down_sum, part_out, active, hidden_half = refs[7:]
        upstream = upstream_in[...]
    hidden = up.shape[1]
    step_rows = 32
    upstream_half = upstream.astype(HALF)
    down_sum[...] = jnp.sum(upstream, axis=0, keepdims=True)
    normed, _ = norm_stats(middle[...])
    feed = (normed * gain[...] + offset[...]).astype(HALF)
    back = dot(upstream_half, down[...], 1, 0)
    hidden_sum[...] = jnp.zeros(hidden_sum.shape, FULL)
    for first in range(0, upstream.shape[0], step_rows):
        inner = slice(first, first + step_rows)
        pre = preact[inner, :]
        square = pre * pre
        tanh_value = jnp.tanh(GELU_COEF * (pre + GELU_CUBE * square * pre))
        active[inner, :] = (0.5 * pre * (1.0 + tanh_value)).astype(HALF)
        slope = 0.5 * (1.0 + tanh_value) + 0.5 * pre * (1.0 - tanh_value * tanh_value) * GELU_COEF * (
            1.0 + 3.0 * GELU_CUBE * square)
        hidden_back = back[inner, :] * slope
        hidden_sum[...] += jnp.sum(hidden_back, axis=0, keepdims=True)
        hidden_half[inner, :] = hidden_back.astype(HALF)
    part_out[...] = dot(hidden_half[...], up[...], 1, 1).astype(HALF)
    grads = (dot(feed, hidden_half[...], 0, 0).astype(HALF), dot(upstream_half, active[...], 0, 0).astype(HALF))
    if spread_pack:
        shards, own, cols = pack.shape[0], pack.shape[2], pack.shape[3]
        for index, grad in enumerate(grads):
            for side in range(2):
                pack[:, 2 * index + side] = grad[:, side * cols:(side + 1) * cols].reshape(shards, own, cols)
    else:
        pack[:, :hidden] = grads[0]
        pack[:, hidden:2 * hidden] = grads[1]


def attend_back_kernel(spread_pack, place, upstream, middle, mine, other, gain, attended, query, key, value,
                       log_total, visible, wide, weights, *refs):
    if spread_pack:
        pack, middle_out, wide_mine, wide_other, sums_out, heads_out, wide_query, wide_both, near = refs
    else:
        _, pack, middle_out, wide_mine, wide_other, sums_out, heads_out, wide_query, wide_both, near = refs
    tokens, width = upstream.shape
    rows, block, keys = visible.shape
    cols = query.shape[1]
    scale = HEAD ** (-0.5)
    feed_back = mine[...].astype(FULL) + other[...].astype(FULL)
    normed, spread = norm_stats(middle[...])
    middle_back = upstream[...] + norm_backward(feed_back, normed, spread, gain[...])
    middle_out[...] = middle_back
    sums_out[...] = jnp.concatenate(
        [jnp.sum(feed_back * normed, axis=0, keepdims=True), jnp.sum(feed_back, axis=0, keepdims=True),
         jnp.sum(middle_back, axis=0, keepdims=True)], axis=0)
    middle_half = middle_back.astype(HALF)
    mix_grad = dot(middle_half, attended[...], 0, 0).astype(HALF)
    near[...] = dot(middle_half, weights[:, 3 * cols:4 * cols], 1, 0).astype(HALF)
    pairs = cols // 128
    low_lane = lax.broadcasted_iota(jnp.int32, (block, 128), 1) < HEAD
    low_key = lax.broadcasted_iota(jnp.int32, (keys, 128), 1) < HEAD
    lane = lax.broadcasted_iota(jnp.int32, (block, 128), 1)
    heads_out[...] = jnp.zeros(heads_out.shape, FULL)

    def one(step, carry):
        row, pair = step // pairs, step % pairs
        at_rows = pl.ds(pl.multiple_of(row * block, block), block)
        at_cols = pl.ds(pl.multiple_of(pair * 128, 128), 128)
        at_values = pl.ds(pl.multiple_of(cols + pair * 128, 128), 128)
        query_two = query[at_rows, at_cols]
        key_two, value_two = key[row, :, at_cols], value[row, :, at_cols]
        back_two = near[at_rows, at_cols]
        product = back_two.astype(FULL) * attended[at_rows, at_cols].astype(FULL)
        shown = visible[row] > 0
        logs = log_total[at_rows, :]
        query_parts, key_parts, value_parts = [], [], []
        for which in range(2):
            lanes = low_lane if which == 0 else ~low_lane
            picked = jnp.where(lanes, query_two, jnp.zeros_like(query_two))
            picked_back = jnp.where(lanes, back_two, jnp.zeros_like(back_two))
            delta = jnp.sum(jnp.where(lanes, product, 0.0), axis=-1, keepdims=True)
            own_log = jnp.sum(jnp.where(lane == 2 * pair + which, logs, 0.0), axis=-1, keepdims=True)
            scores = jnp.where(shown, dot(picked, key_two, 1, 1) * scale, MASKED)
            soft = jnp.exp(scores - own_log)
            score_back = (soft * (dot(picked_back, value_two, 1, 1) - delta) * scale).astype(HALF)
            query_parts.append(dot(score_back, key_two, 1, 0))
            key_parts.append(dot(score_back, query_two, 0, 0))
            value_parts.append(dot(soft.astype(HALF), back_two, 0, 0))
        query_back = jnp.where(low_lane, query_parts[0], query_parts[1])
        key_back = jnp.where(low_key, key_parts[0], key_parts[1])
        value_back = jnp.where(low_key, value_parts[0], value_parts[1])
        heads_out[0:1, at_cols] += jnp.sum(query_back, axis=0, keepdims=True)
        heads_out[1:2, at_cols] += jnp.sum(value_back, axis=0, keepdims=True)
        wide_query[at_rows, at_cols] = query_back.astype(HALF)
        wide_both[row, :, at_cols] = key_back.astype(HALF)
        wide_both[row, :, at_values] = value_back.astype(HALF)
        return carry

    lax.fori_loop(0, rows * pairs, one, 0)
    both = wide_both[...].reshape(rows * keys, 2 * cols)
    own = wide[:, keys - block:, :].reshape(tokens, width)
    query_grad = dot(own, wide_query[...], 0, 0).astype(HALF)
    both_grad = dot(wide[...].reshape(rows * keys, width), both, 0, 0).astype(HALF)
    grads = (query_grad, both_grad[:, :cols], both_grad[:, cols:], mix_grad)
    for index, grad in enumerate(grads):
        if spread_pack:
            pack[:, index] = grad.reshape(pack.shape[0], pack.shape[2], cols)
        else:
            pack[:, index * cols:(index + 1) * cols] = grad
    wide_back = dot(both, weights[:, cols:3 * cols], 1, 1).reshape(rows, keys, width)
    own_back = dot(wide_query[...], weights[:, :cols], 1, 1).reshape(rows, block, width)
    half = width // 2
    low = place[0] == 0

    def put(first, count, values):
        wide_mine[:, first:first + count, :] = jnp.where(low, values[..., :half], values[..., half:])
        wide_other[:, first:first + count, :] = jnp.where(low, values[..., half:], values[..., :half]).astype(HALF)

    put(0, keys - block, wide_back[:, :keys - block])
    put(keys - block, block, wide_back[:, keys - block:] + own_back)


def per_device(
    inputs,
    segment_ids,
    projection,
    head_bias,
    mixing,
    expansion,
    hidden_bias,
    contraction,
    norm_gains,
    offsets,
    cotangent,
):
    layers = projection.shape[0]
    rows, block, width = inputs.shape
    shards = lax.axis_size("shard")
    contexts = lax.axis_size("context")
    own = projection.shape[2]
    heads = head_bias.shape[2]
    head_cols = projection.shape[3]
    hidden = expansion.shape[2]
    tokens = rows * block
    head_scale = HEAD ** (-0.5)
    back_steps = 2

    gathered = []
    for layer in range(layers):
        packed = jnp.concatenate(
            [projection[layer, 0], projection[layer, 1], projection[layer, 2], mixing[layer].T,
             expansion[layer], contraction[layer].T], axis=1)
        gathered.append(lax.all_gather(packed, "shard", axis=0, tiled=True))
    small_parts = [norm_gains, offsets, head_bias, hidden_bias]
    small_sizes = [part.size for part in small_parts]
    small_total = sum(small_sizes)
    small_padded = -(-small_total // 1024) * 1024
    small = jnp.concatenate([part.reshape(-1) for part in small_parts] + [jnp.zeros((small_padded - small_total,), HALF)])
    small = jnp.broadcast_to(small.reshape(1, -1, 128), (shards, small_padded // 128, 128))
    small = lax.all_to_all(small, "shard", 0, 0).reshape(shards, small_padded)

    def widen(index):
        start = sum(small_sizes[:index])
        shape = small_parts[index].shape
        piece = small[:, start:start + small_sizes[index]].astype(FULL).reshape((shards,) + shape)
        piece = jnp.moveaxis(piece, 0, -2)
        return piece.reshape(shape[:-1] + (shards * shape[-1],))

    gains_all, offsets_all = widen(0), widen(1)
    head_all = widen(2).reshape(layers, 2, head_cols)
    hidden_all = widen(3).reshape(layers, hidden)

    seg_before = [from_before(segment_ids, steps) for steps in range(back_steps, 0, -1)]
    segments_all = jnp.concatenate(seg_before + [segment_ids], axis=1)
    query_pos = jnp.arange(block, dtype=jnp.int32) + back_steps * block
    key_pos = jnp.arange((back_steps + 1) * block, dtype=jnp.int32)
    first_key = (back_steps - lax.axis_index("context")) * block
    visible = (segments_all[:, None, :] == segment_ids[:, :, None]) & (
        key_pos[None, None, :] <= query_pos[None, :, None]
    ) & (key_pos >= first_key)[None, None, :]

    mask = visible.astype(FULL)
    keys = (back_steps + 1) * block
    half = width // 2
    place = lax.axis_index("tensor").astype(jnp.int32).reshape(1)
    side_cols = 4 * head_cols

    def row_of(table, layer, index):
        return table[layer, index].reshape(1, -1)

    def weight_specs(*names):
        return {"attend": weight_spec(width, side_cols, 0), "up": weight_spec(width, hidden, 1), "down": weight_spec(width, hidden, 2)}

    specs = weight_specs()
    vmem = whole()
    stream = inputs.reshape(tokens, width)
    kept = []
    parts = ()
    middle = None
    for layer in range(layers):
        weights = gathered[layer]
        outs = [shape((tokens, width), HALF), shape((tokens, half), HALF)]
        gain_row, offset_row = row_of(gains_all, layer, 0), row_of(offsets_all, layer, 0)
        if layer == 0:
            attend_input, sent = call(
                functools.partial(enter_kernel, False), outs, (place, stream, gain_row, offset_row),
                in_specs=[scalars()] + [vmem] * 3, out_specs=[vmem] * 2, name="enter_first")
        else:
            stream, attend_input, sent = call(
                functools.partial(enter_kernel, True), [shape((tokens, width), FULL)] + outs,
                (place, middle) + parts + (row_of(offsets_all, layer - 1, 3), gain_row, offset_row),
                in_specs=[scalars()] + [vmem] * 6, out_specs=[vmem] * 3, name="enter")
        sent = sent.reshape(rows, block, half)
        far, near = from_before(sent, 2), from_before(sent, 1)
        far_other, near_other = pair_other(far), pair_other(near)
        query, key, value, attended, log_total, wide, part = call(
            attend_kernel,
            [shape((tokens, head_cols), HALF), shape((rows, keys, head_cols), HALF), shape((rows, keys, head_cols), HALF),
             shape((tokens, head_cols), HALF), shape((tokens, 128), FULL), shape((rows, keys, width), HALF),
             shape((tokens, width), FULL)],
            (place, attend_input, far, near, far_other, near_other, weights, head_all[layer], mask),
            in_specs=[scalars()] + [vmem] * 5 + [specs["attend"]] + [vmem] * 2, out_specs=[vmem] * 7, name="attend")
        before = stream
        middle, preact, part = call(
            feed_kernel,
            [shape((tokens, width), FULL), shape((tokens, hidden), FULL), shape((tokens, width), FULL)],
            (stream, part, pair_other(part), row_of(offsets_all, layer, 2), row_of(gains_all, layer, 1),
             row_of(offsets_all, layer, 1), weights, hidden_all[layer].reshape(1, -1), weights),
            scratch=[pltpu.VMEM((tokens, hidden), HALF)],
            in_specs=[vmem] * 6 + [specs["up"], vmem, specs["down"]], out_specs=[vmem] * 3, name="feed")
        parts = (part, pair_other(part))
        kept.append((before, query, key, value, attended, log_total, wide, middle, preact))
    stream = middle + (parts[0] + parts[1]) + offsets_all[layers - 1, 3]

    vectors = [None] * layers
    leave = None
    for layer in reversed(range(layers)):
        before, query, key, value, attended, log_total, wide, middle, preact = kept[layer]
        weights = gathered[layer]
        last = layer == layers - 1
        if last:
            feed_pack = shape((width, 2 * hidden + side_cols), HALF)
            feed_pack_spec = pl.BlockSpec((width, 2 * hidden), lambda *_: (0, 0))
            attend_pack = feed_pack
            attend_pack_spec = pl.BlockSpec((width, side_cols), lambda *_: (0, 2 * hidden // side_cols))
        else:
            feed_pack = shape((shards, contexts, own, 2 * hidden // contexts), HALF)
            attend_pack = shape((shards, contexts, own, side_cols // contexts), HALF)
            feed_pack_spec = attend_pack_spec = vmem
        shared = (middle, preact, row_of(gains_all, layer, 1), row_of(offsets_all, layer, 1), weights, weights)
        shared_specs = [vmem] * 4 + [specs["up"], specs["down"]]
        outs = [feed_pack, shape((1, hidden), FULL), shape((1, width), FULL), shape((tokens, width), HALF)]
        outs_specs = [feed_pack_spec] + [vmem] * 3
        scratch = [pltpu.VMEM((tokens, hidden), HALF)] * 2
        if last:
            upstream = cotangent.reshape(tokens, width)
            packed, hidden_sum, down_sum, part = call(
                functools.partial(feed_back_kernel, False, False), outs, (upstream,) + shared, scratch=scratch,
                in_specs=[vmem] + shared_specs, out_specs=outs_specs, name="feed_back_last")
        else:
            upstream, leave_sums, packed, hidden_sum, down_sum, part = call(
                functools.partial(feed_back_kernel, True, True),
                [shape((tokens, width), FULL), shape((2, width), FULL)] + outs, leave + shared, scratch=scratch,
                in_specs=[scalars()] + [vmem] * 5 + shared_specs, out_specs=[vmem] * 2 + outs_specs, name="feed_back")
            vectors[layer + 1] = (leave_sums,) + vectors[layer + 1]
            feed_moved = lax.all_to_all(packed.reshape((shards * contexts,) + packed.shape[2:]), ("shard", "context"), 0, 0)
        operands = (place, upstream, middle, part, pair_other(part), row_of(gains_all, layer, 1), attended,
                    query, key, value, log_total, mask, wide, weights)
        operand_specs = [scalars()] + [vmem] * 12 + [specs["attend"]]
        packed, middle_back, wide_mine, wide_other, sums, head_sums = call(
            functools.partial(attend_back_kernel, not last),
            [attend_pack, shape((tokens, width), FULL), shape((rows, keys, half), FULL), shape((rows, keys, half), HALF),
             shape((3, width), FULL), shape((2, head_cols), FULL)],
            operands + ((packed,) if last else ()),
            scratch=[pltpu.VMEM((tokens, head_cols), HALF), pltpu.VMEM((rows, keys, 2 * head_cols), HALF),
                     pltpu.VMEM((tokens, head_cols), HALF)],
            aliases={len(operands): 0} if last else None,
            in_specs=operand_specs + ([pl.BlockSpec(memory_space=pl.ANY)] if last else []),
            out_specs=[attend_pack_spec] + [vmem] * 5, name="attend_back")
        if last:
            later_share = lax.psum_scatter(packed, "shard", scatter_dimension=0, tiled=True)
        else:
            attend_moved = lax.all_to_all(packed.reshape((shards * contexts,) + packed.shape[2:]), ("shard", "context"), 0, 0)
        wide_sum = wide_mine + pair_other(wide_other).astype(FULL)
        half_back = wide_sum[:, back_steps * block:]
        for steps in range(1, back_steps + 1):
            start = (back_steps - steps) * block
            half_back = half_back + from_after(wide_sum[:, start:start + block].astype(HALF), steps).astype(FULL)
        half_back = half_back.reshape(tokens, half)
        leave = (place, middle_back, before, half_back, pair_other(half_back), row_of(gains_all, layer, 0))
        vectors[layer] = (sums, down_sum, head_sums, hidden_sum)
    upstream, leave_sums = call(
        leave_kernel, [shape((tokens, width), FULL), shape((2, width), FULL)], leave,
        in_specs=[scalars()] + [vmem] * 5, out_specs=[vmem] * 2, name="leave")
    vectors[0] = (leave_sums,) + vectors[0]

    def spread_out(values, shape):
        lead = shape[:-1]
        values = values.reshape(lead + (shards, shape[-1]))
        return jnp.moveaxis(values, -2, 0).reshape(shards, -1)

    gain_sums = jnp.stack([jnp.stack([entry[0][0], entry[1][0]]) for entry in vectors])
    offset_sums = jnp.stack([jnp.concatenate([entry[0][1:2], entry[1][1:], entry[2]]) for entry in vectors])
    head_sums = jnp.stack([entry[3] for entry in vectors])
    hidden_sums = jnp.stack([entry[4] for entry in vectors])
    vector_pack = jnp.concatenate(
        [spread_out(values, part.shape) for values, part in zip((gain_sums, offset_sums, head_sums, hidden_sums), small_parts)]
        + [jnp.zeros((shards, small_padded - small_total), FULL)], axis=1)
    vector_pack = lax.all_to_all(vector_pack.reshape(shards, -1, 128), "shard", 0, 0)
    vector_own = context_sum(jnp.sum(vector_pack, axis=0)).reshape(-1)
    vector_out = []
    for index, part in enumerate(small_parts):
        start = sum(small_sizes[:index])
        vector_out.append(vector_own[start:start + small_sizes[index]].reshape(part.shape))
    gains_grad, offsets_grad, head_grad, hidden_grad = vector_out

    later = later_share.reshape(own, contexts, -1).transpose(1, 0, 2)
    later = jnp.sum(lax.all_to_all(later, "context", 0, 0).astype(FULL), axis=0).astype(HALF)
    feed_sum = jnp.sum(feed_moved.astype(FULL), axis=0).astype(HALF)
    attend_sum = jnp.sum(attend_moved.astype(FULL), axis=0).astype(HALF)
    quarters = jnp.concatenate([feed_sum, attend_sum, later], axis=1)
    quarters = lax.all_gather(quarters, "context", axis=0, tiled=False).astype(FULL)
    feed_cols, attend_cols = feed_sum.shape[1], attend_sum.shape[1]

    def join(piece):
        return jnp.moveaxis(piece, 0, 1).reshape(own, -1)

    feed_first, attend_first = join(quarters[:, :, :feed_cols]), join(quarters[:, :, feed_cols:feed_cols + attend_cols])
    later = join(quarters[:, :, feed_cols + attend_cols:])
    feed_own, attend_own = (feed_first, later[:, :2 * hidden]), (attend_first, later[:, 2 * hidden:])
    projection_grad = jnp.stack(
        [jnp.stack([share[:, k * head_cols:(k + 1) * head_cols] for k in range(3)]) for share in attend_own])
    mixing_grad = jnp.stack([share[:, 3 * head_cols:].T for share in attend_own])
    expansion_grad = jnp.stack([share[:, :hidden] for share in feed_own])
    contraction_grad = jnp.stack([share[:, hidden:].T for share in feed_own])
    return (
        stream.reshape(rows, block, width),
        upstream.reshape(rows, block, width),
        projection_grad,
        head_grad,
        mixing_grad,
        expansion_grad,
        hidden_grad,
        contraction_grad,
        gains_grad,
        offsets_grad,
    )


def solution(mesh):
    in_specs = (
        P("shard", "context", None),
        P("shard", "context"),
        P(None, None, "shard", "tensor"),
        P(None, None, "tensor", "shard"),
        P(None, "tensor", "shard"),
        P(None, "shard", "tensor"),
        P(None, "tensor", "shard"),
        P(None, "tensor", "shard"),
        P(None, None, "shard"),
        P(None, None, "shard"),
        P("shard", "context", None),
    )
    out_specs = (
        P("shard", "context", None),
        P("shard", "context", None),
        P(None, None, "shard", "tensor"),
        P(None, None, "tensor", "shard"),
        P(None, "tensor", "shard"),
        P(None, "shard", "tensor"),
        P(None, "tensor", "shard"),
        P(None, "tensor", "shard"),
        P(None, None, "shard"),
        P(None, None, "shard"),
    )
    return jax.shard_map(
        per_device, mesh=mesh, in_specs=in_specs, out_specs=out_specs, check_vma=False
    )
```

```python
import functools

import jax
import jax.numpy as jnp
from jax import lax
from jax.experimental import pallas as pl
from jax.experimental.pallas import tpu as pltpu
from jax.sharding import PartitionSpec as P

HEAD = 64

EPS = 1e-05
GELU_COEF = 0.7978845608028654
GELU_CUBE = 0.044715
MASKED = -1e30
SIDE = 4
HALF = jnp.bfloat16
FULL = jnp.float32


def gelu_value(preact):
    inner_arg = GELU_COEF * (preact + GELU_CUBE * preact * preact * preact)
    return 0.5 * preact * (1.0 + jnp.tanh(inner_arg))


def norm_backward(upstream, normed, spread, gain_row):
    scaled = upstream * gain_row
    first_mean = jnp.mean(scaled, axis=-1, keepdims=True)
    second_mean = jnp.mean(scaled * normed, axis=-1, keepdims=True)
    return spread * (scaled - first_mean - normed * second_mean)


def dot(left, right, left_dim, right_dim):
    return lax.dot_general(
        left, right, (((left_dim,), (right_dim,)), ((), ())), preferred_element_type=FULL
    )


def from_before(block, steps):
    size = lax.axis_size("context")
    return lax.ppermute(block, "context", [(i, i + steps) for i in range(size - steps)])


def from_after(block, steps):
    size = lax.axis_size("context")
    return lax.ppermute(block, "context", [(i + steps, i) for i in range(size - steps)])


def pair_other(part):
    size = lax.axis_size("tensor")
    return lax.ppermute(part, "tensor", [(i, (i + 1) % size) for i in range(size)])


def context_share(parts):
    size = lax.axis_size("context")
    place = lax.axis_index("context")
    total = lax.dynamic_index_in_dim(parts, place, 0, keepdims=False).astype(FULL)
    for steps in (1, 3, 2):
        piece = lax.dynamic_index_in_dim(parts, (place + steps) % size, 0, keepdims=False)
        total = total + lax.ppermute(piece, "context", [(i, (i + steps) % size) for i in range(size)]).astype(FULL)
    return total


def context_sum(part):
    size = lax.axis_size("context")
    total = part.astype(FULL)
    for steps in (1, 3, 2):
        moved = lax.ppermute(part, "context", [(i, (i + steps) % size) for i in range(size)])
        total = total + moved.astype(FULL)
    return total


def context_gather(part):
    size = lax.axis_size("context")
    place = lax.axis_index("context")
    pieces = [part] + [lax.ppermute(part, "context", [(i, (i + steps) % size) for i in range(size)]) for steps in (1, 2, 3)]
    order = [(place - index) % size for index in range(size)]
    return [lax.select_n(order[index], *pieces) for index in range(size)]


def shard_moves(axis, steps):
    moves = []
    for slow in range(SIDE):
        for fast in range(SIDE):
            target = (slow, (fast + steps) % SIDE) if axis else ((slow + steps) % SIDE, fast)
            moves.append((slow * SIDE + fast, target[0] * SIDE + target[1]))
    return moves


def shard_spread(part, axis):
    return [part] + [lax.ppermute(part, "shard", shard_moves(axis, steps)) for steps in (1, 2, 3)]


def scatter_axis(values, axis, dim):
    place = lax.axis_index("shard")
    place = place % SIDE if axis else place // SIDE
    sent = values if values.dtype == HALF or values.shape[-1] == 128 else values.astype(HALF)
    total = lax.dynamic_index_in_dim(values, place, dim, keepdims=False).astype(FULL)
    for steps in (1, 3, 2):
        piece = lax.dynamic_index_in_dim(sent, (place + steps) % SIDE, dim, keepdims=False)
        total = total + lax.ppermute(piece, "shard", shard_moves(axis, steps)).astype(FULL)
    return total


def scatter_two(first, second):
    first = first.reshape((SIDE, SIDE, -1) + first.shape[1:])
    second = second.reshape((SIDE, SIDE, -1) + second.shape[1:])
    return scatter_axis(scatter_axis(first, 1, 1), 0, 0), scatter_axis(scatter_axis(second, 0, 0), 1, 0)


def call(body, outs, ins, scratch=(), aliases=None, in_specs=None, out_specs=None, name=None):
    return pl.pallas_call(
        body,
        out_shape=outs,
        grid=(1,),
        in_specs=in_specs,
        out_specs=out_specs,
        scratch_shapes=list(scratch),
        input_output_aliases=aliases or {},
        compiler_params=pltpu.CompilerParams(vmem_limit_bytes=58 * 2**20),
        name=name,
    )(*ins)


def whole():
    return pl.BlockSpec(memory_space=pltpu.VMEM)


def scalars():
    return pl.BlockSpec(memory_space=pltpu.SMEM)


def shape(dims, dtype):
    return jax.ShapeDtypeStruct(dims, dtype)


def weight_spec(depth, cols, index):
    return pl.BlockSpec((depth, cols), lambda *_: (0, index))


def norm_stats(stream):
    center = stream - jnp.mean(stream, axis=-1, keepdims=True)
    spread = lax.rsqrt(jnp.mean(center * center, axis=-1, keepdims=True) + EPS)
    return center * spread, spread


def enter_kernel(has_parts, place, *refs):
    if has_parts:
        middle, mine, other, offset_last, gain, offset, stream_out, attend_out, half_out = refs
        stream = middle[...] + (mine[...] + other[...]) + offset_last[...]
        stream_out[...] = stream
    else:
        stream_in, gain, offset, attend_out, half_out = refs
        stream = stream_in[...]
    normed, _ = norm_stats(stream)
    attend = (normed * gain[...] + offset[...]).astype(HALF)
    attend_out[...] = attend
    cols = half_out.shape[1]
    half_out[...] = jnp.where(place[0] == 0, attend[:, :cols], attend[:, cols:])


def assemble(place, pieces, out, first, along_fast):
    rows, cols = pieces[0].shape[1:]
    for later in range(SIDE):
        for early in range(SIDE):
            slow_steps, fast_steps = (later, early) if along_fast else (early, later)
            slow = lax.rem(place[1] + SIDE - slow_steps, SIDE)
            fast = lax.rem(place[2] + SIDE - fast_steps, SIDE)
            start = pl.multiple_of((slow * SIDE + fast) * rows, rows)
            out[pl.ds(start, rows), first:first + cols] = pieces[later][early]


def attend_first_kernel(place, *refs):
    pieces, rest, weights = refs[:2 * SIDE], refs[2 * SIDE:-1], refs[-1]
    assemble(place, pieces[:SIDE], weights, 0, True)
    assemble(place, pieces[SIDE:], weights, weights.shape[1] // 2, False)
    attend_kernel(place, *rest[:5], weights, *rest[5:])


def feed_first_kernel(place, *refs):
    pieces, rest, up, down, active = refs[:2 * SIDE], refs[2 * SIDE:-3], refs[-3], refs[-2], refs[-1]
    assemble(place, pieces[:SIDE], up, 0, True)
    assemble(place, pieces[SIDE:], down, 0, False)
    feed_kernel(*rest[:6], up, rest[6], down, *rest[7:], active)


def attend_kernel(place, own, far_mine, near_mine, far_other, near_other, weights, bias, visible,
                  query_out, key_out, value_out, attended_out, log_out, wide_out, part_out):
    tokens, width = own.shape
    rows, block, keys = visible.shape
    cols = query_out.shape[1]
    half = far_mine.shape[2]
    wide_out[:, keys - block:, :] = own[...].reshape(rows, block, width)

    def put(first, mine, other):
        mine, other = mine[...], other[...]
        low = place[0] == 0
        wide_out[:, first:first + block, :half] = jnp.where(low, mine, other)
        wide_out[:, first:first + block, half:] = jnp.where(low, other, mine)

    put(0, far_mine, far_other)
    put(block, near_mine, near_other)
    query_out[...] = (dot(own[...], weights[:, :cols], 1, 0) + bias[0:1, :]).astype(HALF)
    wide = wide_out[...].reshape(rows * keys, width)
    key_out[...] = dot(wide, weights[:, cols:2 * cols], 1, 0).astype(HALF).reshape(rows, keys, cols)
    value_out[...] = (dot(wide, weights[:, 2 * cols:3 * cols], 1, 0) + bias[1:2, :]).astype(HALF).reshape(rows, keys, cols)
    scale = HEAD ** (-0.5)
    pairs = cols // 128
    low_lane = lax.broadcasted_iota(jnp.int32, (block, 128), 1) < HEAD
    lane = lax.broadcasted_iota(jnp.int32, (block, 128), 1)
    log_out[...] = jnp.zeros(log_out.shape, FULL)

    def one(step, carry):
        row, pair = step // pairs, step % pairs
        at_rows = pl.ds(pl.multiple_of(row * block, block), block)
        at_cols = pl.ds(pl.multiple_of(pair * 128, 128), 128)
        query = query_out[at_rows, at_cols]
        key = key_out[row, :, at_cols]
        value = value_out[row, :, at_cols]
        shown = visible[row] > 0
        outs = []
        logs = log_out[at_rows, :]
        for which in range(2):
            picked = jnp.where(low_lane if which == 0 else ~low_lane, query, jnp.zeros_like(query))
            scores = jnp.where(shown, dot(picked, key, 1, 1) * scale, MASKED)
            top = jnp.max(scores, axis=-1, keepdims=True)
            grown = jnp.exp(scores - top)
            total = jnp.sum(grown, axis=-1, keepdims=True)
            logs = jnp.where(lane == 2 * pair + which, top + jnp.log(total), logs)
            soft = (grown * (1.0 / total)).astype(HALF)
            outs.append(dot(soft, value, 1, 0))
        log_out[at_rows, :] = logs
        attended_out[at_rows, at_cols] = jnp.where(low_lane, outs[0], outs[1]).astype(HALF)
        return carry

    lax.fori_loop(0, rows * pairs, one, 0)
    part_out[...] = dot(attended_out[...], weights[:, 3 * cols:4 * cols], 1, 1)


def feed_kernel(stream, mine, other, offset_mid, gain, offset, up, hidden_bias, down,
                middle_out, preact_out, part_out, active):
    middle = stream[...] + (mine[...] + other[...]) + offset_mid[...]
    middle_out[...] = middle
    normed, _ = norm_stats(middle)
    feed = (normed * gain[...] + offset[...]).astype(HALF)
    preact_out[...] = dot(feed, up[...], 1, 0) + hidden_bias[...]
    step_rows = 32

    def one(step, carry):
        at = pl.ds(pl.multiple_of(step * step_rows, step_rows), step_rows)
        active[at, :] = gelu_value(preact_out[at, :]).astype(HALF)
        return carry

    lax.fori_loop(0, preact_out.shape[0] // step_rows, one, 0)
    part_out[...] = dot(active[...], down[...], 1, 1)


def leave_norm(place, middle_back, stream, mine, other, gain):
    low = place[0] == 0
    mine, other = mine[...], other[...]
    back = jnp.concatenate([jnp.where(low, mine, other), jnp.where(low, other, mine)], axis=1)
    normed, spread = norm_stats(stream[...])
    upstream = middle_back[...] + norm_backward(back, normed, spread, gain[...])
    sums = jnp.concatenate(
        [jnp.sum(back * normed, axis=0, keepdims=True), jnp.sum(back, axis=0, keepdims=True)], axis=0)
    return upstream, sums


def leave_kernel(place, middle_back, stream, mine, other, gain, upstream_out, sums_out):
    upstream, sums = leave_norm(place, middle_back, stream, mine, other, gain)
    upstream_out[...] = upstream
    sums_out[...] = sums


def feed_back_kernel(has_leave, spread_pack, *refs):
    if has_leave:
        place, middle_back, stream, mine, other, gain_one = refs[:6]
        middle, preact, gain, offset, up, down = refs[6:12]
        upstream_out, sums_out, pack, hidden_sum, down_sum, part_out, active, hidden_half = refs[12:]
        upstream, sums = leave_norm(place, middle_back, stream, mine, other, gain_one)
        upstream_out[...] = upstream
        sums_out[...] = sums
    else:
        upstream_in, middle, preact, gain, offset, up, down = refs[:7]
        pack, hidden_sum, down_sum, part_out, active, hidden_half = refs[7:]
        upstream = upstream_in[...]
    hidden = up.shape[1]
    step_rows = 32
    upstream_half = upstream.astype(HALF)
    down_sum[...] = jnp.sum(upstream, axis=0, keepdims=True)
    normed, _ = norm_stats(middle[...])
    feed = (normed * gain[...] + offset[...]).astype(HALF)
    back = dot(upstream_half, down[...], 1, 0)
    hidden_sum[...] = jnp.zeros(hidden_sum.shape, FULL)
    for first in range(0, upstream.shape[0], step_rows):
        inner = slice(first, first + step_rows)
        pre = preact[inner, :]
        square = pre * pre
        tanh_value = jnp.tanh(GELU_COEF * (pre + GELU_CUBE * square * pre))
        active[inner, :] = (0.5 * pre * (1.0 + tanh_value)).astype(HALF)
        slope = 0.5 * (1.0 + tanh_value) + 0.5 * pre * (1.0 - tanh_value * tanh_value) * GELU_COEF * (
            1.0 + 3.0 * GELU_CUBE * square)
        hidden_back = back[inner, :] * slope
        hidden_sum[...] += jnp.sum(hidden_back, axis=0, keepdims=True)
        hidden_half[inner, :] = hidden_back.astype(HALF)
    part_out[...] = dot(hidden_half[...], up[...], 1, 1).astype(HALF)
    grads = (dot(feed, hidden_half[...], 0, 0).astype(HALF), dot(upstream_half, active[...], 0, 0).astype(HALF))
    if spread_pack:
        shards, own, cols = pack.shape[0], pack.shape[2], pack.shape[3]
        for index, grad in enumerate(grads):
            for side in range(2):
                pack[:, 2 * index + side] = grad[:, side * cols:(side + 1) * cols].reshape(shards, own, cols)
    else:
        pack[:, :hidden] = grads[0]
        pack[:, hidden:2 * hidden] = grads[1]


def attend_back_kernel(fresh_pack, place, upstream, middle, mine, other, gain, attended, query, key, value,
                       log_total, visible, wide, weights, *refs):
    if fresh_pack:
        pack, middle_out, wide_mine, wide_other, sums_out, heads_out, wide_query, wide_both, near = refs
    else:
        _, pack, middle_out, wide_mine, wide_other, sums_out, heads_out, wide_query, wide_both, near = refs
    tokens, width = upstream.shape
    rows, block, keys = visible.shape
    cols = query.shape[1]
    scale = HEAD ** (-0.5)
    feed_back = mine[...].astype(FULL) + other[...].astype(FULL)
    normed, spread = norm_stats(middle[...])
    middle_back = upstream[...] + norm_backward(feed_back, normed, spread, gain[...])
    middle_out[...] = middle_back
    sums_out[...] = jnp.concatenate(
        [jnp.sum(feed_back * normed, axis=0, keepdims=True), jnp.sum(feed_back, axis=0, keepdims=True),
         jnp.sum(middle_back, axis=0, keepdims=True)], axis=0)
    middle_half = middle_back.astype(HALF)
    mix_grad = dot(middle_half, attended[...], 0, 0).astype(HALF)
    near[...] = dot(middle_half, weights[:, 3 * cols:4 * cols], 1, 0).astype(HALF)
    pairs = cols // 128
    low_lane = lax.broadcasted_iota(jnp.int32, (block, 128), 1) < HEAD
    low_key = lax.broadcasted_iota(jnp.int32, (keys, 128), 1) < HEAD
    lane = lax.broadcasted_iota(jnp.int32, (block, 128), 1)
    heads_out[...] = jnp.zeros(heads_out.shape, FULL)

    def one(step, carry):
        row, pair = step // pairs, step % pairs
        at_rows = pl.ds(pl.multiple_of(row * block, block), block)
        at_cols = pl.ds(pl.multiple_of(pair * 128, 128), 128)
        at_values = pl.ds(pl.multiple_of(cols + pair * 128, 128), 128)
        query_two = query[at_rows, at_cols]
        key_two, value_two = key[row, :, at_cols], value[row, :, at_cols]
        back_two = near[at_rows, at_cols]
        product = back_two.astype(FULL) * attended[at_rows, at_cols].astype(FULL)
        shown = visible[row] > 0
        logs = log_total[at_rows, :]
        query_parts, key_parts, value_parts = [], [], []
        for which in range(2):
            lanes = low_lane if which == 0 else ~low_lane
            picked = jnp.where(lanes, query_two, jnp.zeros_like(query_two))
            picked_back = jnp.where(lanes, back_two, jnp.zeros_like(back_two))
            delta = jnp.sum(jnp.where(lanes, product, 0.0), axis=-1, keepdims=True)
            own_log = jnp.sum(jnp.where(lane == 2 * pair + which, logs, 0.0), axis=-1, keepdims=True)
            scores = jnp.where(shown, dot(picked, key_two, 1, 1) * scale, MASKED)
            soft = jnp.exp(scores - own_log)
            score_back = (soft * (dot(picked_back, value_two, 1, 1) - delta) * scale).astype(HALF)
            query_parts.append(dot(score_back, key_two, 1, 0))
            key_parts.append(dot(score_back, query_two, 0, 0))
            value_parts.append(dot(soft.astype(HALF), back_two, 0, 0))
        query_back = jnp.where(low_lane, query_parts[0], query_parts[1])
        key_back = jnp.where(low_key, key_parts[0], key_parts[1])
        value_back = jnp.where(low_key, value_parts[0], value_parts[1])
        heads_out[0:1, at_cols] += jnp.sum(query_back, axis=0, keepdims=True)
        heads_out[1:2, at_cols] += jnp.sum(value_back, axis=0, keepdims=True)
        wide_query[at_rows, at_cols] = query_back.astype(HALF)
        wide_both[row, :, at_cols] = key_back.astype(HALF)
        wide_both[row, :, at_values] = value_back.astype(HALF)
        return carry

    lax.fori_loop(0, rows * pairs, one, 0)
    both = wide_both[...].reshape(rows * keys, 2 * cols)
    own = wide[:, keys - block:, :].reshape(tokens, width)
    query_grad = dot(own, wide_query[...], 0, 0).astype(HALF)
    both_grad = dot(wide[...].reshape(rows * keys, width), both, 0, 0).astype(HALF)
    grads = (query_grad, both_grad[:, :cols], both_grad[:, cols:], mix_grad)
    for index, grad in enumerate(grads):
        pack[:, index * cols:(index + 1) * cols] = grad
    wide_back = dot(both, weights[:, cols:3 * cols], 1, 1).reshape(rows, keys, width)
    own_back = dot(wide_query[...], weights[:, :cols], 1, 1).reshape(rows, block, width)
    half = width // 2
    low = place[0] == 0

    def put(first, count, values):
        wide_mine[:, first:first + count, :] = jnp.where(low, values[..., :half], values[..., half:])
        wide_other[:, first:first + count, :] = jnp.where(low, values[..., half:], values[..., :half]).astype(HALF)

    put(0, keys - block, wide_back[:, :keys - block])
    put(keys - block, block, wide_back[:, keys - block:] + own_back)


def per_device(
    inputs,
    segment_ids,
    projection,
    head_bias,
    mixing,
    expansion,
    hidden_bias,
    contraction,
    norm_gains,
    offsets,
    cotangent,
):
    layers = projection.shape[0]
    rows, block, width = inputs.shape
    shards = lax.axis_size("shard")
    contexts = lax.axis_size("context")
    own = projection.shape[2]
    heads = head_bias.shape[2]
    head_cols = projection.shape[3]
    hidden = expansion.shape[2]
    tokens = rows * block
    head_scale = HEAD ** (-0.5)
    back_steps = 2

    gathered = [None]
    for layer in range(1, layers):
        packed = jnp.concatenate(
            [projection[layer, 0], projection[layer, 1], projection[layer, 2], mixing[layer].T,
             expansion[layer], contraction[layer].T], axis=1)
        gathered.append(lax.all_gather(packed, "shard", axis=0, tiled=True))
    near_fast = shard_spread(jnp.concatenate([projection[0, 0], projection[0, 1], expansion[0]], axis=1), 1)
    near_slow = shard_spread(jnp.concatenate([projection[0, 2], mixing[0].T, contraction[0].T], axis=1), 0)
    cut = 2 * projection.shape[3]
    attend_pieces = (shard_spread(jnp.stack([piece[:, :cut] for piece in near_fast]), 0)
                     + shard_spread(jnp.stack([piece[:, :cut] for piece in near_slow]), 1))
    feed_pieces = (shard_spread(jnp.stack([piece[:, cut:] for piece in near_fast]), 0)
                   + shard_spread(jnp.stack([piece[:, cut:] for piece in near_slow]), 1))
    small_parts = [norm_gains, offsets, head_bias, hidden_bias]
    small_sizes = [part.size for part in small_parts]
    small_total = sum(small_sizes)
    small_padded = -(-small_total // 1024) * 1024
    small = jnp.concatenate([part.reshape(-1) for part in small_parts] + [jnp.zeros((small_padded - small_total,), HALF)])
    small = jnp.broadcast_to(small.reshape(1, -1, 128), (shards, small_padded // 128, 128))
    small = lax.all_to_all(small, "shard", 0, 0).reshape(shards, small_padded)

    def widen(index):
        start = sum(small_sizes[:index])
        shape = small_parts[index].shape
        piece = small[:, start:start + small_sizes[index]].astype(FULL).reshape((shards,) + shape)
        piece = jnp.moveaxis(piece, 0, -2)
        return piece.reshape(shape[:-1] + (shards * shape[-1],))

    gains_all, offsets_all = widen(0), widen(1)
    head_all = widen(2).reshape(layers, 2, head_cols)
    hidden_all = widen(3).reshape(layers, hidden)

    seg_before = [from_before(segment_ids, steps) for steps in range(back_steps, 0, -1)]
    segments_all = jnp.concatenate(seg_before + [segment_ids], axis=1)
    query_pos = jnp.arange(block, dtype=jnp.int32) + back_steps * block
    key_pos = jnp.arange((back_steps + 1) * block, dtype=jnp.int32)
    first_key = (back_steps - lax.axis_index("context")) * block
    visible = (segments_all[:, None, :] == segment_ids[:, :, None]) & (
        key_pos[None, None, :] <= query_pos[None, :, None]
    ) & (key_pos >= first_key)[None, None, :]

    mask = visible.astype(FULL)
    keys = (back_steps + 1) * block
    half = width // 2
    shard = lax.axis_index("shard")
    place = jnp.stack([lax.axis_index("tensor"), shard // SIDE, shard % SIDE]).astype(jnp.int32)
    side_cols = 4 * head_cols

    def row_of(table, layer, index):
        return table[layer, index].reshape(1, -1)

    vmem = whole()
    stream = inputs.reshape(tokens, width)
    kept = []
    parts = ()
    middle = None
    for layer in range(layers):
        outs = [shape((tokens, width), HALF), shape((tokens, half), HALF)]
        gain_row, offset_row = row_of(gains_all, layer, 0), row_of(offsets_all, layer, 0)
        if layer == 0:
            attend_input, sent = call(
                functools.partial(enter_kernel, False), outs, (place, stream, gain_row, offset_row),
                in_specs=[scalars()] + [vmem] * 3, out_specs=[vmem] * 2, name="enter_first")
        else:
            stream, attend_input, sent = call(
                functools.partial(enter_kernel, True), [shape((tokens, width), FULL)] + outs,
                (place, middle) + parts + (row_of(offsets_all, layer - 1, 3), gain_row, offset_row),
                in_specs=[scalars()] + [vmem] * 6, out_specs=[vmem] * 3, name="enter")
        sent = sent.reshape(rows, block, half)
        far, near = from_before(sent, 2), from_before(sent, 1)
        far_other, near_other = pair_other(far), pair_other(near)
        attend_outs = [
            shape((tokens, head_cols), HALF), shape((rows, keys, head_cols), HALF), shape((rows, keys, head_cols), HALF),
            shape((tokens, head_cols), HALF), shape((tokens, 128), FULL), shape((rows, keys, width), HALF),
            shape((tokens, width), FULL)]
        attend_args = (attend_input, far, near, far_other, near_other)
        feed_outs = [shape((tokens, width), FULL), shape((tokens, hidden), FULL), shape((tokens, width), FULL)]
        scratch = [pltpu.VMEM((tokens, hidden), HALF)]
        rest = (row_of(offsets_all, layer, 2), row_of(gains_all, layer, 1), row_of(offsets_all, layer, 1))
        hidden_row = hidden_all[layer].reshape(1, -1)
        if layer == 0:
            query, key, value, attended, log_total, wide, part, weights = call(
                attend_first_kernel, attend_outs + [shape((width, side_cols), HALF)],
                (place,) + tuple(attend_pieces) + attend_args + (head_all[layer], mask),
                in_specs=[scalars()] + [vmem] * (2 * SIDE + 7), out_specs=[vmem] * 8, name="attend_first")
            middle, preact, part, up, down = call(
                feed_first_kernel, feed_outs + [shape((width, hidden), HALF)] * 2,
                (place,) + tuple(feed_pieces) + (stream, part, pair_other(part)) + rest + (hidden_row,),
                scratch=scratch, in_specs=[scalars()] + [vmem] * (2 * SIDE + 7), out_specs=[vmem] * 5, name="feed_first")
            held = (weights, up, down)
            specs = (vmem, vmem, vmem)
        else:
            held = (gathered[layer],) * 3
            specs = (weight_spec(width, side_cols, 0), weight_spec(width, hidden, 1), weight_spec(width, hidden, 2))
            query, key, value, attended, log_total, wide, part = call(
                attend_kernel, attend_outs, (place,) + attend_args + (held[0], head_all[layer], mask),
                in_specs=[scalars()] + [vmem] * 5 + [specs[0]] + [vmem] * 2, out_specs=[vmem] * 7, name="attend")
            middle, preact, part = call(
                feed_kernel, feed_outs, (stream, part, pair_other(part)) + rest + (held[1], hidden_row, held[2]),
                scratch=scratch, in_specs=[vmem] * 6 + [specs[1], vmem, specs[2]], out_specs=[vmem] * 3, name="feed")
        before = stream
        parts = (part, pair_other(part))
        kept.append((before, query, key, value, attended, log_total, wide, middle, preact, held, specs))
    stream = middle + (parts[0] + parts[1]) + offsets_all[layers - 1, 3]

    vectors = [None] * layers
    leave = None
    for layer in reversed(range(layers)):
        before, query, key, value, attended, log_total, wide, middle, preact, held, specs = kept[layer]
        last = layer == layers - 1
        if last:
            feed_pack = shape((width, 2 * hidden + side_cols), HALF)
            feed_pack_spec = pl.BlockSpec((width, 2 * hidden), lambda *_: (0, 0))
            attend_pack = feed_pack
            attend_pack_spec = pl.BlockSpec((width, side_cols), lambda *_: (0, 2 * hidden // side_cols))
        else:
            feed_pack = shape((shards, contexts, own, 2 * hidden // contexts), HALF)
            attend_pack = shape((width, side_cols), HALF)
            feed_pack_spec = attend_pack_spec = vmem
        shared = (middle, preact, row_of(gains_all, layer, 1), row_of(offsets_all, layer, 1), held[1], held[2])
        shared_specs = [vmem] * 4 + [specs[1], specs[2]]
        outs = [feed_pack, shape((1, hidden), FULL), shape((1, width), FULL), shape((tokens, width), HALF)]
        outs_specs = [feed_pack_spec] + [vmem] * 3
        scratch = [pltpu.VMEM((tokens, hidden), HALF)] * 2
        if last:
            upstream = cotangent.reshape(tokens, width)
            packed, hidden_sum, down_sum, part = call(
                functools.partial(feed_back_kernel, False, False), outs, (upstream,) + shared, scratch=scratch,
                in_specs=[vmem] + shared_specs, out_specs=outs_specs, name="feed_back_last")
        else:
            upstream, leave_sums, packed, hidden_sum, down_sum, part = call(
                functools.partial(feed_back_kernel, True, True),
                [shape((tokens, width), FULL), shape((2, width), FULL)] + outs, leave + shared, scratch=scratch,
                in_specs=[scalars()] + [vmem] * 5 + shared_specs, out_specs=[vmem] * 2 + outs_specs, name="feed_back")
            vectors[layer + 1] = (leave_sums,) + vectors[layer + 1]
            feed_moved = lax.all_to_all(packed.reshape((shards * contexts,) + packed.shape[2:]), ("shard", "context"), 0, 0)
        operands = (place, upstream, middle, part, pair_other(part), row_of(gains_all, layer, 1), attended,
                    query, key, value, log_total, mask, wide, held[0])
        operand_specs = [scalars()] + [vmem] * 12 + [specs[0]]
        packed, middle_back, wide_mine, wide_other, sums, head_sums = call(
            functools.partial(attend_back_kernel, not last),
            [attend_pack, shape((tokens, width), FULL), shape((rows, keys, half), FULL), shape((rows, keys, half), HALF),
             shape((3, width), FULL), shape((2, head_cols), FULL)],
            operands + ((packed,) if last else ()),
            scratch=[pltpu.VMEM((tokens, head_cols), HALF), pltpu.VMEM((rows, keys, 2 * head_cols), HALF),
                     pltpu.VMEM((tokens, head_cols), HALF)],
            aliases={len(operands): 0} if last else None,
            in_specs=operand_specs + ([pl.BlockSpec(memory_space=pl.ANY)] if last else []),
            out_specs=[attend_pack_spec] + [vmem] * 5, name="attend_back")
        if last:
            later_share = lax.psum_scatter(packed, "shard", scatter_dimension=0, tiled=True)
        else:
            attend_first = scatter_two(packed[:, :side_cols // 2], packed[:, side_cols // 2:])
        wide_sum = wide_mine + pair_other(wide_other).astype(FULL)
        half_back = wide_sum[:, back_steps * block:]
        for steps in range(1, back_steps + 1):
            start = (back_steps - steps) * block
            half_back = half_back + from_after(wide_sum[:, start:start + block].astype(HALF), steps).astype(FULL)
        half_back = half_back.reshape(tokens, half)
        leave = (place, middle_back, before, half_back, pair_other(half_back), row_of(gains_all, layer, 0))
        vectors[layer] = (sums, down_sum, head_sums, hidden_sum)
    upstream, leave_sums = call(
        leave_kernel, [shape((tokens, width), FULL), shape((2, width), FULL)], leave,
        in_specs=[scalars()] + [vmem] * 5, out_specs=[vmem] * 2, name="leave")
    vectors[0] = (leave_sums,) + vectors[0]

    def spread_out(values, shape):
        lead = shape[:-1]
        values = values.reshape(lead + (shards, shape[-1]))
        return jnp.moveaxis(values, -2, 0).reshape(shards, -1)

    gain_sums = jnp.stack([jnp.stack([entry[0][0], entry[1][0]]) for entry in vectors])
    offset_sums = jnp.stack([jnp.concatenate([entry[0][1:2], entry[1][1:], entry[2]]) for entry in vectors])
    head_sums = jnp.stack([entry[3] for entry in vectors])
    hidden_sums = jnp.stack([entry[4] for entry in vectors])
    vector_pack = jnp.concatenate(
        [spread_out(values, part.shape) for values, part in zip((gain_sums, offset_sums, head_sums, hidden_sums), small_parts)]
        + [jnp.zeros((shards, small_padded - small_total), FULL)], axis=1)
    vector_pack = vector_pack.reshape(SIDE, SIDE, -1, 128)
    vector_own = context_sum(scatter_axis(scatter_axis(vector_pack, 1, 1), 0, 0)).reshape(-1)
    vector_out = []
    for index, part in enumerate(small_parts):
        start = sum(small_sizes[:index])
        vector_out.append(vector_own[start:start + small_sizes[index]].reshape(part.shape))
    gains_grad, offsets_grad, head_grad, hidden_grad = vector_out

    later = later_share.reshape(own, contexts, -1).transpose(1, 0, 2)
    later = context_share(later).astype(HALF)
    feed_sum = jnp.sum(feed_moved.astype(FULL), axis=0).astype(HALF)
    feed_cols = feed_sum.shape[1]
    quarters = context_gather(jnp.concatenate([feed_sum, later], axis=1))
    feed_first = jnp.concatenate([piece[:, :feed_cols] for piece in quarters], axis=1).astype(FULL)
    later = jnp.concatenate([piece[:, feed_cols:] for piece in quarters], axis=1).astype(FULL)
    attend_first = context_sum(jnp.concatenate(attend_first, axis=1).astype(HALF))
    feed_own, attend_own = (feed_first, later[:, :2 * hidden]), (attend_first, later[:, 2 * hidden:])
    projection_grad = jnp.stack(
        [jnp.stack([share[:, k * head_cols:(k + 1) * head_cols] for k in range(3)]) for share in attend_own])
    mixing_grad = jnp.stack([share[:, 3 * head_cols:].T for share in attend_own])
    expansion_grad = jnp.stack([share[:, :hidden] for share in feed_own])
    contraction_grad = jnp.stack([share[:, hidden:].T for share in feed_own])
    return (
        stream.reshape(rows, block, width),
        upstream.reshape(rows, block, width),
        projection_grad,
        head_grad,
        mixing_grad,
        expansion_grad,
        hidden_grad,
        contraction_grad,
        gains_grad,
        offsets_grad,
    )


def solution(mesh):
    in_specs = (
        P("shard", "context", None),
        P("shard", "context"),
        P(None, None, "shard", "tensor"),
        P(None, None, "tensor", "shard"),
        P(None, "tensor", "shard"),
        P(None, "shard", "tensor"),
        P(None, "tensor", "shard"),
        P(None, "tensor", "shard"),
        P(None, None, "shard"),
        P(None, None, "shard"),
        P("shard", "context", None),
    )
    out_specs = (
        P("shard", "context", None),
        P("shard", "context", None),
        P(None, None, "shard", "tensor"),
        P(None, None, "tensor", "shard"),
        P(None, "tensor", "shard"),
        P(None, "shard", "tensor"),
        P(None, "tensor", "shard"),
        P(None, "tensor", "shard"),
        P(None, None, "shard"),
        P(None, None, "shard"),
    )
    return jax.shard_map(
        per_device, mesh=mesh, in_specs=in_specs, out_specs=out_specs, check_vma=False
    )
```

```python
import functools

import jax
import jax.numpy as jnp
from jax import lax
from jax.experimental import pallas as pl
from jax.experimental.pallas import tpu as pltpu
from jax.sharding import PartitionSpec as P

HEAD = 64

EPS = 1e-05
GELU_COEF = 0.7978845608028654
GELU_CUBE = 0.044715
MASKED = -1e30
HALF = jnp.bfloat16
FULL = jnp.float32


def gelu_value(preact):
    inner_arg = GELU_COEF * (preact + GELU_CUBE * preact * preact * preact)
    return 0.5 * preact * (1.0 + jnp.tanh(inner_arg))


def norm_backward(upstream, normed, spread, gain_row):
    scaled = upstream * gain_row
    first_mean = jnp.mean(scaled, axis=-1, keepdims=True)
    second_mean = jnp.mean(scaled * normed, axis=-1, keepdims=True)
    return spread * (scaled - first_mean - normed * second_mean)


def dot(left, right, left_dim, right_dim):
    return lax.dot_general(
        left, right, (((left_dim,), (right_dim,)), ((), ())), preferred_element_type=FULL
    )


def from_before(block, steps):
    size = lax.axis_size("context")
    return lax.ppermute(block, "context", [(i, i + steps) for i in range(size - steps)])


def from_after(block, steps):
    size = lax.axis_size("context")
    return lax.ppermute(block, "context", [(i + steps, i) for i in range(size - steps)])


def context_sum(part):
    size = lax.axis_size("context")
    total = part.astype(FULL)
    for steps in range(1, size):
        moved = lax.ppermute(part, "context", [(i, (i + steps) % size) for i in range(size)])
        total = total + moved.astype(FULL)
    return total


def pair_other(part):
    size = lax.axis_size("tensor")
    return lax.ppermute(part, "tensor", [(i, (i + 1) % size) for i in range(size)])


def call(body, outs, ins, scratch=(), aliases=None, in_specs=None, out_specs=None, name=None):
    return pl.pallas_call(
        body,
        out_shape=outs,
        grid=(1,),
        in_specs=in_specs,
        out_specs=out_specs,
        scratch_shapes=list(scratch),
        input_output_aliases=aliases or {},
        compiler_params=pltpu.CompilerParams(vmem_limit_bytes=58 * 2**20),
        name=name,
    )(*ins)


def whole():
    return pl.BlockSpec(memory_space=pltpu.VMEM)


def scalars():
    return pl.BlockSpec(memory_space=pltpu.SMEM)


def shape(dims, dtype):
    return jax.ShapeDtypeStruct(dims, dtype)


def weight_spec(depth, cols, index):
    return pl.BlockSpec((depth, cols), lambda *_: (0, index))


def norm_stats(stream):
    center = stream - jnp.mean(stream, axis=-1, keepdims=True)
    spread = lax.rsqrt(jnp.mean(center * center, axis=-1, keepdims=True) + EPS)
    return center * spread, spread


def enter_kernel(has_parts, place, *refs):
    if has_parts:
        middle, mine, other, offset_last, gain, offset, stream_out, attend_out, half_out = refs
        stream = middle[...] + (mine[...] + other[...]) + offset_last[...]
        stream_out[...] = stream
    else:
        stream_in, gain, offset, attend_out, half_out = refs
        stream = stream_in[...]
    normed, _ = norm_stats(stream)
    attend = (normed * gain[...] + offset[...]).astype(HALF)
    attend_out[...] = attend
    cols = half_out.shape[1]
    half_out[...] = jnp.where(place[0] == 0, attend[:, :cols], attend[:, cols:])


def attend_kernel(place, own, far_mine, near_mine, far_other, near_other, weights, bias, visible,
                  query_out, key_out, value_out, attended_out, log_out, wide_out, part_out):
    tokens, width = own.shape
    rows, block, keys = visible.shape
    cols = query_out.shape[1]
    half = far_mine.shape[2]
    wide_out[:, keys - block:, :] = own[...].reshape(rows, block, width)

    def put(first, mine, other):
        mine, other = mine[...], other[...]
        low = place[0] == 0
        wide_out[:, first:first + block, :half] = jnp.where(low, mine, other)
        wide_out[:, first:first + block, half:] = jnp.where(low, other, mine)

    put(0, far_mine, far_other)
    put(block, near_mine, near_other)
    query_out[...] = (dot(own[...], weights[:, :cols], 1, 0) + bias[0:1, :]).astype(HALF)
    wide = wide_out[...].reshape(rows * keys, width)
    key_out[...] = dot(wide, weights[:, cols:2 * cols], 1, 0).astype(HALF).reshape(rows, keys, cols)
    value_out[...] = (dot(wide, weights[:, 2 * cols:3 * cols], 1, 0) + bias[1:2, :]).astype(HALF).reshape(rows, keys, cols)
    scale = HEAD ** (-0.5)
    pairs = cols // 128
    low_lane = lax.broadcasted_iota(jnp.int32, (block, 128), 1) < HEAD
    lane = lax.broadcasted_iota(jnp.int32, (block, 128), 1)
    log_out[...] = jnp.zeros(log_out.shape, FULL)

    def one(step, carry):
        row, pair = step // pairs, step % pairs
        at_rows = pl.ds(pl.multiple_of(row * block, block), block)
        at_cols = pl.ds(pl.multiple_of(pair * 128, 128), 128)
        query = query_out[at_rows, at_cols]
        key = key_out[row, :, at_cols]
        value = value_out[row, :, at_cols]
        shown = visible[row] > 0
        outs = []
        logs = log_out[at_rows, :]
        for which in range(2):
            picked = jnp.where(low_lane if which == 0 else ~low_lane, query, jnp.zeros_like(query))
            scores = jnp.where(shown, dot(picked, key, 1, 1) * scale, MASKED)
            top = jnp.max(scores, axis=-1, keepdims=True)
            grown = jnp.exp(scores - top)
            total = jnp.sum(grown, axis=-1, keepdims=True)
            logs = jnp.where(lane == 2 * pair + which, top + jnp.log(total), logs)
            soft = (grown * (1.0 / total)).astype(HALF)
            outs.append(dot(soft, value, 1, 0))
        log_out[at_rows, :] = logs
        attended_out[at_rows, at_cols] = jnp.where(low_lane, outs[0], outs[1]).astype(HALF)
        return carry

    lax.fori_loop(0, rows * pairs, one, 0)
    part_out[...] = dot(attended_out[...], weights[:, 3 * cols:4 * cols], 1, 1)


def feed_kernel(stream, mine, other, offset_mid, gain, offset, up, hidden_bias, down,
                middle_out, preact_out, part_out, active):
    middle = stream[...] + (mine[...] + other[...]) + offset_mid[...]
    middle_out[...] = middle
    normed, _ = norm_stats(middle)
    feed = (normed * gain[...] + offset[...]).astype(HALF)
    preact_out[...] = dot(feed, up[...], 1, 0) + hidden_bias[...]
    step_rows = 32

    def one(step, carry):
        at = pl.ds(pl.multiple_of(step * step_rows, step_rows), step_rows)
        active[at, :] = gelu_value(preact_out[at, :]).astype(HALF)
        return carry

    lax.fori_loop(0, preact_out.shape[0] // step_rows, one, 0)
    part_out[...] = dot(active[...], down[...], 1, 1)


def leave_norm(place, middle_back, stream, mine, other, gain):
    low = place[0] == 0
    mine, other = mine[...], other[...]
    back = jnp.concatenate([jnp.where(low, mine, other), jnp.where(low, other, mine)], axis=1)
    normed, spread = norm_stats(stream[...])
    upstream = middle_back[...] + norm_backward(back, normed, spread, gain[...])
    sums = jnp.concatenate(
        [jnp.sum(back * normed, axis=0, keepdims=True), jnp.sum(back, axis=0, keepdims=True)], axis=0)
    return upstream, sums


def leave_kernel(place, middle_back, stream, mine, other, gain, upstream_out, sums_out):
    upstream, sums = leave_norm(place, middle_back, stream, mine, other, gain)
    upstream_out[...] = upstream
    sums_out[...] = sums


def feed_back_kernel(has_leave, *refs):
    if has_leave:
        place, middle_back, stream, mine, other, gain_one = refs[:6]
        middle, preact, gain, offset, up, down, _ = refs[6:13]
        upstream_out, sums_out, pack, hidden_sum, down_sum, part_out, active, hidden_half = refs[13:]
        upstream, sums = leave_norm(place, middle_back, stream, mine, other, gain_one)
        upstream_out[...] = upstream
        sums_out[...] = sums
    else:
        upstream_in, middle, preact, gain, offset, up, down = refs[:7]
        pack, hidden_sum, down_sum, part_out, active, hidden_half = refs[7:]
        upstream = upstream_in[...]
    hidden = up.shape[1]
    step_rows = 32
    upstream_half = upstream.astype(HALF)
    down_sum[...] = jnp.sum(upstream, axis=0, keepdims=True)
    normed, _ = norm_stats(middle[...])
    feed = (normed * gain[...] + offset[...]).astype(HALF)
    back = dot(upstream_half, down[...], 1, 0)
    hidden_sum[...] = jnp.zeros(hidden_sum.shape, FULL)
    for first in range(0, upstream.shape[0], step_rows):
        inner = slice(first, first + step_rows)
        pre = preact[inner, :]
        square = pre * pre
        tanh_value = jnp.tanh(GELU_COEF * (pre + GELU_CUBE * square * pre))
        active[inner, :] = (0.5 * pre * (1.0 + tanh_value)).astype(HALF)
        slope = 0.5 * (1.0 + tanh_value) + 0.5 * pre * (1.0 - tanh_value * tanh_value) * GELU_COEF * (
            1.0 + 3.0 * GELU_CUBE * square)
        hidden_back = back[inner, :] * slope
        hidden_sum[...] += jnp.sum(hidden_back, axis=0, keepdims=True)
        hidden_half[inner, :] = hidden_back.astype(HALF)
    part_out[...] = dot(hidden_half[...], up[...], 1, 1).astype(HALF)
    pack[:, :hidden] = dot(feed, hidden_half[...], 0, 0).astype(HALF)
    pack[:, hidden:2 * hidden] = dot(upstream_half, active[...], 0, 0).astype(HALF)


def attend_back_kernel(spread_pack, place, upstream, middle, mine, other, gain, attended, query, key, value,
                       log_total, visible, wide, weights, *refs):
    if spread_pack:
        pack, middle_out, wide_mine, wide_other, sums_out, heads_out, wide_query, wide_both, near = refs
    else:
        _, pack, middle_out, wide_mine, wide_other, sums_out, heads_out, wide_query, wide_both, near = refs
    tokens, width = upstream.shape
    rows, block, keys = visible.shape
    cols = query.shape[1]
    scale = HEAD ** (-0.5)
    feed_back = mine[...].astype(FULL) + other[...].astype(FULL)
    normed, spread = norm_stats(middle[...])
    middle_back = upstream[...] + norm_backward(feed_back, normed, spread, gain[...])
    middle_out[...] = middle_back
    sums_out[...] = jnp.concatenate(
        [jnp.sum(feed_back * normed, axis=0, keepdims=True), jnp.sum(feed_back, axis=0, keepdims=True),
         jnp.sum(middle_back, axis=0, keepdims=True)], axis=0)
    middle_half = middle_back.astype(HALF)
    mix_grad = dot(middle_half, attended[...], 0, 0).astype(HALF)
    near[...] = dot(middle_half, weights[:, 3 * cols:4 * cols], 1, 0).astype(HALF)
    pairs = cols // 128
    low_lane = lax.broadcasted_iota(jnp.int32, (block, 128), 1) < HEAD
    low_key = lax.broadcasted_iota(jnp.int32, (keys, 128), 1) < HEAD
    lane = lax.broadcasted_iota(jnp.int32, (block, 128), 1)
    heads_out[...] = jnp.zeros(heads_out.shape, FULL)

    def one(step, carry):
        row, pair = step // pairs, step % pairs
        at_rows = pl.ds(pl.multiple_of(row * block, block), block)
        at_cols = pl.ds(pl.multiple_of(pair * 128, 128), 128)
        at_values = pl.ds(pl.multiple_of(cols + pair * 128, 128), 128)
        query_two = query[at_rows, at_cols]
        key_two, value_two = key[row, :, at_cols], value[row, :, at_cols]
        back_two = near[at_rows, at_cols]
        product = back_two.astype(FULL) * attended[at_rows, at_cols].astype(FULL)
        shown = visible[row] > 0
        logs = log_total[at_rows, :]
        query_parts, key_parts, value_parts = [], [], []
        for which in range(2):
            lanes = low_lane if which == 0 else ~low_lane
            picked = jnp.where(lanes, query_two, jnp.zeros_like(query_two))
            picked_back = jnp.where(lanes, back_two, jnp.zeros_like(back_two))
            delta = jnp.sum(jnp.where(lanes, product, 0.0), axis=-1, keepdims=True)
            own_log = jnp.sum(jnp.where(lane == 2 * pair + which, logs, 0.0), axis=-1, keepdims=True)
            scores = jnp.where(shown, dot(picked, key_two, 1, 1) * scale, MASKED)
            soft = jnp.exp(scores - own_log)
            score_back = (soft * (dot(picked_back, value_two, 1, 1) - delta) * scale).astype(HALF)
            query_parts.append(dot(score_back, key_two, 1, 0))
            key_parts.append(dot(score_back, query_two, 0, 0))
            value_parts.append(dot(soft.astype(HALF), back_two, 0, 0))
        query_back = jnp.where(low_lane, query_parts[0], query_parts[1])
        key_back = jnp.where(low_key, key_parts[0], key_parts[1])
        value_back = jnp.where(low_key, value_parts[0], value_parts[1])
        heads_out[0:1, at_cols] += jnp.sum(query_back, axis=0, keepdims=True)
        heads_out[1:2, at_cols] += jnp.sum(value_back, axis=0, keepdims=True)
        wide_query[at_rows, at_cols] = query_back.astype(HALF)
        wide_both[row, :, at_cols] = key_back.astype(HALF)
        wide_both[row, :, at_values] = value_back.astype(HALF)
        return carry

    lax.fori_loop(0, rows * pairs, one, 0)
    both = wide_both[...].reshape(rows * keys, 2 * cols)
    own = wide[:, keys - block:, :].reshape(tokens, width)
    query_grad = dot(own, wide_query[...], 0, 0).astype(HALF)
    both_grad = dot(wide[...].reshape(rows * keys, width), both, 0, 0).astype(HALF)
    grads = (query_grad, both_grad[:, :cols], both_grad[:, cols:], mix_grad)
    for index, grad in enumerate(grads):
        if spread_pack:
            pack[:, index] = grad.reshape(pack.shape[0], pack.shape[2], cols)
        else:
            pack[:, index * cols:(index + 1) * cols] = grad
    wide_back = dot(both, weights[:, cols:3 * cols], 1, 1).reshape(rows, keys, width)
    own_back = dot(wide_query[...], weights[:, :cols], 1, 1).reshape(rows, block, width)
    half = width // 2
    low = place[0] == 0

    def put(first, count, values):
        wide_mine[:, first:first + count, :] = jnp.where(low, values[..., :half], values[..., half:])
        wide_other[:, first:first + count, :] = jnp.where(low, values[..., half:], values[..., :half]).astype(HALF)

    put(0, keys - block, wide_back[:, :keys - block])
    put(keys - block, block, wide_back[:, keys - block:] + own_back)


def per_device(
    inputs,
    segment_ids,
    projection,
    head_bias,
    mixing,
    expansion,
    hidden_bias,
    contraction,
    norm_gains,
    offsets,
    cotangent,
):
    layers = projection.shape[0]
    rows, block, width = inputs.shape
    shards = lax.axis_size("shard")
    contexts = lax.axis_size("context")
    own = projection.shape[2]
    heads = head_bias.shape[2]
    head_cols = projection.shape[3]
    hidden = expansion.shape[2]
    tokens = rows * block
    head_scale = HEAD ** (-0.5)
    back_steps = 2

    def attend_block(layer):
        return [projection[layer, 0], projection[layer, 1], projection[layer, 2], mixing[layer].T]

    others = [expansion[0], contraction[0].T]
    for layer in range(1, layers):
        others += attend_block(layer) + [expansion[layer], contraction[layer].T]
    gathered = lax.all_gather(jnp.concatenate(others, axis=1), "shard", axis=0, tiled=True)
    small_parts = [norm_gains, offsets, head_bias, hidden_bias]
    small_sizes = [part.size for part in small_parts]
    small_total = sum(small_sizes)
    small_padded = -(-small_total // 1024) * 1024
    small_rows = small_padded // 128
    small = jnp.concatenate([part.reshape(-1) for part in small_parts] + [jnp.zeros((own * 128 - small_total,), HALF)])
    first = jnp.concatenate(attend_block(0) + [small.reshape(own, 128)], axis=1)
    first = lax.all_to_all(jnp.broadcast_to(first[None], (shards,) + first.shape), "shard", 0, 0)
    small = first[:, :small_rows, first.shape[2] - 128:].reshape(shards, small_padded)
    first = first.reshape(shards * own, -1)

    def widen(index):
        start = sum(small_sizes[:index])
        shape = small_parts[index].shape
        piece = small[:, start:start + small_sizes[index]].astype(FULL).reshape((shards,) + shape)
        piece = jnp.moveaxis(piece, 0, -2)
        return piece.reshape(shape[:-1] + (shards * shape[-1],))

    gains_all, offsets_all = widen(0), widen(1)
    head_all = widen(2).reshape(layers, 2, head_cols)
    hidden_all = widen(3).reshape(layers, hidden)

    seg_before = [from_before(segment_ids, steps) for steps in range(back_steps, 0, -1)]
    segments_all = jnp.concatenate(seg_before + [segment_ids], axis=1)
    query_pos = jnp.arange(block, dtype=jnp.int32) + back_steps * block
    key_pos = jnp.arange((back_steps + 1) * block, dtype=jnp.int32)
    first_key = (back_steps - lax.axis_index("context")) * block
    visible = (segments_all[:, None, :] == segment_ids[:, :, None]) & (
        key_pos[None, None, :] <= query_pos[None, :, None]
    ) & (key_pos >= first_key)[None, None, :]

    mask = visible.astype(FULL)
    keys = (back_steps + 1) * block
    half = width // 2
    place = lax.axis_index("tensor").astype(jnp.int32).reshape(1)
    side_cols = 4 * head_cols

    def row_of(table, layer, index):
        return table[layer, index].reshape(1, -1)

    def weights_of(layer):
        if layer == 0:
            places = (0, 0, 1)
        else:
            places = (2 + 3 * (layer - 1), 3 + 3 * (layer - 1), 4 + 3 * (layer - 1))
        arrays = (first if layer == 0 else gathered, gathered, gathered)
        return arrays, tuple(weight_spec(width, cols, at) for cols, at in zip((side_cols, hidden, hidden), places))

    vmem = whole()
    stream = inputs.reshape(tokens, width)
    kept = []
    parts = ()
    middle = None
    for layer in range(layers):
        held, specs = weights_of(layer)
        outs = [shape((tokens, width), HALF), shape((tokens, half), HALF)]
        gain_row, offset_row = row_of(gains_all, layer, 0), row_of(offsets_all, layer, 0)
        if layer == 0:
            attend_input, sent = call(
                functools.partial(enter_kernel, False), outs, (place, stream, gain_row, offset_row),
                in_specs=[scalars()] + [vmem] * 3, out_specs=[vmem] * 2, name="enter_first")
        else:
            stream, attend_input, sent = call(
                functools.partial(enter_kernel, True), [shape((tokens, width), FULL)] + outs,
                (place, middle) + parts + (row_of(offsets_all, layer - 1, 3), gain_row, offset_row),
                in_specs=[scalars()] + [vmem] * 6, out_specs=[vmem] * 3, name="enter")
        sent = sent.reshape(rows, block, half)
        far, near = from_before(sent, 2), from_before(sent, 1)
        far_other, near_other = pair_other(far), pair_other(near)
        query, key, value, attended, log_total, wide, part = call(
            attend_kernel,
            [shape((tokens, head_cols), HALF), shape((rows, keys, head_cols), HALF), shape((rows, keys, head_cols), HALF),
             shape((tokens, head_cols), HALF), shape((tokens, 128), FULL), shape((rows, keys, width), HALF),
             shape((tokens, width), FULL)],
            (place, attend_input, far, near, far_other, near_other, held[0], head_all[layer], mask),
            in_specs=[scalars()] + [vmem] * 5 + [specs[0]] + [vmem] * 2, out_specs=[vmem] * 7, name="attend")
        before = stream
        middle, preact, part = call(
            feed_kernel,
            [shape((tokens, width), FULL), shape((tokens, hidden), FULL), shape((tokens, width), FULL)],
            (stream, part, pair_other(part), row_of(offsets_all, layer, 2), row_of(gains_all, layer, 1),
             row_of(offsets_all, layer, 1), held[1], hidden_all[layer].reshape(1, -1), held[2]),
            scratch=[pltpu.VMEM((tokens, hidden), HALF)],
            in_specs=[vmem] * 6 + [specs[1], vmem, specs[2]], out_specs=[vmem] * 3, name="feed")
        parts = (part, pair_other(part))
        kept.append((before, query, key, value, attended, log_total, wide, middle, preact))
    stream = middle + (parts[0] + parts[1]) + offsets_all[layers - 1, 3]

    pack_shape = shape((width, layers * 2 * hidden + (layers - 1) * side_cols), HALF)
    feed_blocks = layers * 2 * hidden // side_cols
    vectors = [None] * layers
    leave = None
    packed = None
    unread = pl.BlockSpec(memory_space=pl.ANY)
    for layer in reversed(range(layers)):
        before, query, key, value, attended, log_total, wide, middle, preact = kept[layer]
        held, specs = weights_of(layer)
        last = layer == layers - 1
        feed_pack_spec = pl.BlockSpec((width, 2 * hidden), functools.partial(lambda at, *_: (0, at), layer))
        shared = (middle, preact, row_of(gains_all, layer, 1), row_of(offsets_all, layer, 1), held[1], held[2])
        shared_specs = [vmem] * 4 + [specs[1], specs[2]]
        outs = [pack_shape, shape((1, hidden), FULL), shape((1, width), FULL), shape((tokens, width), HALF)]
        outs_specs = [feed_pack_spec] + [vmem] * 3
        scratch = [pltpu.VMEM((tokens, hidden), HALF)] * 2
        if last:
            upstream = cotangent.reshape(tokens, width)
            packed, hidden_sum, down_sum, part = call(
                functools.partial(feed_back_kernel, False), outs, (upstream,) + shared, scratch=scratch,
                in_specs=[vmem] + shared_specs, out_specs=outs_specs, name="feed_back_last")
        else:
            operands = leave + shared
            upstream, leave_sums, packed, hidden_sum, down_sum, part = call(
                functools.partial(feed_back_kernel, True),
                [shape((tokens, width), FULL), shape((2, width), FULL)] + outs, operands + (packed,), scratch=scratch,
                aliases={len(operands): 2},
                in_specs=[scalars()] + [vmem] * 5 + shared_specs + [unread], out_specs=[vmem] * 2 + outs_specs, name="feed_back")
            vectors[layer + 1] = (leave_sums,) + vectors[layer + 1]
        if layer == 0:
            share = lax.psum_scatter(packed, "shard", scatter_dimension=0, tiled=True)
            attend_pack = shape((shards, contexts, own, side_cols // contexts), HALF)
            attend_pack_spec = vmem
        else:
            attend_pack = pack_shape
            attend_pack_spec = pl.BlockSpec(
                (width, side_cols), functools.partial(lambda at, *_: (0, at), feed_blocks + layer - 1))
        operands = (place, upstream, middle, part, pair_other(part), row_of(gains_all, layer, 1), attended,
                    query, key, value, log_total, mask, wide, held[0])
        attend_packed, middle_back, wide_mine, wide_other, sums, head_sums = call(
            functools.partial(attend_back_kernel, layer == 0),
            [attend_pack, shape((tokens, width), FULL), shape((rows, keys, half), FULL), shape((rows, keys, half), HALF),
             shape((3, width), FULL), shape((2, head_cols), FULL)],
            operands + (() if layer == 0 else (packed,)),
            scratch=[pltpu.VMEM((tokens, head_cols), HALF), pltpu.VMEM((rows, keys, 2 * head_cols), HALF),
                     pltpu.VMEM((tokens, head_cols), HALF)],
            aliases=None if layer == 0 else {len(operands): 0},
            in_specs=[scalars()] + [vmem] * 12 + [specs[0]] + ([] if layer == 0 else [unread]),
            out_specs=[attend_pack_spec] + [vmem] * 5, name="attend_back")
        if layer == 0:
            attend_moved = lax.all_to_all(
                attend_packed.reshape((shards * contexts,) + attend_packed.shape[2:]), ("shard", "context"), 0, 0)
        else:
            packed = attend_packed
        wide_sum = wide_mine + pair_other(wide_other).astype(FULL)
        half_back = wide_sum[:, back_steps * block:]
        for steps in range(1, back_steps + 1):
            start = (back_steps - steps) * block
            half_back = half_back + from_after(wide_sum[:, start:start + block].astype(HALF), steps).astype(FULL)
        half_back = half_back.reshape(tokens, half)
        leave = (place, middle_back, before, half_back, pair_other(half_back), row_of(gains_all, layer, 0))
        vectors[layer] = (sums, down_sum, head_sums, hidden_sum)
    upstream, leave_sums = call(
        leave_kernel, [shape((tokens, width), FULL), shape((2, width), FULL)], leave,
        in_specs=[scalars()] + [vmem] * 5, out_specs=[vmem] * 2, name="leave")
    vectors[0] = (leave_sums,) + vectors[0]

    def spread_out(values, shape):
        lead = shape[:-1]
        values = values.reshape(lead + (shards, shape[-1]))
        return jnp.moveaxis(values, -2, 0).reshape(shards, -1)

    gain_sums = jnp.stack([jnp.stack([entry[0][0], entry[1][0]]) for entry in vectors])
    offset_sums = jnp.stack([jnp.concatenate([entry[0][1:2], entry[1][1:], entry[2]]) for entry in vectors])
    head_sums = jnp.stack([entry[3] for entry in vectors])
    hidden_sums = jnp.stack([entry[4] for entry in vectors])
    vector_pack = jnp.concatenate(
        [spread_out(values, part.shape) for values, part in zip((gain_sums, offset_sums, head_sums, hidden_sums), small_parts)]
        + [jnp.zeros((shards, small_padded - small_total), FULL)], axis=1)
    vector_pack, attend_moved = lax.optimization_barrier((vector_pack, attend_moved))
    vector_pack = lax.all_to_all(vector_pack.reshape(shards, -1, 128), "shard", 0, 0)
    vector_own = context_sum(jnp.sum(vector_pack, axis=0)).reshape(-1)
    vector_out = []
    for index, part in enumerate(small_parts):
        start = sum(small_sizes[:index])
        vector_out.append(vector_own[start:start + small_sizes[index]].reshape(part.shape))
    gains_grad, offsets_grad, head_grad, hidden_grad = vector_out

    share = share.reshape(own, contexts, -1).transpose(1, 0, 2)
    share = jnp.sum(lax.all_to_all(share, "context", 0, 0).astype(FULL), axis=0).astype(HALF)
    attend_sum = jnp.sum(attend_moved.astype(FULL), axis=0).astype(HALF)
    quarters = lax.all_gather(jnp.concatenate([share, attend_sum], axis=1), "context", axis=0, tiled=False).astype(FULL)
    share_cols = share.shape[1]

    def join(piece):
        return jnp.moveaxis(piece, 0, 1).reshape(own, -1)

    attend_own, share = [join(quarters[:, :, share_cols:])], join(quarters[:, :, :share_cols])
    feed_own = [share[:, 2 * hidden * layer:2 * hidden * (layer + 1)] for layer in range(layers)]
    for layer in range(1, layers):
        start = 2 * hidden * layers + side_cols * (layer - 1)
        attend_own.append(share[:, start:start + side_cols])
    projection_grad = jnp.stack(
        [jnp.stack([share[:, k * head_cols:(k + 1) * head_cols] for k in range(3)]) for share in attend_own])
    mixing_grad = jnp.stack([share[:, 3 * head_cols:].T for share in attend_own])
    expansion_grad = jnp.stack([share[:, :hidden] for share in feed_own])
    contraction_grad = jnp.stack([share[:, hidden:].T for share in feed_own])
    return (
        stream.reshape(rows, block, width),
        upstream.reshape(rows, block, width),
        projection_grad,
        head_grad,
        mixing_grad,
        expansion_grad,
        hidden_grad,
        contraction_grad,
        gains_grad,
        offsets_grad,
    )


def solution(mesh):
    in_specs = (
        P("shard", "context", None),
        P("shard", "context"),
        P(None, None, "shard", "tensor"),
        P(None, None, "tensor", "shard"),
        P(None, "tensor", "shard"),
        P(None, "shard", "tensor"),
        P(None, "tensor", "shard"),
        P(None, "tensor", "shard"),
        P(None, None, "shard"),
        P(None, None, "shard"),
        P("shard", "context", None),
    )
    out_specs = (
        P("shard", "context", None),
        P("shard", "context", None),
        P(None, None, "shard", "tensor"),
        P(None, None, "tensor", "shard"),
        P(None, "tensor", "shard"),
        P(None, "shard", "tensor"),
        P(None, "tensor", "shard"),
        P(None, "tensor", "shard"),
        P(None, None, "shard"),
        P(None, None, "shard"),
    )
    return jax.shard_map(
        per_device, mesh=mesh, in_specs=in_specs, out_specs=out_specs, check_vma=False
    )
```

```python
import functools

import jax
import jax.numpy as jnp
from jax import lax
from jax.experimental import pallas as pl
from jax.experimental.pallas import tpu as pltpu
from jax.sharding import PartitionSpec as P

HEAD = 64

EPS = 1e-05
GELU_COEF = 0.7978845608028654
GELU_CUBE = 0.044715
MASKED = -1e30
HALF = jnp.bfloat16
FULL = jnp.float32


def gelu_value(preact):
    inner_arg = GELU_COEF * (preact + GELU_CUBE * preact * preact * preact)
    return 0.5 * preact * (1.0 + jnp.tanh(inner_arg))


def norm_backward(upstream, normed, spread, gain_row):
    scaled = upstream * gain_row
    first_mean = jnp.mean(scaled, axis=-1, keepdims=True)
    second_mean = jnp.mean(scaled * normed, axis=-1, keepdims=True)
    return spread * (scaled - first_mean - normed * second_mean)


def dot(left, right, left_dim, right_dim):
    return lax.dot_general(
        left, right, (((left_dim,), (right_dim,)), ((), ())), preferred_element_type=FULL
    )


def from_before(block, steps):
    size = lax.axis_size("context")
    return lax.ppermute(block, "context", [(i, i + steps) for i in range(size - steps)])


def from_after(block, steps):
    size = lax.axis_size("context")
    return lax.ppermute(block, "context", [(i + steps, i) for i in range(size - steps)])


def context_share(parts):
    size = lax.axis_size("context")
    place = lax.axis_index("context")
    total = lax.dynamic_index_in_dim(parts, place, 0, keepdims=False).astype(FULL)
    for steps in range(1, size):
        piece = lax.dynamic_index_in_dim(parts, (place + steps) % size, 0, keepdims=False)
        total = total + lax.ppermute(piece, "context", [(i, (i + steps) % size) for i in range(size)]).astype(FULL)
    return total


def context_spread(part):
    size = lax.axis_size("context")
    return [part] + [
        lax.ppermute(part, "context", [(i, (i + steps) % size) for i in range(size)]) for steps in range(1, size)]


def context_sum(part):
    size = lax.axis_size("context")
    total = part.astype(FULL)
    for steps in range(1, size):
        moved = lax.ppermute(part, "context", [(i, (i + steps) % size) for i in range(size)])
        total = total + moved.astype(FULL)
    return total


def pair_other(part):
    size = lax.axis_size("tensor")
    return lax.ppermute(part, "tensor", [(i, (i + 1) % size) for i in range(size)])


def call(body, outs, ins, scratch=(), aliases=None, in_specs=None, out_specs=None, name=None):
    return pl.pallas_call(
        body,
        out_shape=outs,
        grid=(1,),
        in_specs=in_specs,
        out_specs=out_specs,
        scratch_shapes=list(scratch),
        input_output_aliases=aliases or {},
        compiler_params=pltpu.CompilerParams(vmem_limit_bytes=58 * 2**20),
        name=name,
    )(*ins)


def whole():
    return pl.BlockSpec(memory_space=pltpu.VMEM)


def scalars():
    return pl.BlockSpec(memory_space=pltpu.SMEM)


def shape(dims, dtype):
    return jax.ShapeDtypeStruct(dims, dtype)


def weight_spec(depth, cols, index):
    return pl.BlockSpec((depth, cols), lambda *_: (0, index))


def norm_stats(stream):
    center = stream - jnp.mean(stream, axis=-1, keepdims=True)
    spread = lax.rsqrt(jnp.mean(center * center, axis=-1, keepdims=True) + EPS)
    return center * spread, spread


def enter_kernel(has_parts, place, *refs):
    if has_parts:
        middle, mine, other, offset_last, gain, offset, stream_out, attend_out, half_out = refs
        stream = middle[...] + (mine[...] + other[...]) + offset_last[...]
        stream_out[...] = stream
    else:
        stream_in, gain, offset, attend_out, half_out = refs
        stream = stream_in[...]
    normed, _ = norm_stats(stream)
    attend = (normed * gain[...] + offset[...]).astype(HALF)
    attend_out[...] = attend
    cols = half_out.shape[1]
    half_out[...] = jnp.where(place[0] == 0, attend[:, :cols], attend[:, cols:])


def assemble(place, pieces, out):
    count, cols = len(pieces), pieces[0].shape[1]
    for index, piece in enumerate(pieces):
        source = lax.rem(place[1] + count - index, count)
        out[:, pl.ds(pl.multiple_of(source * cols, cols), cols)] = piece[...]


def attend_first_kernel(count, place, *refs):
    pieces, rest, weights = refs[:count], refs[count:-1], refs[-1]
    assemble(place, pieces, weights)
    attend_kernel(place, *rest[:5], weights, *rest[5:])


def feed_first_kernel(count, place, *refs):
    pieces, rest, up, active = refs[:count], refs[count:-2], refs[-2], refs[-1]
    assemble(place, pieces, up)
    feed_kernel(*rest[:6], up, *rest[6:], active)


def attend_kernel(place, own, far_mine, near_mine, far_other, near_other, weights, bias, visible,
                  query_out, key_out, value_out, attended_out, log_out, wide_out, part_out):
    tokens, width = own.shape
    rows, block, keys = visible.shape
    cols = query_out.shape[1]
    half = far_mine.shape[2]
    wide_out[:, keys - block:, :] = own[...].reshape(rows, block, width)

    def put(first, mine, other):
        mine, other = mine[...], other[...]
        low = place[0] == 0
        wide_out[:, first:first + block, :half] = jnp.where(low, mine, other)
        wide_out[:, first:first + block, half:] = jnp.where(low, other, mine)

    put(0, far_mine, far_other)
    put(block, near_mine, near_other)
    query_out[...] = (dot(own[...], weights[:, :cols], 1, 0) + bias[0:1, :]).astype(HALF)
    wide = wide_out[...].reshape(rows * keys, width)
    key_out[...] = dot(wide, weights[:, cols:2 * cols], 1, 0).astype(HALF).reshape(rows, keys, cols)
    value_out[...] = (dot(wide, weights[:, 2 * cols:3 * cols], 1, 0) + bias[1:2, :]).astype(HALF).reshape(rows, keys, cols)
    scale = HEAD ** (-0.5)
    pairs = cols // 128
    low_lane = lax.broadcasted_iota(jnp.int32, (block, 128), 1) < HEAD
    lane = lax.broadcasted_iota(jnp.int32, (block, 128), 1)
    log_out[...] = jnp.zeros(log_out.shape, FULL)

    def one(step, carry):
        row, pair = step // pairs, step % pairs
        at_rows = pl.ds(pl.multiple_of(row * block, block), block)
        at_cols = pl.ds(pl.multiple_of(pair * 128, 128), 128)
        query = query_out[at_rows, at_cols]
        key = key_out[row, :, at_cols]
        value = value_out[row, :, at_cols]
        shown = visible[row] > 0
        outs = []
        logs = log_out[at_rows, :]
        for which in range(2):
            picked = jnp.where(low_lane if which == 0 else ~low_lane, query, jnp.zeros_like(query))
            scores = jnp.where(shown, dot(picked, key, 1, 1) * scale, MASKED)
            top = jnp.max(scores, axis=-1, keepdims=True)
            grown = jnp.exp(scores - top)
            total = jnp.sum(grown, axis=-1, keepdims=True)
            logs = jnp.where(lane == 2 * pair + which, top + jnp.log(total), logs)
            soft = (grown * (1.0 / total)).astype(HALF)
            outs.append(dot(soft, value, 1, 0))
        log_out[at_rows, :] = logs
        attended_out[at_rows, at_cols] = jnp.where(low_lane, outs[0], outs[1]).astype(HALF)
        return carry

    lax.fori_loop(0, rows * pairs, one, 0)
    part_out[...] = dot(attended_out[...], weights[:, 3 * cols:4 * cols], 1, 1)


def feed_kernel(stream, mine, other, offset_mid, gain, offset, up, hidden_bias, down,
                middle_out, preact_out, part_out, active):
    middle = stream[...] + (mine[...] + other[...]) + offset_mid[...]
    middle_out[...] = middle
    normed, _ = norm_stats(middle)
    feed = (normed * gain[...] + offset[...]).astype(HALF)
    preact_out[...] = dot(feed, up[...], 1, 0) + hidden_bias[...]
    step_rows = 32

    def one(step, carry):
        at = pl.ds(pl.multiple_of(step * step_rows, step_rows), step_rows)
        active[at, :] = gelu_value(preact_out[at, :]).astype(HALF)
        return carry

    lax.fori_loop(0, preact_out.shape[0] // step_rows, one, 0)
    part_out[...] = dot(active[...], down[...], 1, 1)


def leave_norm(place, middle_back, stream, mine, other, gain):
    low = place[0] == 0
    mine, other = mine[...], other[...]
    back = jnp.concatenate([jnp.where(low, mine, other), jnp.where(low, other, mine)], axis=1)
    normed, spread = norm_stats(stream[...])
    upstream = middle_back[...] + norm_backward(back, normed, spread, gain[...])
    sums = jnp.concatenate(
        [jnp.sum(back * normed, axis=0, keepdims=True), jnp.sum(back, axis=0, keepdims=True)], axis=0)
    return upstream, sums


def leave_kernel(place, middle_back, stream, mine, other, gain, upstream_out, sums_out):
    upstream, sums = leave_norm(place, middle_back, stream, mine, other, gain)
    upstream_out[...] = upstream
    sums_out[...] = sums


def feed_back_kernel(has_leave, spread_pack, *refs):
    if has_leave:
        place, middle_back, stream, mine, other, gain_one = refs[:6]
        middle, preact, gain, offset, up, down = refs[6:12]
        upstream_out, sums_out, pack, hidden_sum, down_sum, part_out, active, hidden_half = refs[12:]
        upstream, sums = leave_norm(place, middle_back, stream, mine, other, gain_one)
        upstream_out[...] = upstream
        sums_out[...] = sums
    else:
        upstream_in, middle, preact, gain, offset, up, down = refs[:7]
        pack, hidden_sum, down_sum, part_out, active, hidden_half = refs[7:]
        upstream = upstream_in[...]
    hidden = up.shape[1]
    step_rows = 32
    upstream_half = upstream.astype(HALF)
    down_sum[...] = jnp.sum(upstream, axis=0, keepdims=True)
    normed, _ = norm_stats(middle[...])
    feed = (normed * gain[...] + offset[...]).astype(HALF)
    back = dot(upstream_half, down[...], 1, 0)
    hidden_sum[...] = jnp.zeros(hidden_sum.shape, FULL)
    for first in range(0, upstream.shape[0], step_rows):
        inner = slice(first, first + step_rows)
        pre = preact[inner, :]
        square = pre * pre
        tanh_value = jnp.tanh(GELU_COEF * (pre + GELU_CUBE * square * pre))
        active[inner, :] = (0.5 * pre * (1.0 + tanh_value)).astype(HALF)
        slope = 0.5 * (1.0 + tanh_value) + 0.5 * pre * (1.0 - tanh_value * tanh_value) * GELU_COEF * (
            1.0 + 3.0 * GELU_CUBE * square)
        hidden_back = back[inner, :] * slope
        hidden_sum[...] += jnp.sum(hidden_back, axis=0, keepdims=True)
        hidden_half[inner, :] = hidden_back.astype(HALF)
    part_out[...] = dot(hidden_half[...], up[...], 1, 1).astype(HALF)
    grads = (dot(feed, hidden_half[...], 0, 0).astype(HALF), dot(upstream_half, active[...], 0, 0).astype(HALF))
    for index, grad in enumerate(grads):
        if spread_pack:
            shards, count, own, cols = pack.shape
            for side in range(count // 2):
                pack[:, count // 2 * index + side] = grad[:, side * cols:(side + 1) * cols].reshape(shards, own, cols)
        else:
            pack[:, index * hidden:(index + 1) * hidden] = grad


def attend_back_kernel(spread_pack, place, upstream, middle, mine, other, gain, attended, query, key, value,
                       log_total, visible, wide, weights, *refs):
    if spread_pack:
        pack, middle_out, wide_mine, wide_other, sums_out, heads_out, wide_query, wide_both, near = refs
    else:
        _, pack, middle_out, wide_mine, wide_other, sums_out, heads_out, wide_query, wide_both, near = refs
    tokens, width = upstream.shape
    rows, block, keys = visible.shape
    cols = query.shape[1]
    scale = HEAD ** (-0.5)
    feed_back = mine[...].astype(FULL) + other[...].astype(FULL)
    normed, spread = norm_stats(middle[...])
    middle_back = upstream[...] + norm_backward(feed_back, normed, spread, gain[...])
    middle_out[...] = middle_back
    sums_out[...] = jnp.concatenate(
        [jnp.sum(feed_back * normed, axis=0, keepdims=True), jnp.sum(feed_back, axis=0, keepdims=True),
         jnp.sum(middle_back, axis=0, keepdims=True)], axis=0)
    middle_half = middle_back.astype(HALF)
    mix_grad = dot(middle_half, attended[...], 0, 0).astype(HALF)
    near[...] = dot(middle_half, weights[:, 3 * cols:4 * cols], 1, 0).astype(HALF)
    pairs = cols // 128
    low_lane = lax.broadcasted_iota(jnp.int32, (block, 128), 1) < HEAD
    low_key = lax.broadcasted_iota(jnp.int32, (keys, 128), 1) < HEAD
    lane = lax.broadcasted_iota(jnp.int32, (block, 128), 1)
    heads_out[...] = jnp.zeros(heads_out.shape, FULL)

    def one(step, carry):
        row, pair = step // pairs, step % pairs
        at_rows = pl.ds(pl.multiple_of(row * block, block), block)
        at_cols = pl.ds(pl.multiple_of(pair * 128, 128), 128)
        at_values = pl.ds(pl.multiple_of(cols + pair * 128, 128), 128)
        query_two = query[at_rows, at_cols]
        key_two, value_two = key[row, :, at_cols], value[row, :, at_cols]
        back_two = near[at_rows, at_cols]
        product = back_two.astype(FULL) * attended[at_rows, at_cols].astype(FULL)
        shown = visible[row] > 0
        logs = log_total[at_rows, :]
        query_parts, key_parts, value_parts = [], [], []
        for which in range(2):
            lanes = low_lane if which == 0 else ~low_lane
            picked = jnp.where(lanes, query_two, jnp.zeros_like(query_two))
            picked_back = jnp.where(lanes, back_two, jnp.zeros_like(back_two))
            delta = jnp.sum(jnp.where(lanes, product, 0.0), axis=-1, keepdims=True)
            own_log = jnp.sum(jnp.where(lane == 2 * pair + which, logs, 0.0), axis=-1, keepdims=True)
            scores = jnp.where(shown, dot(picked, key_two, 1, 1) * scale, MASKED)
            soft = jnp.exp(scores - own_log)
            score_back = (soft * (dot(picked_back, value_two, 1, 1) - delta) * scale).astype(HALF)
            query_parts.append(dot(score_back, key_two, 1, 0))
            key_parts.append(dot(score_back, query_two, 0, 0))
            value_parts.append(dot(soft.astype(HALF), back_two, 0, 0))
        query_back = jnp.where(low_lane, query_parts[0], query_parts[1])
        key_back = jnp.where(low_key, key_parts[0], key_parts[1])
        value_back = jnp.where(low_key, value_parts[0], value_parts[1])
        heads_out[0:1, at_cols] += jnp.sum(query_back, axis=0, keepdims=True)
        heads_out[1:2, at_cols] += jnp.sum(value_back, axis=0, keepdims=True)
        wide_query[at_rows, at_cols] = query_back.astype(HALF)
        wide_both[row, :, at_cols] = key_back.astype(HALF)
        wide_both[row, :, at_values] = value_back.astype(HALF)
        return carry

    lax.fori_loop(0, rows * pairs, one, 0)
    both = wide_both[...].reshape(rows * keys, 2 * cols)
    own = wide[:, keys - block:, :].reshape(tokens, width)
    query_grad = dot(own, wide_query[...], 0, 0).astype(HALF)
    both_grad = dot(wide[...].reshape(rows * keys, width), both, 0, 0).astype(HALF)
    grads = (query_grad, both_grad[:, :cols], both_grad[:, cols:], mix_grad)
    for index, grad in enumerate(grads):
        if spread_pack:
            pack[index] = grad
        else:
            pack[:, index * cols:(index + 1) * cols] = grad
    wide_back = dot(both, weights[:, cols:3 * cols], 1, 1).reshape(rows, keys, width)
    own_back = dot(wide_query[...], weights[:, :cols], 1, 1).reshape(rows, block, width)
    half = width // 2
    low = place[0] == 0

    def put(first, count, values):
        wide_mine[:, first:first + count, :] = jnp.where(low, values[..., :half], values[..., half:])
        wide_other[:, first:first + count, :] = jnp.where(low, values[..., half:], values[..., :half]).astype(HALF)

    put(0, keys - block, wide_back[:, :keys - block])
    put(keys - block, block, wide_back[:, keys - block:] + own_back)


def per_device(
    inputs,
    segment_ids,
    projection,
    head_bias,
    mixing,
    expansion,
    hidden_bias,
    contraction,
    norm_gains,
    offsets,
    cotangent,
):
    layers = projection.shape[0]
    rows, block, width = inputs.shape
    shards = lax.axis_size("shard")
    contexts = lax.axis_size("context")
    own = projection.shape[2]
    heads = head_bias.shape[2]
    head_cols = projection.shape[3]
    hidden = expansion.shape[2]
    tokens = rows * block
    head_scale = HEAD ** (-0.5)
    back_steps = 2

    def attend_block(layer):
        return [projection[layer, 0], projection[layer, 1], projection[layer, 2], mixing[layer].T]

    others = [contraction[0].T]
    for layer in range(1, layers):
        others += attend_block(layer) + [expansion[layer], contraction[layer].T]
    gathered = lax.all_gather(jnp.concatenate(others, axis=1), "shard", axis=0, tiled=True)
    small_parts = [norm_gains, offsets, head_bias, hidden_bias]
    small_sizes = [part.size for part in small_parts]
    small_total = sum(small_sizes)
    small_padded = -(-small_total // 1024) * 1024
    small_rows = small_padded // 128
    small = jnp.concatenate([part.reshape(-1) for part in small_parts] + [jnp.zeros((own * 128 - small_total,), HALF)])
    turn = lax.axis_index("context")
    quarter_cols, quarter_hidden = 4 * head_cols // contexts, hidden // contexts
    quarter = [
        lax.dynamic_slice_in_dim(jnp.concatenate(attend_block(0), axis=1), turn * quarter_cols, quarter_cols, 1),
        lax.dynamic_slice_in_dim(expansion[0], turn * quarter_hidden, quarter_hidden, 1), small.reshape(own, 128)]
    first = jnp.concatenate(quarter, axis=1)
    first = lax.all_to_all(jnp.broadcast_to(first[None], (shards,) + first.shape), "shard", 0, 0)
    small = first[:, :small_rows, first.shape[2] - 128:].reshape(shards, small_padded)
    first = first.reshape(shards * own, -1)
    attend_pieces = context_spread(first[:, :quarter_cols])
    up_pieces = context_spread(first[:, quarter_cols:quarter_cols + quarter_hidden])

    def widen(index):
        start = sum(small_sizes[:index])
        shape = small_parts[index].shape
        piece = small[:, start:start + small_sizes[index]].astype(FULL).reshape((shards,) + shape)
        piece = jnp.moveaxis(piece, 0, -2)
        return piece.reshape(shape[:-1] + (shards * shape[-1],))

    gains_all, offsets_all = widen(0), widen(1)
    head_all = widen(2).reshape(layers, 2, head_cols)
    hidden_all = widen(3).reshape(layers, hidden)

    seg_before = [from_before(segment_ids, steps) for steps in range(back_steps, 0, -1)]
    segments_all = jnp.concatenate(seg_before + [segment_ids], axis=1)
    query_pos = jnp.arange(block, dtype=jnp.int32) + back_steps * block
    key_pos = jnp.arange((back_steps + 1) * block, dtype=jnp.int32)
    first_key = (back_steps - lax.axis_index("context")) * block
    visible = (segments_all[:, None, :] == segment_ids[:, :, None]) & (
        key_pos[None, None, :] <= query_pos[None, :, None]
    ) & (key_pos >= first_key)[None, None, :]

    mask = visible.astype(FULL)
    keys = (back_steps + 1) * block
    half = width // 2
    place = jnp.stack([lax.axis_index("tensor"), turn]).astype(jnp.int32)
    side_cols = 4 * head_cols

    def row_of(table, layer, index):
        return table[layer, index].reshape(1, -1)

    vmem = whole()
    stream = inputs.reshape(tokens, width)
    kept = []
    parts = ()
    middle = None
    for layer in range(layers):
        outs = [shape((tokens, width), HALF), shape((tokens, half), HALF)]
        gain_row, offset_row = row_of(gains_all, layer, 0), row_of(offsets_all, layer, 0)
        if layer == 0:
            attend_input, sent = call(
                functools.partial(enter_kernel, False), outs, (place, stream, gain_row, offset_row),
                in_specs=[scalars()] + [vmem] * 3, out_specs=[vmem] * 2, name="enter_first")
        else:
            stream, attend_input, sent = call(
                functools.partial(enter_kernel, True), [shape((tokens, width), FULL)] + outs,
                (place, middle) + parts + (row_of(offsets_all, layer - 1, 3), gain_row, offset_row),
                in_specs=[scalars()] + [vmem] * 6, out_specs=[vmem] * 3, name="enter")
        sent = sent.reshape(rows, block, half)
        far, near = from_before(sent, 2), from_before(sent, 1)
        far_other, near_other = pair_other(far), pair_other(near)
        attend_outs = [
            shape((tokens, head_cols), HALF), shape((rows, keys, head_cols), HALF), shape((rows, keys, head_cols), HALF),
            shape((tokens, head_cols), HALF), shape((tokens, 128), FULL), shape((rows, keys, width), HALF),
            shape((tokens, width), FULL)]
        attend_args = (attend_input, far, near, far_other, near_other)
        feed_outs = [shape((tokens, width), FULL), shape((tokens, hidden), FULL), shape((tokens, width), FULL)]
        scratch = [pltpu.VMEM((tokens, hidden), HALF)]
        rest = (row_of(offsets_all, layer, 2), row_of(gains_all, layer, 1), row_of(offsets_all, layer, 1))
        hidden_row = hidden_all[layer].reshape(1, -1)
        if layer == 0:
            query, key, value, attended, log_total, wide, part, weights = call(
                functools.partial(attend_first_kernel, contexts), attend_outs + [shape((width, side_cols), HALF)],
                (place,) + tuple(attend_pieces) + attend_args + (head_all[layer], mask),
                in_specs=[scalars()] + [vmem] * (contexts + 7), out_specs=[vmem] * 8, name="attend_first")
            specs = (vmem, vmem, weight_spec(width, hidden, 0))
            middle, preact, part, up = call(
                functools.partial(feed_first_kernel, contexts), feed_outs + [shape((width, hidden), HALF)],
                (place,) + tuple(up_pieces) + (stream, part, pair_other(part)) + rest + (hidden_row, gathered),
                scratch=scratch, in_specs=[scalars()] + [vmem] * (contexts + 7) + [specs[2]], out_specs=[vmem] * 4,
                name="feed_first")
            held = (weights, up, gathered)
        else:
            held = (gathered,) * 3
            start = 1 + 3 * (layer - 1)
            specs = (weight_spec(width, side_cols, start), weight_spec(width, hidden, start + 1), weight_spec(width, hidden, start + 2))
            query, key, value, attended, log_total, wide, part = call(
                attend_kernel, attend_outs, (place,) + attend_args + (held[0], head_all[layer], mask),
                in_specs=[scalars()] + [vmem] * 5 + [specs[0]] + [vmem] * 2, out_specs=[vmem] * 7, name="attend")
            middle, preact, part = call(
                feed_kernel, feed_outs, (stream, part, pair_other(part)) + rest + (held[1], hidden_row, held[2]),
                scratch=scratch, in_specs=[vmem] * 6 + [specs[1], vmem, specs[2]], out_specs=[vmem] * 3, name="feed")
        before = stream
        parts = (part, pair_other(part))
        kept.append((before, query, key, value, attended, log_total, wide, middle, preact, held, specs))
    stream = middle + (parts[0] + parts[1]) + offsets_all[layers - 1, 3]

    vectors = [None] * layers
    leave = None
    shares = [None] * layers
    unread = pl.BlockSpec(memory_space=pl.ANY)
    for layer in reversed(range(layers)):
        before, query, key, value, attended, log_total, wide, middle, preact, held, specs = kept[layer]
        last = layer == layers - 1
        if layer == 0:
            feed_pack = shape((shards, contexts, own, 2 * hidden // contexts), HALF)
            attend_pack = shape((contexts, width, side_cols // contexts), HALF)
            feed_pack_spec = attend_pack_spec = vmem
        else:
            feed_pack = attend_pack = shape((width, 2 * hidden + side_cols), HALF)
            feed_pack_spec = pl.BlockSpec((width, 2 * hidden), lambda *_: (0, 0))
            attend_pack_spec = pl.BlockSpec((width, side_cols), lambda *_: (0, 2 * hidden // side_cols))
        shared = (middle, preact, row_of(gains_all, layer, 1), row_of(offsets_all, layer, 1), held[1], held[2])
        shared_specs = [vmem] * 4 + [specs[1], specs[2]]
        outs = [feed_pack, shape((1, hidden), FULL), shape((1, width), FULL), shape((tokens, width), HALF)]
        outs_specs = [feed_pack_spec] + [vmem] * 3
        scratch = [pltpu.VMEM((tokens, hidden), HALF)] * 2
        if last:
            upstream = cotangent.reshape(tokens, width)
            packed, hidden_sum, down_sum, part = call(
                functools.partial(feed_back_kernel, False, layer == 0), outs, (upstream,) + shared, scratch=scratch,
                in_specs=[vmem] + shared_specs, out_specs=outs_specs, name="feed_back_last")
        else:
            upstream, leave_sums, packed, hidden_sum, down_sum, part = call(
                functools.partial(feed_back_kernel, True, layer == 0),
                [shape((tokens, width), FULL), shape((2, width), FULL)] + outs, leave + shared, scratch=scratch,
                in_specs=[scalars()] + [vmem] * 5 + shared_specs, out_specs=[vmem] * 2 + outs_specs, name="feed_back")
            vectors[layer + 1] = (leave_sums,) + vectors[layer + 1]
        if layer == 0:
            feed_moved = lax.all_to_all(packed.reshape((shards * contexts,) + packed.shape[2:]), ("shard", "context"), 0, 0)
        operands = (place, upstream, middle, part, pair_other(part), row_of(gains_all, layer, 1), attended,
                    query, key, value, log_total, mask, wide, held[0])
        attend_packed, middle_back, wide_mine, wide_other, sums, head_sums = call(
            functools.partial(attend_back_kernel, layer == 0),
            [attend_pack, shape((tokens, width), FULL), shape((rows, keys, half), FULL), shape((rows, keys, half), HALF),
             shape((3, width), FULL), shape((2, head_cols), FULL)],
            operands + (() if layer == 0 else (packed,)),
            scratch=[pltpu.VMEM((tokens, head_cols), HALF), pltpu.VMEM((rows, keys, 2 * head_cols), HALF),
                     pltpu.VMEM((tokens, head_cols), HALF)],
            aliases=None if layer == 0 else {len(operands): 0},
            in_specs=[scalars()] + [vmem] * 12 + [specs[0]] + ([] if layer == 0 else [unread]),
            out_specs=[attend_pack_spec] + [vmem] * 5, name="attend_back")
        if layer == 0:
            attend_quarter = context_share(attend_packed).astype(HALF)
        else:
            shares[layer] = lax.psum_scatter(attend_packed, "shard", scatter_dimension=0, tiled=True)
        wide_sum = wide_mine + pair_other(wide_other).astype(FULL)
        half_back = wide_sum[:, back_steps * block:]
        for steps in range(1, back_steps + 1):
            start = (back_steps - steps) * block
            half_back = half_back + from_after(wide_sum[:, start:start + block].astype(HALF), steps).astype(FULL)
        half_back = half_back.reshape(tokens, half)
        leave = (place, middle_back, before, half_back, pair_other(half_back), row_of(gains_all, layer, 0))
        vectors[layer] = (sums, down_sum, head_sums, hidden_sum)
    upstream, leave_sums = call(
        leave_kernel, [shape((tokens, width), FULL), shape((2, width), FULL)], leave,
        in_specs=[scalars()] + [vmem] * 5, out_specs=[vmem] * 2, name="leave")
    vectors[0] = (leave_sums,) + vectors[0]

    def spread_out(values, shape):
        lead = shape[:-1]
        values = values.reshape(lead + (shards, shape[-1]))
        return jnp.moveaxis(values, -2, 0).reshape(shards, -1)

    gain_sums = jnp.stack([jnp.stack([entry[0][0], entry[1][0]]) for entry in vectors])
    offset_sums = jnp.stack([jnp.concatenate([entry[0][1:2], entry[1][1:], entry[2]]) for entry in vectors])
    head_sums = jnp.stack([entry[3] for entry in vectors])
    hidden_sums = jnp.stack([entry[4] for entry in vectors])
    vector_pack = jnp.concatenate(
        [spread_out(values, part.shape) for values, part in zip((gain_sums, offset_sums, head_sums, hidden_sums), small_parts)]
        + [jnp.zeros((shards, small_padded - small_total), FULL)], axis=1)
    vector_pack = context_sum(vector_pack.reshape(shards * small_rows, 128)).astype(HALF)
    vector_pack = jnp.pad(vector_pack.reshape(shards, small_rows, 128), ((0, 0), (0, own - small_rows), (0, 0)))
    final = jnp.concatenate([attend_quarter.reshape(shards, own, -1), vector_pack], axis=2)
    final, feed_moved = lax.optimization_barrier((final, feed_moved))
    final = jnp.sum(lax.all_to_all(final, "shard", 0, 0).astype(FULL), axis=0)
    attend_sum = final[:, :side_cols // contexts].astype(HALF)
    vector_own = final[:small_rows, side_cols // contexts:].reshape(-1)
    vector_out = []
    for index, part in enumerate(small_parts):
        start = sum(small_sizes[:index])
        vector_out.append(vector_own[start:start + small_sizes[index]].reshape(part.shape))
    gains_grad, offsets_grad, head_grad, hidden_grad = vector_out

    own_quarters = [jnp.sum(feed_moved.astype(FULL), axis=0).astype(HALF), attend_sum]
    for layer in range(1, layers):
        share = shares[layer].reshape(own, contexts, -1).transpose(1, 0, 2)
        own_quarters.append(context_share(share).astype(HALF))
    quarters = lax.all_gather(jnp.concatenate(own_quarters, axis=1), "context", axis=0, tiled=False).astype(FULL)
    joined, start = [], 0
    for piece in own_quarters:
        part = quarters[:, :, start:start + piece.shape[1]]
        joined.append(jnp.moveaxis(part, 0, 1).reshape(own, -1))
        start += piece.shape[1]
    feed_own = [joined[0]] + [share[:, :2 * hidden] for share in joined[2:]]
    attend_own = [joined[1]] + [share[:, 2 * hidden:] for share in joined[2:]]
    projection_grad = jnp.stack(
        [jnp.stack([share[:, k * head_cols:(k + 1) * head_cols] for k in range(3)]) for share in attend_own])
    mixing_grad = jnp.stack([share[:, 3 * head_cols:].T for share in attend_own])
    expansion_grad = jnp.stack([share[:, :hidden] for share in feed_own])
    contraction_grad = jnp.stack([share[:, hidden:].T for share in feed_own])
    return (
        stream.reshape(rows, block, width),
        upstream.reshape(rows, block, width),
        projection_grad,
        head_grad,
        mixing_grad,
        expansion_grad,
        hidden_grad,
        contraction_grad,
        gains_grad,
        offsets_grad,
    )


def solution(mesh):
    in_specs = (
        P("shard", "context", None),
        P("shard", "context"),
        P(None, None, "shard", "tensor"),
        P(None, None, "tensor", "shard"),
        P(None, "tensor", "shard"),
        P(None, "shard", "tensor"),
        P(None, "tensor", "shard"),
        P(None, "tensor", "shard"),
        P(None, None, "shard"),
        P(None, None, "shard"),
        P("shard", "context", None),
    )
    out_specs = (
        P("shard", "context", None),
        P("shard", "context", None),
        P(None, None, "shard", "tensor"),
        P(None, None, "tensor", "shard"),
        P(None, "tensor", "shard"),
        P(None, "shard", "tensor"),
        P(None, "tensor", "shard"),
        P(None, "tensor", "shard"),
        P(None, None, "shard"),
        P(None, None, "shard"),
    )
    return jax.shard_map(
        per_device, mesh=mesh, in_specs=in_specs, out_specs=out_specs, check_vma=False
    )
```

```python
import functools

import jax
import jax.numpy as jnp
from jax import lax
from jax.experimental import pallas as pl
from jax.experimental.pallas import tpu as pltpu
from jax.sharding import PartitionSpec as P

HEAD = 64

EPS = 1e-05
GELU_COEF = 0.7978845608028654
GELU_CUBE = 0.044715
MASKED = -1e30
HALF = jnp.bfloat16
FULL = jnp.float32


def gelu_value(preact):
    inner_arg = GELU_COEF * (preact + GELU_CUBE * preact * preact * preact)
    return 0.5 * preact * (1.0 + jnp.tanh(inner_arg))


def norm_backward(upstream, normed, spread, gain_row):
    scaled = upstream * gain_row
    first_mean = jnp.mean(scaled, axis=-1, keepdims=True)
    second_mean = jnp.mean(scaled * normed, axis=-1, keepdims=True)
    return spread * (scaled - first_mean - normed * second_mean)


def dot(left, right, left_dim, right_dim):
    return lax.dot_general(
        left, right, (((left_dim,), (right_dim,)), ((), ())), preferred_element_type=FULL
    )


def from_before(block, steps):
    size = lax.axis_size("context")
    return lax.ppermute(block, "context", [(i, i + steps) for i in range(size - steps)])


def from_after(block, steps):
    size = lax.axis_size("context")
    return lax.ppermute(block, "context", [(i + steps, i) for i in range(size - steps)])


def context_share(parts):
    size = lax.axis_size("context")
    place = lax.axis_index("context")
    total = lax.dynamic_index_in_dim(parts, place, 0, keepdims=False).astype(FULL)
    for steps in range(1, size):
        piece = lax.dynamic_index_in_dim(parts, (place + steps) % size, 0, keepdims=False)
        total = total + lax.ppermute(piece, "context", [(i, (i + steps) % size) for i in range(size)]).astype(FULL)
    return total


def context_spread(part):
    size = lax.axis_size("context")
    return [part] + [
        lax.ppermute(part, "context", [(i, (i + steps) % size) for i in range(size)]) for steps in range(1, size)]


def context_sum(part):
    size = lax.axis_size("context")
    total = part.astype(FULL)
    for steps in range(1, size):
        moved = lax.ppermute(part, "context", [(i, (i + steps) % size) for i in range(size)])
        total = total + moved.astype(FULL)
    return total


def pair_other(part):
    size = lax.axis_size("tensor")
    return lax.ppermute(part, "tensor", [(i, (i + 1) % size) for i in range(size)])


def call(body, outs, ins, scratch=(), aliases=None, in_specs=None, out_specs=None, name=None):
    return pl.pallas_call(
        body,
        out_shape=outs,
        grid=(1,),
        in_specs=in_specs,
        out_specs=out_specs,
        scratch_shapes=list(scratch),
        input_output_aliases=aliases or {},
        compiler_params=pltpu.CompilerParams(vmem_limit_bytes=58 * 2**20),
        name=name,
    )(*ins)


def whole():
    return pl.BlockSpec(memory_space=pltpu.VMEM)


def scalars():
    return pl.BlockSpec(memory_space=pltpu.SMEM)


def shape(dims, dtype):
    return jax.ShapeDtypeStruct(dims, dtype)


def weight_spec(depth, cols, index):
    return pl.BlockSpec((depth, cols), lambda *_: (0, index))


def norm_stats(stream):
    center = stream - jnp.mean(stream, axis=-1, keepdims=True)
    spread = lax.rsqrt(jnp.mean(center * center, axis=-1, keepdims=True) + EPS)
    return center * spread, spread


def enter_kernel(has_parts, place, *refs):
    if has_parts:
        middle, mine, other, offset_last, gain, offset, stream_out, attend_out, half_out = refs
        stream = middle[...] + (mine[...] + other[...]) + offset_last[...]
        stream_out[...] = stream
    else:
        stream_in, gain, offset, attend_out, half_out = refs
        stream = stream_in[...]
    normed, _ = norm_stats(stream)
    attend = (normed * gain[...] + offset[...]).astype(HALF)
    attend_out[...] = attend
    cols = half_out.shape[1]
    half_out[...] = jnp.where(place[0] == 0, attend[:, :cols], attend[:, cols:])


def assemble(place, pieces, out):
    count, cols = len(pieces), pieces[0].shape[1]
    for index, piece in enumerate(pieces):
        source = lax.rem(place[1] + count - index, count)
        out[:, pl.ds(pl.multiple_of(source * cols, cols), cols)] = piece[...]


def attend_first_kernel(count, place, *refs):
    pieces, rest, weights = refs[:count], refs[count:-1], refs[-1]
    assemble(place, pieces, weights)
    attend_kernel(place, *rest[:5], weights, *rest[5:])


def attend_kernel(place, own, far_mine, near_mine, far_other, near_other, weights, bias, visible,
                  query_out, key_out, value_out, attended_out, log_out, wide_out, part_out):
    tokens, width = own.shape
    rows, block, keys = visible.shape
    cols = query_out.shape[1]
    half = far_mine.shape[2]
    wide_out[:, keys - block:, :] = own[...].reshape(rows, block, width)

    def put(first, mine, other):
        mine, other = mine[...], other[...]
        low = place[0] == 0
        wide_out[:, first:first + block, :half] = jnp.where(low, mine, other)
        wide_out[:, first:first + block, half:] = jnp.where(low, other, mine)

    put(0, far_mine, far_other)
    put(block, near_mine, near_other)
    query_out[...] = (dot(own[...], weights[:, :cols], 1, 0) + bias[0:1, :]).astype(HALF)
    wide = wide_out[...].reshape(rows * keys, width)
    key_out[...] = dot(wide, weights[:, cols:2 * cols], 1, 0).astype(HALF).reshape(rows, keys, cols)
    value_out[...] = (dot(wide, weights[:, 2 * cols:3 * cols], 1, 0) + bias[1:2, :]).astype(HALF).reshape(rows, keys, cols)
    scale = HEAD ** (-0.5)
    pairs = cols // 128
    low_lane = lax.broadcasted_iota(jnp.int32, (block, 128), 1) < HEAD
    lane = lax.broadcasted_iota(jnp.int32, (block, 128), 1)
    log_out[...] = jnp.zeros(log_out.shape, FULL)

    def one(step, carry):
        row, pair = step // pairs, step % pairs
        at_rows = pl.ds(pl.multiple_of(row * block, block), block)
        at_cols = pl.ds(pl.multiple_of(pair * 128, 128), 128)
        query = query_out[at_rows, at_cols]
        key = key_out[row, :, at_cols]
        value = value_out[row, :, at_cols]
        shown = visible[row] > 0
        outs = []
        logs = log_out[at_rows, :]
        for which in range(2):
            picked = jnp.where(low_lane if which == 0 else ~low_lane, query, jnp.zeros_like(query))
            scores = jnp.where(shown, dot(picked, key, 1, 1) * scale, MASKED)
            top = jnp.max(scores, axis=-1, keepdims=True)
            grown = jnp.exp(scores - top)
            total = jnp.sum(grown, axis=-1, keepdims=True)
            logs = jnp.where(lane == 2 * pair + which, top + jnp.log(total), logs)
            soft = (grown * (1.0 / total)).astype(HALF)
            outs.append(dot(soft, value, 1, 0))
        log_out[at_rows, :] = logs
        attended_out[at_rows, at_cols] = jnp.where(low_lane, outs[0], outs[1]).astype(HALF)
        return carry

    lax.fori_loop(0, rows * pairs, one, 0)
    part_out[...] = dot(attended_out[...], weights[:, 3 * cols:4 * cols], 1, 1)


def feed_kernel(stream, mine, other, offset_mid, gain, offset, up, hidden_bias, down,
                middle_out, preact_out, part_out, active):
    middle = stream[...] + (mine[...] + other[...]) + offset_mid[...]
    middle_out[...] = middle
    normed, _ = norm_stats(middle)
    feed = (normed * gain[...] + offset[...]).astype(HALF)
    preact_out[...] = dot(feed, up[...], 1, 0) + hidden_bias[...]
    step_rows = 32

    def one(step, carry):
        at = pl.ds(pl.multiple_of(step * step_rows, step_rows), step_rows)
        active[at, :] = gelu_value(preact_out[at, :]).astype(HALF)
        return carry

    lax.fori_loop(0, preact_out.shape[0] // step_rows, one, 0)
    part_out[...] = dot(active[...], down[...], 1, 1)


def leave_norm(place, middle_back, stream, mine, other, gain):
    low = place[0] == 0
    mine, other = mine[...], other[...]
    back = jnp.concatenate([jnp.where(low, mine, other), jnp.where(low, other, mine)], axis=1)
    normed, spread = norm_stats(stream[...])
    upstream = middle_back[...] + norm_backward(back, normed, spread, gain[...])
    sums = jnp.concatenate(
        [jnp.sum(back * normed, axis=0, keepdims=True), jnp.sum(back, axis=0, keepdims=True)], axis=0)
    return upstream, sums


def leave_kernel(place, middle_back, stream, mine, other, gain, upstream_out, sums_out):
    upstream, sums = leave_norm(place, middle_back, stream, mine, other, gain)
    upstream_out[...] = upstream
    sums_out[...] = sums


def feed_back_kernel(has_leave, *refs):
    if has_leave:
        place, middle_back, stream, mine, other, gain_one = refs[:6]
        middle, preact, gain, offset, up, down, _ = refs[6:13]
        upstream_out, sums_out, pack, hidden_sum, down_sum, part_out, active, hidden_half = refs[13:]
        upstream, sums = leave_norm(place, middle_back, stream, mine, other, gain_one)
        upstream_out[...] = upstream
        sums_out[...] = sums
    else:
        upstream_in, middle, preact, gain, offset, up, down = refs[:7]
        pack, hidden_sum, down_sum, part_out, active, hidden_half = refs[7:]
        upstream = upstream_in[...]
    hidden = up.shape[1]
    step_rows = 32
    upstream_half = upstream.astype(HALF)
    down_sum[...] = jnp.sum(upstream, axis=0, keepdims=True)
    normed, _ = norm_stats(middle[...])
    feed = (normed * gain[...] + offset[...]).astype(HALF)
    back = dot(upstream_half, down[...], 1, 0)
    hidden_sum[...] = jnp.zeros(hidden_sum.shape, FULL)
    for first in range(0, upstream.shape[0], step_rows):
        inner = slice(first, first + step_rows)
        pre = preact[inner, :]
        square = pre * pre
        tanh_value = jnp.tanh(GELU_COEF * (pre + GELU_CUBE * square * pre))
        active[inner, :] = (0.5 * pre * (1.0 + tanh_value)).astype(HALF)
        slope = 0.5 * (1.0 + tanh_value) + 0.5 * pre * (1.0 - tanh_value * tanh_value) * GELU_COEF * (
            1.0 + 3.0 * GELU_CUBE * square)
        hidden_back = back[inner, :] * slope
        hidden_sum[...] += jnp.sum(hidden_back, axis=0, keepdims=True)
        hidden_half[inner, :] = hidden_back.astype(HALF)
    part_out[...] = dot(hidden_half[...], up[...], 1, 1).astype(HALF)
    pack[:, :hidden] = dot(feed, hidden_half[...], 0, 0).astype(HALF)
    pack[:, hidden:2 * hidden] = dot(upstream_half, active[...], 0, 0).astype(HALF)


def attend_back_kernel(spread_pack, place, upstream, middle, mine, other, gain, attended, query, key, value,
                       log_total, visible, wide, weights, *refs):
    if spread_pack:
        pack, middle_out, wide_mine, wide_other, sums_out, heads_out, wide_query, wide_both, near = refs
    else:
        _, pack, middle_out, wide_mine, wide_other, sums_out, heads_out, wide_query, wide_both, near = refs
    tokens, width = upstream.shape
    rows, block, keys = visible.shape
    cols = query.shape[1]
    scale = HEAD ** (-0.5)
    feed_back = mine[...].astype(FULL) + other[...].astype(FULL)
    normed, spread = norm_stats(middle[...])
    middle_back = upstream[...] + norm_backward(feed_back, normed, spread, gain[...])
    middle_out[...] = middle_back
    sums_out[...] = jnp.concatenate(
        [jnp.sum(feed_back * normed, axis=0, keepdims=True), jnp.sum(feed_back, axis=0, keepdims=True),
         jnp.sum(middle_back, axis=0, keepdims=True)], axis=0)
    middle_half = middle_back.astype(HALF)
    mix_grad = dot(middle_half, attended[...], 0, 0).astype(HALF)
    near[...] = dot(middle_half, weights[:, 3 * cols:4 * cols], 1, 0).astype(HALF)
    pairs = cols // 128
    low_lane = lax.broadcasted_iota(jnp.int32, (block, 128), 1) < HEAD
    low_key = lax.broadcasted_iota(jnp.int32, (keys, 128), 1) < HEAD
    lane = lax.broadcasted_iota(jnp.int32, (block, 128), 1)
    heads_out[...] = jnp.zeros(heads_out.shape, FULL)

    def one(step, carry):
        row, pair = step // pairs, step % pairs
        at_rows = pl.ds(pl.multiple_of(row * block, block), block)
        at_cols = pl.ds(pl.multiple_of(pair * 128, 128), 128)
        at_values = pl.ds(pl.multiple_of(cols + pair * 128, 128), 128)
        query_two = query[at_rows, at_cols]
        key_two, value_two = key[row, :, at_cols], value[row, :, at_cols]
        back_two = near[at_rows, at_cols]
        product = back_two.astype(FULL) * attended[at_rows, at_cols].astype(FULL)
        shown = visible[row] > 0
        logs = log_total[at_rows, :]
        query_parts, key_parts, value_parts = [], [], []
        for which in range(2):
            lanes = low_lane if which == 0 else ~low_lane
            picked = jnp.where(lanes, query_two, jnp.zeros_like(query_two))
            picked_back = jnp.where(lanes, back_two, jnp.zeros_like(back_two))
            delta = jnp.sum(jnp.where(lanes, product, 0.0), axis=-1, keepdims=True)
            own_log = jnp.sum(jnp.where(lane == 2 * pair + which, logs, 0.0), axis=-1, keepdims=True)
            scores = jnp.where(shown, dot(picked, key_two, 1, 1) * scale, MASKED)
            soft = jnp.exp(scores - own_log)
            score_back = (soft * (dot(picked_back, value_two, 1, 1) - delta) * scale).astype(HALF)
            query_parts.append(dot(score_back, key_two, 1, 0))
            key_parts.append(dot(score_back, query_two, 0, 0))
            value_parts.append(dot(soft.astype(HALF), back_two, 0, 0))
        query_back = jnp.where(low_lane, query_parts[0], query_parts[1])
        key_back = jnp.where(low_key, key_parts[0], key_parts[1])
        value_back = jnp.where(low_key, value_parts[0], value_parts[1])
        heads_out[0:1, at_cols] += jnp.sum(query_back, axis=0, keepdims=True)
        heads_out[1:2, at_cols] += jnp.sum(value_back, axis=0, keepdims=True)
        wide_query[at_rows, at_cols] = query_back.astype(HALF)
        wide_both[row, :, at_cols] = key_back.astype(HALF)
        wide_both[row, :, at_values] = value_back.astype(HALF)
        return carry

    lax.fori_loop(0, rows * pairs, one, 0)
    both = wide_both[...].reshape(rows * keys, 2 * cols)
    own = wide[:, keys - block:, :].reshape(tokens, width)
    query_grad = dot(own, wide_query[...], 0, 0).astype(HALF)
    both_grad = dot(wide[...].reshape(rows * keys, width), both, 0, 0).astype(HALF)
    grads = (query_grad, both_grad[:, :cols], both_grad[:, cols:], mix_grad)
    for index, grad in enumerate(grads):
        if spread_pack:
            pack[index] = grad
        else:
            pack[:, index * cols:(index + 1) * cols] = grad
    wide_back = dot(both, weights[:, cols:3 * cols], 1, 1).reshape(rows, keys, width)
    own_back = dot(wide_query[...], weights[:, :cols], 1, 1).reshape(rows, block, width)
    half = width // 2
    low = place[0] == 0

    def put(first, count, values):
        wide_mine[:, first:first + count, :] = jnp.where(low, values[..., :half], values[..., half:])
        wide_other[:, first:first + count, :] = jnp.where(low, values[..., half:], values[..., :half]).astype(HALF)

    put(0, keys - block, wide_back[:, :keys - block])
    put(keys - block, block, wide_back[:, keys - block:] + own_back)


def per_device(
    inputs,
    segment_ids,
    projection,
    head_bias,
    mixing,
    expansion,
    hidden_bias,
    contraction,
    norm_gains,
    offsets,
    cotangent,
):
    layers = projection.shape[0]
    rows, block, width = inputs.shape
    shards = lax.axis_size("shard")
    contexts = lax.axis_size("context")
    own = projection.shape[2]
    heads = head_bias.shape[2]
    head_cols = projection.shape[3]
    hidden = expansion.shape[2]
    tokens = rows * block
    head_scale = HEAD ** (-0.5)
    back_steps = 2

    def attend_block(layer):
        return [projection[layer, 0], projection[layer, 1], projection[layer, 2], mixing[layer].T]

    others = [expansion[0], contraction[0].T]
    for layer in range(1, layers):
        others += attend_block(layer) + [expansion[layer], contraction[layer].T]
    gathered = lax.all_gather(jnp.concatenate(others, axis=1), "shard", axis=0, tiled=True)
    small_parts = [norm_gains, offsets, head_bias, hidden_bias]
    small_sizes = [part.size for part in small_parts]
    small_total = sum(small_sizes)
    small_padded = -(-small_total // 1024) * 1024
    small_rows = small_padded // 128
    small = jnp.concatenate([part.reshape(-1) for part in small_parts] + [jnp.zeros((own * 128 - small_total,), HALF)])
    turn = lax.axis_index("context")
    quarter_cols = 4 * head_cols // contexts
    first = jnp.concatenate([
        lax.dynamic_slice_in_dim(jnp.concatenate(attend_block(0), axis=1), turn * quarter_cols, quarter_cols, 1),
        small.reshape(own, 128)], axis=1)
    first = lax.all_to_all(jnp.broadcast_to(first[None], (shards,) + first.shape), "shard", 0, 0)
    small = first[:, :small_rows, first.shape[2] - 128:].reshape(shards, small_padded)
    attend_pieces = context_spread(first.reshape(shards * own, -1)[:, :quarter_cols])

    def widen(index):
        start = sum(small_sizes[:index])
        shape = small_parts[index].shape
        piece = small[:, start:start + small_sizes[index]].astype(FULL).reshape((shards,) + shape)
        piece = jnp.moveaxis(piece, 0, -2)
        return piece.reshape(shape[:-1] + (shards * shape[-1],))

    gains_all, offsets_all = widen(0), widen(1)
    head_all = widen(2).reshape(layers, 2, head_cols)
    hidden_all = widen(3).reshape(layers, hidden)

    seg_before = [from_before(segment_ids, steps) for steps in range(back_steps, 0, -1)]
    segments_all = jnp.concatenate(seg_before + [segment_ids], axis=1)
    query_pos = jnp.arange(block, dtype=jnp.int32) + back_steps * block
    key_pos = jnp.arange((back_steps + 1) * block, dtype=jnp.int32)
    first_key = (back_steps - lax.axis_index("context")) * block
    visible = (segments_all[:, None, :] == segment_ids[:, :, None]) & (
        key_pos[None, None, :] <= query_pos[None, :, None]
    ) & (key_pos >= first_key)[None, None, :]

    mask = visible.astype(FULL)
    keys = (back_steps + 1) * block
    half = width // 2
    place = jnp.stack([lax.axis_index("tensor"), turn]).astype(jnp.int32)
    side_cols = 4 * head_cols

    def row_of(table, layer, index):
        return table[layer, index].reshape(1, -1)

    def gathered_spec(layer, member):
        at = member if layer == 0 else 2 + 3 * (layer - 1) + member
        return weight_spec(width, side_cols, at)

    vmem = whole()
    stream = inputs.reshape(tokens, width)
    kept = []
    parts = ()
    middle = None
    for layer in range(layers):
        outs = [shape((tokens, width), HALF), shape((tokens, half), HALF)]
        gain_row, offset_row = row_of(gains_all, layer, 0), row_of(offsets_all, layer, 0)
        if layer == 0:
            attend_input, sent = call(
                functools.partial(enter_kernel, False), outs, (place, stream, gain_row, offset_row),
                in_specs=[scalars()] + [vmem] * 3, out_specs=[vmem] * 2, name="enter_first")
        else:
            stream, attend_input, sent = call(
                functools.partial(enter_kernel, True), [shape((tokens, width), FULL)] + outs,
                (place, middle) + parts + (row_of(offsets_all, layer - 1, 3), gain_row, offset_row),
                in_specs=[scalars()] + [vmem] * 6, out_specs=[vmem] * 3, name="enter")
        sent = sent.reshape(rows, block, half)
        far, near = from_before(sent, 2), from_before(sent, 1)
        far_other, near_other = pair_other(far), pair_other(near)
        attend_outs = [
            shape((tokens, head_cols), HALF), shape((rows, keys, head_cols), HALF), shape((rows, keys, head_cols), HALF),
            shape((tokens, head_cols), HALF), shape((tokens, 128), FULL), shape((rows, keys, width), HALF),
            shape((tokens, width), FULL)]
        attend_args = (attend_input, far, near, far_other, near_other)
        if layer == 0:
            query, key, value, attended, log_total, wide, part, weights = call(
                functools.partial(attend_first_kernel, contexts), attend_outs + [shape((width, side_cols), HALF)],
                (place,) + tuple(attend_pieces) + attend_args + (head_all[layer], mask),
                in_specs=[scalars()] + [vmem] * (contexts + 7), out_specs=[vmem] * 8, name="attend_first")
            held = (weights, gathered, gathered)
            specs = (vmem, gathered_spec(0, 0), gathered_spec(0, 1))
        else:
            held = (gathered,) * 3
            specs = tuple(gathered_spec(layer, member) for member in range(3))
            query, key, value, attended, log_total, wide, part = call(
                attend_kernel, attend_outs, (place,) + attend_args + (held[0], head_all[layer], mask),
                in_specs=[scalars()] + [vmem] * 5 + [specs[0]] + [vmem] * 2, out_specs=[vmem] * 7, name="attend")
        before = stream
        middle, preact, part = call(
            feed_kernel,
            [shape((tokens, width), FULL), shape((tokens, hidden), FULL), shape((tokens, width), FULL)],
            (stream, part, pair_other(part), row_of(offsets_all, layer, 2), row_of(gains_all, layer, 1),
             row_of(offsets_all, layer, 1), held[1], hidden_all[layer].reshape(1, -1), held[2]),
            scratch=[pltpu.VMEM((tokens, hidden), HALF)],
            in_specs=[vmem] * 6 + [specs[1], vmem, specs[2]], out_specs=[vmem] * 3, name="feed")
        parts = (part, pair_other(part))
        kept.append((before, query, key, value, attended, log_total, wide, middle, preact, held, specs))
    stream = middle + (parts[0] + parts[1]) + offsets_all[layers - 1, 3]

    pack_shape = shape((width, layers * 2 * hidden + (layers - 1) * side_cols), HALF)
    feed_blocks = layers * 2 * hidden // side_cols
    vectors = [None] * layers
    leave = None
    packed = None
    unread = pl.BlockSpec(memory_space=pl.ANY)
    for layer in reversed(range(layers)):
        before, query, key, value, attended, log_total, wide, middle, preact, held, specs = kept[layer]
        last = layer == layers - 1
        feed_pack_spec = pl.BlockSpec((width, 2 * hidden), functools.partial(lambda at, *_: (0, at), layer))
        shared = (middle, preact, row_of(gains_all, layer, 1), row_of(offsets_all, layer, 1), held[1], held[2])
        shared_specs = [vmem] * 4 + [specs[1], specs[2]]
        outs = [pack_shape, shape((1, hidden), FULL), shape((1, width), FULL), shape((tokens, width), HALF)]
        outs_specs = [feed_pack_spec] + [vmem] * 3
        scratch = [pltpu.VMEM((tokens, hidden), HALF)] * 2
        if last:
            upstream = cotangent.reshape(tokens, width)
            packed, hidden_sum, down_sum, part = call(
                functools.partial(feed_back_kernel, False), outs, (upstream,) + shared, scratch=scratch,
                in_specs=[vmem] + shared_specs, out_specs=outs_specs, name="feed_back_last")
        else:
            operands = leave + shared
            upstream, leave_sums, packed, hidden_sum, down_sum, part = call(
                functools.partial(feed_back_kernel, True),
                [shape((tokens, width), FULL), shape((2, width), FULL)] + outs, operands + (packed,), scratch=scratch,
                aliases={len(operands): 2},
                in_specs=[scalars()] + [vmem] * 5 + shared_specs + [unread], out_specs=[vmem] * 2 + outs_specs, name="feed_back")
            vectors[layer + 1] = (leave_sums,) + vectors[layer + 1]
        if layer == 0:
            share = lax.psum_scatter(packed, "shard", scatter_dimension=0, tiled=True)
            attend_pack = shape((contexts, width, side_cols // contexts), HALF)
            attend_pack_spec = vmem
        else:
            attend_pack = pack_shape
            attend_pack_spec = pl.BlockSpec(
                (width, side_cols), functools.partial(lambda at, *_: (0, at), feed_blocks + layer - 1))
        operands = (place, upstream, middle, part, pair_other(part), row_of(gains_all, layer, 1), attended,
                    query, key, value, log_total, mask, wide, held[0])
        attend_packed, middle_back, wide_mine, wide_other, sums, head_sums = call(
            functools.partial(attend_back_kernel, layer == 0),
            [attend_pack, shape((tokens, width), FULL), shape((rows, keys, half), FULL), shape((rows, keys, half), HALF),
             shape((3, width), FULL), shape((2, head_cols), FULL)],
            operands + (() if layer == 0 else (packed,)),
            scratch=[pltpu.VMEM((tokens, head_cols), HALF), pltpu.VMEM((rows, keys, 2 * head_cols), HALF),
                     pltpu.VMEM((tokens, head_cols), HALF)],
            aliases=None if layer == 0 else {len(operands): 0},
            in_specs=[scalars()] + [vmem] * 12 + [specs[0]] + ([] if layer == 0 else [unread]),
            out_specs=[attend_pack_spec] + [vmem] * 5, name="attend_back")
        if layer == 0:
            attend_quarter = context_share(attend_packed).astype(HALF)
        else:
            packed = attend_packed
        wide_sum = wide_mine + pair_other(wide_other).astype(FULL)
        half_back = wide_sum[:, back_steps * block:]
        for steps in range(1, back_steps + 1):
            start = (back_steps - steps) * block
            half_back = half_back + from_after(wide_sum[:, start:start + block].astype(HALF), steps).astype(FULL)
        half_back = half_back.reshape(tokens, half)
        leave = (place, middle_back, before, half_back, pair_other(half_back), row_of(gains_all, layer, 0))
        vectors[layer] = (sums, down_sum, head_sums, hidden_sum)
    upstream, leave_sums = call(
        leave_kernel, [shape((tokens, width), FULL), shape((2, width), FULL)], leave,
        in_specs=[scalars()] + [vmem] * 5, out_specs=[vmem] * 2, name="leave")
    vectors[0] = (leave_sums,) + vectors[0]

    def spread_out(values, shape):
        lead = shape[:-1]
        values = values.reshape(lead + (shards, shape[-1]))
        return jnp.moveaxis(values, -2, 0).reshape(shards, -1)

    gain_sums = jnp.stack([jnp.stack([entry[0][0], entry[1][0]]) for entry in vectors])
    offset_sums = jnp.stack([jnp.concatenate([entry[0][1:2], entry[1][1:], entry[2]]) for entry in vectors])
    head_sums = jnp.stack([entry[3] for entry in vectors])
    hidden_sums = jnp.stack([entry[4] for entry in vectors])
    vector_pack = jnp.concatenate(
        [spread_out(values, part.shape) for values, part in zip((gain_sums, offset_sums, head_sums, hidden_sums), small_parts)]
        + [jnp.zeros((shards, small_padded - small_total), FULL)], axis=1)
    vector_pack = context_sum(vector_pack.reshape(shards * small_rows, 128)).astype(HALF)
    vector_pack = jnp.pad(vector_pack.reshape(shards, small_rows, 128), ((0, 0), (0, own - small_rows), (0, 0)))
    final = jnp.concatenate([attend_quarter.reshape(shards, own, -1), vector_pack], axis=2)
    final = jnp.sum(lax.all_to_all(final, "shard", 0, 0).astype(FULL), axis=0)
    attend_sum = final[:, :side_cols // contexts].astype(HALF)
    vector_own = final[:small_rows, side_cols // contexts:].reshape(-1)
    vector_out = []
    for index, part in enumerate(small_parts):
        start = sum(small_sizes[:index])
        vector_out.append(vector_own[start:start + small_sizes[index]].reshape(part.shape))
    gains_grad, offsets_grad, head_grad, hidden_grad = vector_out

    share = share.reshape(own, contexts, -1).transpose(1, 0, 2)
    share = jnp.sum(lax.all_to_all(share, "context", 0, 0).astype(FULL), axis=0).astype(HALF)
    quarters = lax.all_gather(jnp.concatenate([share, attend_sum], axis=1), "context", axis=0, tiled=False).astype(FULL)
    share_cols = share.shape[1]

    def join(piece):
        return jnp.moveaxis(piece, 0, 1).reshape(own, -1)

    attend_own, share = [join(quarters[:, :, share_cols:])], join(quarters[:, :, :share_cols])
    feed_own = [share[:, 2 * hidden * layer:2 * hidden * (layer + 1)] for layer in range(layers)]
    for layer in range(1, layers):
        start = 2 * hidden * layers + side_cols * (layer - 1)
        attend_own.append(share[:, start:start + side_cols])
    projection_grad = jnp.stack(
        [jnp.stack([share[:, k * head_cols:(k + 1) * head_cols] for k in range(3)]) for share in attend_own])
    mixing_grad = jnp.stack([share[:, 3 * head_cols:].T for share in attend_own])
    expansion_grad = jnp.stack([share[:, :hidden] for share in feed_own])
    contraction_grad = jnp.stack([share[:, hidden:].T for share in feed_own])
    return (
        stream.reshape(rows, block, width),
        upstream.reshape(rows, block, width),
        projection_grad,
        head_grad,
        mixing_grad,
        expansion_grad,
        hidden_grad,
        contraction_grad,
        gains_grad,
        offsets_grad,
    )


def solution(mesh):
    in_specs = (
        P("shard", "context", None),
        P("shard", "context"),
        P(None, None, "shard", "tensor"),
        P(None, None, "tensor", "shard"),
        P(None, "tensor", "shard"),
        P(None, "shard", "tensor"),
        P(None, "tensor", "shard"),
        P(None, "tensor", "shard"),
        P(None, None, "shard"),
        P(None, None, "shard"),
        P("shard", "context", None),
    )
    out_specs = (
        P("shard", "context", None),
        P("shard", "context", None),
        P(None, None, "shard", "tensor"),
        P(None, None, "tensor", "shard"),
        P(None, "tensor", "shard"),
        P(None, "shard", "tensor"),
        P(None, "tensor", "shard"),
        P(None, "tensor", "shard"),
        P(None, None, "shard"),
        P(None, None, "shard"),
    )
    return jax.shard_map(
        per_device, mesh=mesh, in_specs=in_specs, out_specs=out_specs, check_vma=False
    )
```

```python
import functools

import jax
import jax.numpy as jnp
from jax import lax
from jax.experimental import pallas as pl
from jax.experimental.pallas import tpu as pltpu
from jax.sharding import PartitionSpec as P

HEAD = 64

EPS = 1e-05
GELU_COEF = 0.7978845608028654
GELU_CUBE = 0.044715
MASKED = -1e30
HALF = jnp.bfloat16
FULL = jnp.float32


def gelu_value(preact):
    inner_arg = GELU_COEF * (preact + GELU_CUBE * preact * preact * preact)
    return 0.5 * preact * (1.0 + jnp.tanh(inner_arg))


def norm_backward(upstream, normed, spread, gain_row):
    scaled = upstream * gain_row
    first_mean = jnp.mean(scaled, axis=-1, keepdims=True)
    second_mean = jnp.mean(scaled * normed, axis=-1, keepdims=True)
    return spread * (scaled - first_mean - normed * second_mean)


def dot(left, right, left_dim, right_dim):
    return lax.dot_general(
        left, right, (((left_dim,), (right_dim,)), ((), ())), preferred_element_type=FULL
    )


def from_before(block, steps):
    size = lax.axis_size("context")
    return lax.ppermute(block, "context", [(i, i + steps) for i in range(size - steps)])


def from_after(block, steps):
    size = lax.axis_size("context")
    return lax.ppermute(block, "context", [(i + steps, i) for i in range(size - steps)])


def context_share(parts):
    size = lax.axis_size("context")
    place = lax.axis_index("context")
    total = lax.dynamic_index_in_dim(parts, place, 0, keepdims=False).astype(FULL)
    for steps in range(1, size):
        piece = lax.dynamic_index_in_dim(parts, (place + steps) % size, 0, keepdims=False)
        total = total + lax.ppermute(piece, "context", [(i, (i + steps) % size) for i in range(size)]).astype(FULL)
    return total


def context_spread(part):
    size = lax.axis_size("context")
    return [part] + [
        lax.ppermute(part, "context", [(i, (i + steps) % size) for i in range(size)]) for steps in range(1, size)]


def context_sum(part):
    size = lax.axis_size("context")
    total = part.astype(FULL)
    for steps in range(1, size):
        moved = lax.ppermute(part, "context", [(i, (i + steps) % size) for i in range(size)])
        total = total + moved.astype(FULL)
    return total


def pair_other(part):
    size = lax.axis_size("tensor")
    return lax.ppermute(part, "tensor", [(i, (i + 1) % size) for i in range(size)])


def call(body, outs, ins, scratch=(), aliases=None, in_specs=None, out_specs=None, name=None):
    return pl.pallas_call(
        body,
        out_shape=outs,
        grid=(1,),
        in_specs=in_specs,
        out_specs=out_specs,
        scratch_shapes=list(scratch),
        input_output_aliases=aliases or {},
        compiler_params=pltpu.CompilerParams(vmem_limit_bytes=58 * 2**20),
        name=name,
    )(*ins)


def whole():
    return pl.BlockSpec(memory_space=pltpu.VMEM)


def scalars():
    return pl.BlockSpec(memory_space=pltpu.SMEM)


def shape(dims, dtype):
    return jax.ShapeDtypeStruct(dims, dtype)


def weight_spec(depth, cols, index):
    return pl.BlockSpec((depth, cols), lambda *_: (0, index))


def norm_stats(stream):
    center = stream - jnp.mean(stream, axis=-1, keepdims=True)
    spread = lax.rsqrt(jnp.mean(center * center, axis=-1, keepdims=True) + EPS)
    return center * spread, spread


def enter_kernel(has_parts, place, *refs):
    if has_parts:
        middle, mine, other, offset_last, gain, offset, stream_out, attend_out, half_out = refs
        stream = middle[...] + (mine[...] + other[...]) + offset_last[...]
        stream_out[...] = stream
    else:
        stream_in, gain, offset, attend_out, half_out = refs
        stream = stream_in[...]
    normed, _ = norm_stats(stream)
    attend = (normed * gain[...] + offset[...]).astype(HALF)
    attend_out[...] = attend
    cols = half_out.shape[1]
    half_out[...] = jnp.where(place[0] == 0, attend[:, :cols], attend[:, cols:])


def assemble(place, pieces, out):
    count, cols = len(pieces), pieces[0].shape[1]
    for index, piece in enumerate(pieces):
        source = lax.rem(place[1] + count - index, count)
        out[:, pl.ds(pl.multiple_of(source * cols, cols), cols)] = piece[...]


def attend_first_kernel(count, place, *refs):
    pieces, rest, weights = refs[:count], refs[count:-1], refs[-1]
    assemble(place, pieces, weights)
    attend_kernel(place, *rest[:5], weights, *rest[5:])


def attend_kernel(place, own, far_mine, near_mine, far_other, near_other, weights, bias, visible,
                  query_out, key_out, value_out, attended_out, log_out, wide_out, part_out):
    tokens, width = own.shape
    rows, block, keys = visible.shape
    cols = query_out.shape[1]
    half = far_mine.shape[2]
    wide_out[:, keys - block:, :] = own[...].reshape(rows, block, width)

    def put(first, mine, other):
        mine, other = mine[...], other[...]
        low = place[0] == 0
        wide_out[:, first:first + block, :half] = jnp.where(low, mine, other)
        wide_out[:, first:first + block, half:] = jnp.where(low, other, mine)

    put(0, far_mine, far_other)
    put(block, near_mine, near_other)
    query_out[...] = (dot(own[...], weights[:, :cols], 1, 0) + bias[0:1, :]).astype(HALF)
    wide = wide_out[...].reshape(rows * keys, width)
    key_out[...] = dot(wide, weights[:, cols:2 * cols], 1, 0).astype(HALF).reshape(rows, keys, cols)
    value_out[...] = (dot(wide, weights[:, 2 * cols:3 * cols], 1, 0) + bias[1:2, :]).astype(HALF).reshape(rows, keys, cols)
    scale = HEAD ** (-0.5)
    pairs = cols // 128
    low_lane = lax.broadcasted_iota(jnp.int32, (block, 128), 1) < HEAD
    lane = lax.broadcasted_iota(jnp.int32, (block, 128), 1)
    log_out[...] = jnp.zeros(log_out.shape, FULL)

    def one(step, carry):
        row, pair = step // pairs, step % pairs
        at_rows = pl.ds(pl.multiple_of(row * block, block), block)
        at_cols = pl.ds(pl.multiple_of(pair * 128, 128), 128)
        query = query_out[at_rows, at_cols]
        key = key_out[row, :, at_cols]
        value = value_out[row, :, at_cols]
        shown = visible[row] > 0
        outs = []
        logs = log_out[at_rows, :]
        for which in range(2):
            picked = jnp.where(low_lane if which == 0 else ~low_lane, query, jnp.zeros_like(query))
            scores = jnp.where(shown, dot(picked, key, 1, 1) * scale, MASKED)
            top = jnp.max(scores, axis=-1, keepdims=True)
            grown = jnp.exp(scores - top)
            total = jnp.sum(grown, axis=-1, keepdims=True)
            logs = jnp.where(lane == 2 * pair + which, top + jnp.log(total), logs)
            soft = (grown * (1.0 / total)).astype(HALF)
            outs.append(dot(soft, value, 1, 0))
        log_out[at_rows, :] = logs
        attended_out[at_rows, at_cols] = jnp.where(low_lane, outs[0], outs[1]).astype(HALF)
        return carry

    lax.fori_loop(0, rows * pairs, one, 0)
    part_out[...] = dot(attended_out[...], weights[:, 3 * cols:4 * cols], 1, 1)


def feed_kernel(stream, mine, other, offset_mid, gain, offset, up, hidden_bias, down,
                middle_out, preact_out, part_out, active):
    middle = stream[...] + (mine[...] + other[...]) + offset_mid[...]
    middle_out[...] = middle
    normed, _ = norm_stats(middle)
    feed = (normed * gain[...] + offset[...]).astype(HALF)
    preact_out[...] = dot(feed, up[...], 1, 0) + hidden_bias[...]
    step_rows = 32

    def one(step, carry):
        at = pl.ds(pl.multiple_of(step * step_rows, step_rows), step_rows)
        active[at, :] = gelu_value(preact_out[at, :]).astype(HALF)
        return carry

    lax.fori_loop(0, preact_out.shape[0] // step_rows, one, 0)
    part_out[...] = dot(active[...], down[...], 1, 1)


def leave_norm(place, middle_back, stream, mine, other, gain):
    low = place[0] == 0
    mine, other = mine[...], other[...]
    back = jnp.concatenate([jnp.where(low, mine, other), jnp.where(low, other, mine)], axis=1)
    normed, spread = norm_stats(stream[...])
    upstream = middle_back[...] + norm_backward(back, normed, spread, gain[...])
    sums = jnp.concatenate(
        [jnp.sum(back * normed, axis=0, keepdims=True), jnp.sum(back, axis=0, keepdims=True)], axis=0)
    return upstream, sums


def leave_kernel(place, middle_back, stream, mine, other, gain, upstream_out, sums_out):
    upstream, sums = leave_norm(place, middle_back, stream, mine, other, gain)
    upstream_out[...] = upstream
    sums_out[...] = sums


def feed_back_kernel(has_leave, spread_pack, *refs):
    if has_leave:
        place, middle_back, stream, mine, other, gain_one = refs[:6]
        middle, preact, gain, offset, up, down = refs[6:12]
        upstream_out, sums_out = refs[12:14]
        rest = refs[14:]
        upstream, sums = leave_norm(place, middle_back, stream, mine, other, gain_one)
        upstream_out[...] = upstream
        sums_out[...] = sums
    else:
        upstream_in, middle, preact, gain, offset, up, down = refs[:7]
        rest = refs[7:]
        upstream = upstream_in[...]
    packs, (hidden_sum, down_sum, part_out, active, hidden_half) = rest[:-5], rest[-5:]
    hidden = up.shape[1]
    step_rows = 32
    upstream_half = upstream.astype(HALF)
    down_sum[...] = jnp.sum(upstream, axis=0, keepdims=True)
    normed, _ = norm_stats(middle[...])
    feed = (normed * gain[...] + offset[...]).astype(HALF)
    back = dot(upstream_half, down[...], 1, 0)
    hidden_sum[...] = jnp.zeros(hidden_sum.shape, FULL)
    for first in range(0, upstream.shape[0], step_rows):
        inner = slice(first, first + step_rows)
        pre = preact[inner, :]
        square = pre * pre
        tanh_value = jnp.tanh(GELU_COEF * (pre + GELU_CUBE * square * pre))
        active[inner, :] = (0.5 * pre * (1.0 + tanh_value)).astype(HALF)
        slope = 0.5 * (1.0 + tanh_value) + 0.5 * pre * (1.0 - tanh_value * tanh_value) * GELU_COEF * (
            1.0 + 3.0 * GELU_CUBE * square)
        hidden_back = back[inner, :] * slope
        hidden_sum[...] += jnp.sum(hidden_back, axis=0, keepdims=True)
        hidden_half[inner, :] = hidden_back.astype(HALF)
    part_out[...] = dot(hidden_half[...], up[...], 1, 1).astype(HALF)
    up_grad = dot(feed, hidden_half[...], 0, 0).astype(HALF)
    down_grad = dot(upstream_half, active[...], 0, 0).astype(HALF)
    if spread_pack:
        count, cols = packs[0].shape[0], packs[0].shape[2]
        for side in range(count):
            packs[0][side] = up_grad[:, side * cols:(side + 1) * cols]
        packs[1][...] = down_grad
    else:
        packs[0][:, :hidden] = up_grad
        packs[0][:, hidden:] = down_grad


def attend_back_kernel(spread_pack, place, upstream, middle, mine, other, gain, attended, query, key, value,
                       log_total, visible, wide, weights, *refs):
    if spread_pack:
        pack, middle_out, wide_mine, wide_other, sums_out, heads_out, wide_query, wide_both, near = refs
    else:
        _, pack, middle_out, wide_mine, wide_other, sums_out, heads_out, wide_query, wide_both, near = refs
    tokens, width = upstream.shape
    rows, block, keys = visible.shape
    cols = query.shape[1]
    scale = HEAD ** (-0.5)
    feed_back = mine[...].astype(FULL) + other[...].astype(FULL)
    normed, spread = norm_stats(middle[...])
    middle_back = upstream[...] + norm_backward(feed_back, normed, spread, gain[...])
    middle_out[...] = middle_back
    sums_out[...] = jnp.concatenate(
        [jnp.sum(feed_back * normed, axis=0, keepdims=True), jnp.sum(feed_back, axis=0, keepdims=True),
         jnp.sum(middle_back, axis=0, keepdims=True)], axis=0)
    middle_half = middle_back.astype(HALF)
    mix_grad = dot(middle_half, attended[...], 0, 0).astype(HALF)
    near[...] = dot(middle_half, weights[:, 3 * cols:4 * cols], 1, 0).astype(HALF)
    pairs = cols // 128
    low_lane = lax.broadcasted_iota(jnp.int32, (block, 128), 1) < HEAD
    low_key = lax.broadcasted_iota(jnp.int32, (keys, 128), 1) < HEAD
    lane = lax.broadcasted_iota(jnp.int32, (block, 128), 1)
    heads_out[...] = jnp.zeros(heads_out.shape, FULL)

    def one(step, carry):
        row, pair = step // pairs, step % pairs
        at_rows = pl.ds(pl.multiple_of(row * block, block), block)
        at_cols = pl.ds(pl.multiple_of(pair * 128, 128), 128)
        at_values = pl.ds(pl.multiple_of(cols + pair * 128, 128), 128)
        query_two = query[at_rows, at_cols]
        key_two, value_two = key[row, :, at_cols], value[row, :, at_cols]
        back_two = near[at_rows, at_cols]
        product = back_two.astype(FULL) * attended[at_rows, at_cols].astype(FULL)
        shown = visible[row] > 0
        logs = log_total[at_rows, :]
        query_parts, key_parts, value_parts = [], [], []
        for which in range(2):
            lanes = low_lane if which == 0 else ~low_lane
            picked = jnp.where(lanes, query_two, jnp.zeros_like(query_two))
            picked_back = jnp.where(lanes, back_two, jnp.zeros_like(back_two))
            delta = jnp.sum(jnp.where(lanes, product, 0.0), axis=-1, keepdims=True)
            own_log = jnp.sum(jnp.where(lane == 2 * pair + which, logs, 0.0), axis=-1, keepdims=True)
            scores = jnp.where(shown, dot(picked, key_two, 1, 1) * scale, MASKED)
            soft = jnp.exp(scores - own_log)
            score_back = (soft * (dot(picked_back, value_two, 1, 1) - delta) * scale).astype(HALF)
            query_parts.append(dot(score_back, key_two, 1, 0))
            key_parts.append(dot(score_back, query_two, 0, 0))
            value_parts.append(dot(soft.astype(HALF), back_two, 0, 0))
        query_back = jnp.where(low_lane, query_parts[0], query_parts[1])
        key_back = jnp.where(low_key, key_parts[0], key_parts[1])
        value_back = jnp.where(low_key, value_parts[0], value_parts[1])
        heads_out[0:1, at_cols] += jnp.sum(query_back, axis=0, keepdims=True)
        heads_out[1:2, at_cols] += jnp.sum(value_back, axis=0, keepdims=True)
        wide_query[at_rows, at_cols] = query_back.astype(HALF)
        wide_both[row, :, at_cols] = key_back.astype(HALF)
        wide_both[row, :, at_values] = value_back.astype(HALF)
        return carry

    lax.fori_loop(0, rows * pairs, one, 0)
    both = wide_both[...].reshape(rows * keys, 2 * cols)
    own = wide[:, keys - block:, :].reshape(tokens, width)
    query_grad = dot(own, wide_query[...], 0, 0).astype(HALF)
    both_grad = dot(wide[...].reshape(rows * keys, width), both, 0, 0).astype(HALF)
    grads = (query_grad, both_grad[:, :cols], both_grad[:, cols:], mix_grad)
    for index, grad in enumerate(grads):
        if spread_pack:
            pack[index] = grad
        else:
            pack[:, index * cols:(index + 1) * cols] = grad
    wide_back = dot(both, weights[:, cols:3 * cols], 1, 1).reshape(rows, keys, width)
    own_back = dot(wide_query[...], weights[:, :cols], 1, 1).reshape(rows, block, width)
    half = width // 2
    low = place[0] == 0

    def put(first, count, values):
        wide_mine[:, first:first + count, :] = jnp.where(low, values[..., :half], values[..., half:])
        wide_other[:, first:first + count, :] = jnp.where(low, values[..., half:], values[..., :half]).astype(HALF)

    put(0, keys - block, wide_back[:, :keys - block])
    put(keys - block, block, wide_back[:, keys - block:] + own_back)


def per_device(
    inputs,
    segment_ids,
    projection,
    head_bias,
    mixing,
    expansion,
    hidden_bias,
    contraction,
    norm_gains,
    offsets,
    cotangent,
):
    layers = projection.shape[0]
    rows, block, width = inputs.shape
    shards = lax.axis_size("shard")
    contexts = lax.axis_size("context")
    own = projection.shape[2]
    heads = head_bias.shape[2]
    head_cols = projection.shape[3]
    hidden = expansion.shape[2]
    tokens = rows * block
    head_scale = HEAD ** (-0.5)
    back_steps = 2

    def attend_block(layer):
        return [projection[layer, 0], projection[layer, 1], projection[layer, 2], mixing[layer].T]

    others = [expansion[0], contraction[0].T]
    for layer in range(1, layers):
        others += attend_block(layer) + [expansion[layer], contraction[layer].T]
    gathered = lax.all_gather(jnp.concatenate(others, axis=1), "shard", axis=0, tiled=True)
    small_parts = [norm_gains, offsets, head_bias, hidden_bias]
    small_sizes = [part.size for part in small_parts]
    small_total = sum(small_sizes)
    small_padded = -(-small_total // 1024) * 1024
    small_rows = small_padded // 128
    small = jnp.concatenate([part.reshape(-1) for part in small_parts] + [jnp.zeros((own * 128 - small_total,), HALF)])
    turn = lax.axis_index("context")
    quarter_cols = 4 * head_cols // contexts
    first = jnp.concatenate([
        lax.dynamic_slice_in_dim(jnp.concatenate(attend_block(0), axis=1), turn * quarter_cols, quarter_cols, 1),
        small.reshape(own, 128)], axis=1)
    first = lax.all_to_all(jnp.broadcast_to(first[None], (shards,) + first.shape), "shard", 0, 0)
    small = first[:, :small_rows, first.shape[2] - 128:].reshape(shards, small_padded)
    attend_pieces = context_spread(first.reshape(shards * own, -1)[:, :quarter_cols])

    def widen(index):
        start = sum(small_sizes[:index])
        shape = small_parts[index].shape
        piece = small[:, start:start + small_sizes[index]].astype(FULL).reshape((shards,) + shape)
        piece = jnp.moveaxis(piece, 0, -2)
        return piece.reshape(shape[:-1] + (shards * shape[-1],))

    gains_all, offsets_all = widen(0), widen(1)
    head_all = widen(2).reshape(layers, 2, head_cols)
    hidden_all = widen(3).reshape(layers, hidden)

    seg_before = [from_before(segment_ids, steps) for steps in range(back_steps, 0, -1)]
    segments_all = jnp.concatenate(seg_before + [segment_ids], axis=1)
    query_pos = jnp.arange(block, dtype=jnp.int32) + back_steps * block
    key_pos = jnp.arange((back_steps + 1) * block, dtype=jnp.int32)
    first_key = (back_steps - lax.axis_index("context")) * block
    visible = (segments_all[:, None, :] == segment_ids[:, :, None]) & (
        key_pos[None, None, :] <= query_pos[None, :, None]
    ) & (key_pos >= first_key)[None, None, :]

    mask = visible.astype(FULL)
    keys = (back_steps + 1) * block
    half = width // 2
    place = jnp.stack([lax.axis_index("tensor"), turn]).astype(jnp.int32)
    side_cols = 4 * head_cols

    def row_of(table, layer, index):
        return table[layer, index].reshape(1, -1)

    def gathered_spec(layer, member):
        at = member if layer == 0 else 2 + 3 * (layer - 1) + member
        return weight_spec(width, side_cols, at)

    vmem = whole()
    stream = inputs.reshape(tokens, width)
    kept = []
    parts = ()
    middle = None
    for layer in range(layers):
        outs = [shape((tokens, width), HALF), shape((tokens, half), HALF)]
        gain_row, offset_row = row_of(gains_all, layer, 0), row_of(offsets_all, layer, 0)
        if layer == 0:
            attend_input, sent = call(
                functools.partial(enter_kernel, False), outs, (place, stream, gain_row, offset_row),
                in_specs=[scalars()] + [vmem] * 3, out_specs=[vmem] * 2, name="enter_first")
        else:
            stream, attend_input, sent = call(
                functools.partial(enter_kernel, True), [shape((tokens, width), FULL)] + outs,
                (place, middle) + parts + (row_of(offsets_all, layer - 1, 3), gain_row, offset_row),
                in_specs=[scalars()] + [vmem] * 6, out_specs=[vmem] * 3, name="enter")
        sent = sent.reshape(rows, block, half)
        far, near = from_before(sent, 2), from_before(sent, 1)
        far_other, near_other = pair_other(far), pair_other(near)
        attend_outs = [
            shape((tokens, head_cols), HALF), shape((rows, keys, head_cols), HALF), shape((rows, keys, head_cols), HALF),
            shape((tokens, head_cols), HALF), shape((tokens, 128), FULL), shape((rows, keys, width), HALF),
            shape((tokens, width), FULL)]
        attend_args = (attend_input, far, near, far_other, near_other)
        if layer == 0:
            query, key, value, attended, log_total, wide, part, weights = call(
                functools.partial(attend_first_kernel, contexts), attend_outs + [shape((width, side_cols), HALF)],
                (place,) + tuple(attend_pieces) + attend_args + (head_all[layer], mask),
                in_specs=[scalars()] + [vmem] * (contexts + 7), out_specs=[vmem] * 8, name="attend_first")
            held = (weights, gathered, gathered)
            specs = (vmem, gathered_spec(0, 0), gathered_spec(0, 1))
        else:
            held = (gathered,) * 3
            specs = tuple(gathered_spec(layer, member) for member in range(3))
            query, key, value, attended, log_total, wide, part = call(
                attend_kernel, attend_outs, (place,) + attend_args + (held[0], head_all[layer], mask),
                in_specs=[scalars()] + [vmem] * 5 + [specs[0]] + [vmem] * 2, out_specs=[vmem] * 7, name="attend")
        before = stream
        middle, preact, part = call(
            feed_kernel,
            [shape((tokens, width), FULL), shape((tokens, hidden), FULL), shape((tokens, width), FULL)],
            (stream, part, pair_other(part), row_of(offsets_all, layer, 2), row_of(gains_all, layer, 1),
             row_of(offsets_all, layer, 1), held[1], hidden_all[layer].reshape(1, -1), held[2]),
            scratch=[pltpu.VMEM((tokens, hidden), HALF)],
            in_specs=[vmem] * 6 + [specs[1], vmem, specs[2]], out_specs=[vmem] * 3, name="feed")
        parts = (part, pair_other(part))
        kept.append((before, query, key, value, attended, log_total, wide, middle, preact, held, specs))
    stream = middle + (parts[0] + parts[1]) + offsets_all[layers - 1, 3]

    vectors = [None] * layers
    leave = None
    shares = [None] * layers
    unread = pl.BlockSpec(memory_space=pl.ANY)
    for layer in reversed(range(layers)):
        before, query, key, value, attended, log_total, wide, middle, preact, held, specs = kept[layer]
        last = layer == layers - 1
        if layer == 0:
            feed_packs = [shape((contexts, width, hidden // contexts), HALF), shape((width, hidden), HALF)]
            feed_pack_specs = [vmem] * 2
            attend_pack = shape((contexts, width, side_cols // contexts), HALF)
            attend_pack_spec = vmem
        else:
            attend_pack = shape((width, 2 * hidden + side_cols), HALF)
            feed_packs = [attend_pack]
            feed_pack_specs = [pl.BlockSpec((width, 2 * hidden), lambda *_: (0, 0))]
            attend_pack_spec = pl.BlockSpec((width, side_cols), lambda *_: (0, 2 * hidden // side_cols))
        shared = (middle, preact, row_of(gains_all, layer, 1), row_of(offsets_all, layer, 1), held[1], held[2])
        shared_specs = [vmem] * 4 + [specs[1], specs[2]]
        outs = feed_packs + [shape((1, hidden), FULL), shape((1, width), FULL), shape((tokens, width), HALF)]
        outs_specs = feed_pack_specs + [vmem] * 3
        scratch = [pltpu.VMEM((tokens, hidden), HALF)] * 2
        if last:
            upstream = cotangent.reshape(tokens, width)
            packed, hidden_sum, down_sum, part = call(
                functools.partial(feed_back_kernel, False, layer == 0), outs, (upstream,) + shared, scratch=scratch,
                in_specs=[vmem] + shared_specs, out_specs=outs_specs, name="feed_back_last")
        else:
            upstream, leave_sums, up_packed, packed, hidden_sum, down_sum, part = call(
                functools.partial(feed_back_kernel, True, layer == 0),
                [shape((tokens, width), FULL), shape((2, width), FULL)] + outs, leave + shared, scratch=scratch,
                in_specs=[scalars()] + [vmem] * 5 + shared_specs, out_specs=[vmem] * 2 + outs_specs, name="feed_back")
            vectors[layer + 1] = (leave_sums,) + vectors[layer + 1]
        if layer == 0:
            down_moved = lax.all_to_all(packed.reshape(shards, own, hidden), "shard", 0, 0)
        operands = (place, upstream, middle, part, pair_other(part), row_of(gains_all, layer, 1), attended,
                    query, key, value, log_total, mask, wide, held[0])
        attend_packed, middle_back, wide_mine, wide_other, sums, head_sums = call(
            functools.partial(attend_back_kernel, layer == 0),
            [attend_pack, shape((tokens, width), FULL), shape((rows, keys, half), FULL), shape((rows, keys, half), HALF),
             shape((3, width), FULL), shape((2, head_cols), FULL)],
            operands + (() if layer == 0 else (packed,)),
            scratch=[pltpu.VMEM((tokens, head_cols), HALF), pltpu.VMEM((rows, keys, 2 * head_cols), HALF),
                     pltpu.VMEM((tokens, head_cols), HALF)],
            aliases=None if layer == 0 else {len(operands): 0},
            in_specs=[scalars()] + [vmem] * 12 + [specs[0]] + ([] if layer == 0 else [unread]),
            out_specs=[attend_pack_spec] + [vmem] * 5, name="attend_back")
        if layer == 0:
            first_quarter = context_share(jnp.concatenate([up_packed, attend_packed], axis=2)).astype(HALF)
        else:
            shares[layer] = lax.psum_scatter(attend_packed, "shard", scatter_dimension=0, tiled=True)
        wide_sum = wide_mine + pair_other(wide_other).astype(FULL)
        half_back = wide_sum[:, back_steps * block:]
        for steps in range(1, back_steps + 1):
            start = (back_steps - steps) * block
            half_back = half_back + from_after(wide_sum[:, start:start + block].astype(HALF), steps).astype(FULL)
        half_back = half_back.reshape(tokens, half)
        leave = (place, middle_back, before, half_back, pair_other(half_back), row_of(gains_all, layer, 0))
        vectors[layer] = (sums, down_sum, head_sums, hidden_sum)
    upstream, leave_sums = call(
        leave_kernel, [shape((tokens, width), FULL), shape((2, width), FULL)], leave,
        in_specs=[scalars()] + [vmem] * 5, out_specs=[vmem] * 2, name="leave")
    vectors[0] = (leave_sums,) + vectors[0]

    def spread_out(values, shape):
        lead = shape[:-1]
        values = values.reshape(lead + (shards, shape[-1]))
        return jnp.moveaxis(values, -2, 0).reshape(shards, -1)

    gain_sums = jnp.stack([jnp.stack([entry[0][0], entry[1][0]]) for entry in vectors])
    offset_sums = jnp.stack([jnp.concatenate([entry[0][1:2], entry[1][1:], entry[2]]) for entry in vectors])
    head_sums = jnp.stack([entry[3] for entry in vectors])
    hidden_sums = jnp.stack([entry[4] for entry in vectors])
    vector_pack = jnp.concatenate(
        [spread_out(values, part.shape) for values, part in zip((gain_sums, offset_sums, head_sums, hidden_sums), small_parts)]
        + [jnp.zeros((shards, small_padded - small_total), FULL)], axis=1)
    vector_pack = context_sum(vector_pack.reshape(shards * small_rows, 128)).astype(HALF)
    vector_pack = jnp.pad(vector_pack.reshape(shards, small_rows, 128), ((0, 0), (0, own - small_rows), (0, 0)))
    final = jnp.concatenate([first_quarter.reshape(shards, own, -1), vector_pack], axis=2)
    final, down_moved, shares[1] = lax.optimization_barrier((final, down_moved, shares[1]))
    final = jnp.sum(lax.all_to_all(final, "shard", 0, 0).astype(FULL), axis=0)
    first_cols = final.shape[1] - 128
    up_cols = hidden // contexts
    vector_own = final[:small_rows, first_cols:].reshape(-1)
    vector_out = []
    for index, part in enumerate(small_parts):
        start = sum(small_sizes[:index])
        vector_out.append(vector_own[start:start + small_sizes[index]].reshape(part.shape))
    gains_grad, offsets_grad, head_grad, hidden_grad = vector_out

    down_own = jnp.sum(down_moved.astype(FULL), axis=0).astype(HALF)
    pieces = [down_own.reshape(own, contexts, -1)] + [shares[layer].reshape(own, contexts, -1) for layer in range(1, layers)]
    later = context_share(jnp.concatenate(pieces, axis=2).transpose(1, 0, 2)).astype(HALF)
    sizes = [up_cols, first_cols - up_cols] + [piece.shape[2] for piece in pieces]
    quarters = jnp.concatenate([final[:, :first_cols].astype(HALF), later], axis=1)
    quarters = lax.all_gather(quarters, "context", axis=0, tiled=False).astype(FULL)
    joined, start = [], 0
    for size in sizes:
        joined.append(jnp.moveaxis(quarters[:, :, start:start + size], 0, 1).reshape(own, -1))
        start += size
    up_own = [joined[0]] + [share[:, :hidden] for share in joined[3:]]
    down_own = [joined[2]] + [share[:, hidden:2 * hidden] for share in joined[3:]]
    attend_own = [joined[1]] + [share[:, 2 * hidden:] for share in joined[3:]]
    projection_grad = jnp.stack(
        [jnp.stack([share[:, k * head_cols:(k + 1) * head_cols] for k in range(3)]) for share in attend_own])
    mixing_grad = jnp.stack([share[:, 3 * head_cols:].T for share in attend_own])
    expansion_grad = jnp.stack(up_own)
    contraction_grad = jnp.stack([share.T for share in down_own])
    return (
        stream.reshape(rows, block, width),
        upstream.reshape(rows, block, width),
        projection_grad,
        head_grad,
        mixing_grad,
        expansion_grad,
        hidden_grad,
        contraction_grad,
        gains_grad,
        offsets_grad,
    )


def solution(mesh):
    in_specs = (
        P("shard", "context", None),
        P("shard", "context"),
        P(None, None, "shard", "tensor"),
        P(None, None, "tensor", "shard"),
        P(None, "tensor", "shard"),
        P(None, "shard", "tensor"),
        P(None, "tensor", "shard"),
        P(None, "tensor", "shard"),
        P(None, None, "shard"),
        P(None, None, "shard"),
        P("shard", "context", None),
    )
    out_specs = (
        P("shard", "context", None),
        P("shard", "context", None),
        P(None, None, "shard", "tensor"),
        P(None, None, "tensor", "shard"),
        P(None, "tensor", "shard"),
        P(None, "shard", "tensor"),
        P(None, "tensor", "shard"),
        P(None, "tensor", "shard"),
        P(None, None, "shard"),
        P(None, None, "shard"),
    )
    return jax.shard_map(
        per_device, mesh=mesh, in_specs=in_specs, out_specs=out_specs, check_vma=False
    )
```

```python
import functools

import jax
import jax.numpy as jnp
from jax import lax
from jax.experimental import pallas as pl
from jax.experimental.pallas import tpu as pltpu
from jax.sharding import PartitionSpec as P

HEAD = 64

EPS = 1e-05
GELU_COEF = 0.7978845608028654
GELU_CUBE = 0.044715
MASKED = -1e30
HALF = jnp.bfloat16
FULL = jnp.float32


def gelu_value(preact):
    inner_arg = GELU_COEF * (preact + GELU_CUBE * preact * preact * preact)
    return 0.5 * preact * (1.0 + jnp.tanh(inner_arg))


def norm_backward(upstream, normed, spread, gain_row):
    scaled = upstream * gain_row
    first_mean = jnp.mean(scaled, axis=-1, keepdims=True)
    second_mean = jnp.mean(scaled * normed, axis=-1, keepdims=True)
    return spread * (scaled - first_mean - normed * second_mean)


def dot(left, right, left_dim, right_dim):
    return lax.dot_general(
        left, right, (((left_dim,), (right_dim,)), ((), ())), preferred_element_type=FULL
    )


def from_before(block, steps):
    size = lax.axis_size("context")
    return lax.ppermute(block, "context", [(i, i + steps) for i in range(size - steps)])


def from_after(block, steps):
    size = lax.axis_size("context")
    return lax.ppermute(block, "context", [(i + steps, i) for i in range(size - steps)])


def context_share(parts):
    size = lax.axis_size("context")
    place = lax.axis_index("context")
    total = lax.dynamic_index_in_dim(parts, place, 0, keepdims=False).astype(FULL)
    for steps in range(1, size):
        piece = lax.dynamic_index_in_dim(parts, (place + steps) % size, 0, keepdims=False)
        total = total + lax.ppermute(piece, "context", [(i, (i + steps) % size) for i in range(size)]).astype(FULL)
    return total


def context_spread(part):
    size = lax.axis_size("context")
    return [part] + [
        lax.ppermute(part, "context", [(i, (i + steps) % size) for i in range(size)]) for steps in range(1, size)]


def context_sum(part):
    size = lax.axis_size("context")
    total = part.astype(FULL)
    for steps in range(1, size):
        moved = lax.ppermute(part, "context", [(i, (i + steps) % size) for i in range(size)])
        total = total + moved.astype(FULL)
    return total


def pair_other(part):
    size = lax.axis_size("tensor")
    return lax.ppermute(part, "tensor", [(i, (i + 1) % size) for i in range(size)])


def call(body, outs, ins, scratch=(), aliases=None, in_specs=None, out_specs=None, name=None):
    return pl.pallas_call(
        body,
        out_shape=outs,
        grid=(1,),
        in_specs=in_specs,
        out_specs=out_specs,
        scratch_shapes=list(scratch),
        input_output_aliases=aliases or {},
        compiler_params=pltpu.CompilerParams(vmem_limit_bytes=58 * 2**20),
        name=name,
    )(*ins)


def whole():
    return pl.BlockSpec(memory_space=pltpu.VMEM)


def scalars():
    return pl.BlockSpec(memory_space=pltpu.SMEM)


def shape(dims, dtype):
    return jax.ShapeDtypeStruct(dims, dtype)


def weight_spec(depth, cols, index):
    return pl.BlockSpec((depth, cols), lambda *_: (0, index))


def norm_stats(stream):
    center = stream - jnp.mean(stream, axis=-1, keepdims=True)
    spread = lax.rsqrt(jnp.mean(center * center, axis=-1, keepdims=True) + EPS)
    return center * spread, spread


def enter_kernel(has_parts, place, *refs):
    if has_parts:
        middle, mine, other, offset_last, gain, offset, stream_out, attend_out, half_out = refs
        stream = middle[...] + (mine[...] + other[...]) + offset_last[...]
        stream_out[...] = stream
    else:
        stream_in, gain, offset, attend_out, half_out = refs
        stream = stream_in[...]
    normed, _ = norm_stats(stream)
    attend = (normed * gain[...] + offset[...]).astype(HALF)
    attend_out[...] = attend
    cols = half_out.shape[1]
    half_out[...] = jnp.where(place[0] == 0, attend[:, :cols], attend[:, cols:])


def assemble(place, pieces, out):
    count, cols = len(pieces), pieces[0].shape[1]
    for index, piece in enumerate(pieces):
        source = lax.rem(place[1] + count - index, count)
        out[:, pl.ds(pl.multiple_of(source * cols, cols), cols)] = piece[...]


def attend_first_kernel(count, place, *refs):
    pieces, rest, weights = refs[:count], refs[count:-1], refs[-1]
    assemble(place, pieces, weights)
    attend_kernel(place, *rest[:5], weights, *rest[5:])


def attend_kernel(place, own, far_mine, near_mine, far_other, near_other, weights, bias, visible,
                  query_out, key_out, value_out, attended_out, log_out, wide_out, part_out):
    tokens, width = own.shape
    rows, block, keys = visible.shape
    cols = query_out.shape[1]
    half = far_mine.shape[2]
    wide_out[:, keys - block:, :] = own[...].reshape(rows, block, width)

    def put(first, mine, other):
        mine, other = mine[...], other[...]
        low = place[0] == 0
        wide_out[:, first:first + block, :half] = jnp.where(low, mine, other)
        wide_out[:, first:first + block, half:] = jnp.where(low, other, mine)

    put(0, far_mine, far_other)
    put(block, near_mine, near_other)
    query_out[...] = (dot(own[...], weights[:, :cols], 1, 0) + bias[0:1, :]).astype(HALF)
    wide = wide_out[...].reshape(rows * keys, width)
    key_out[...] = dot(wide, weights[:, cols:2 * cols], 1, 0).astype(HALF).reshape(rows, keys, cols)
    value_out[...] = (dot(wide, weights[:, 2 * cols:3 * cols], 1, 0) + bias[1:2, :]).astype(HALF).reshape(rows, keys, cols)
    scale = HEAD ** (-0.5)
    pairs = cols // 128
    low_lane = lax.broadcasted_iota(jnp.int32, (block, 128), 1) < HEAD
    lane = lax.broadcasted_iota(jnp.int32, (block, 128), 1)
    log_out[...] = jnp.zeros(log_out.shape, FULL)

    def one(step, carry):
        row, pair = step // pairs, step % pairs
        at_rows = pl.ds(pl.multiple_of(row * block, block), block)
        at_cols = pl.ds(pl.multiple_of(pair * 128, 128), 128)
        query = query_out[at_rows, at_cols]
        key = key_out[row, :, at_cols]
        value = value_out[row, :, at_cols]
        shown = visible[row] > 0
        outs = []
        logs = log_out[at_rows, :]
        for which in range(2):
            picked = jnp.where(low_lane if which == 0 else ~low_lane, query, jnp.zeros_like(query))
            scores = jnp.where(shown, dot(picked, key, 1, 1) * scale, MASKED)
            top = jnp.max(scores, axis=-1, keepdims=True)
            grown = jnp.exp(scores - top)
            total = jnp.sum(grown, axis=-1, keepdims=True)
            logs = jnp.where(lane == 2 * pair + which, top + jnp.log(total), logs)
            soft = (grown * (1.0 / total)).astype(HALF)
            outs.append(dot(soft, value, 1, 0))
        log_out[at_rows, :] = logs
        attended_out[at_rows, at_cols] = jnp.where(low_lane, outs[0], outs[1]).astype(HALF)
        return carry

    lax.fori_loop(0, rows * pairs, one, 0)
    part_out[...] = dot(attended_out[...], weights[:, 3 * cols:4 * cols], 1, 1)


def feed_kernel(stream, mine, other, offset_mid, gain, offset, up, hidden_bias, down,
                middle_out, preact_out, part_out, active):
    middle = stream[...] + (mine[...] + other[...]) + offset_mid[...]
    middle_out[...] = middle
    normed, _ = norm_stats(middle)
    feed = (normed * gain[...] + offset[...]).astype(HALF)
    preact_out[...] = dot(feed, up[...], 1, 0) + hidden_bias[...]
    step_rows = 32

    def one(step, carry):
        at = pl.ds(pl.multiple_of(step * step_rows, step_rows), step_rows)
        active[at, :] = gelu_value(preact_out[at, :]).astype(HALF)
        return carry

    lax.fori_loop(0, preact_out.shape[0] // step_rows, one, 0)
    part_out[...] = dot(active[...], down[...], 1, 1)


def leave_norm(place, middle_back, stream, mine, other, gain):
    low = place[0] == 0
    mine, other = mine[...], other[...]
    back = jnp.concatenate([jnp.where(low, mine, other), jnp.where(low, other, mine)], axis=1)
    normed, spread = norm_stats(stream[...])
    upstream = middle_back[...] + norm_backward(back, normed, spread, gain[...])
    sums = jnp.concatenate(
        [jnp.sum(back * normed, axis=0, keepdims=True), jnp.sum(back, axis=0, keepdims=True)], axis=0)
    return upstream, sums


def leave_kernel(place, middle_back, stream, mine, other, gain, upstream_out, sums_out):
    upstream, sums = leave_norm(place, middle_back, stream, mine, other, gain)
    upstream_out[...] = upstream
    sums_out[...] = sums


def feed_back_kernel(has_leave, *refs):
    if has_leave:
        place, middle_back, stream, mine, other, gain_one = refs[:6]
        middle, preact, gain, offset, up, down = refs[6:12]
        upstream_out, sums_out = refs[12:14]
        rest = refs[14:]
        upstream, sums = leave_norm(place, middle_back, stream, mine, other, gain_one)
        upstream_out[...] = upstream
        sums_out[...] = sums
    else:
        upstream_in, middle, preact, gain, offset, up, down = refs[:7]
        rest = refs[7:]
        upstream = upstream_in[...]
    packs, (hidden_sum, down_sum, part_out, active, hidden_half) = rest[:-5], rest[-5:]
    hidden = up.shape[1]
    step_rows = 32
    upstream_half = upstream.astype(HALF)
    down_sum[...] = jnp.sum(upstream, axis=0, keepdims=True)
    normed, _ = norm_stats(middle[...])
    feed = (normed * gain[...] + offset[...]).astype(HALF)
    back = dot(upstream_half, down[...], 1, 0)
    hidden_sum[...] = jnp.zeros(hidden_sum.shape, FULL)
    for first in range(0, upstream.shape[0], step_rows):
        inner = slice(first, first + step_rows)
        pre = preact[inner, :]
        square = pre * pre
        tanh_value = jnp.tanh(GELU_COEF * (pre + GELU_CUBE * square * pre))
        active[inner, :] = (0.5 * pre * (1.0 + tanh_value)).astype(HALF)
        slope = 0.5 * (1.0 + tanh_value) + 0.5 * pre * (1.0 - tanh_value * tanh_value) * GELU_COEF * (
            1.0 + 3.0 * GELU_CUBE * square)
        hidden_back = back[inner, :] * slope
        hidden_sum[...] += jnp.sum(hidden_back, axis=0, keepdims=True)
        hidden_half[inner, :] = hidden_back.astype(HALF)
    part_out[...] = dot(hidden_half[...], up[...], 1, 1).astype(HALF)
    up_grad = dot(feed, hidden_half[...], 0, 0).astype(HALF)
    down_grad = dot(upstream_half, active[...], 0, 0).astype(HALF)
    packs[0][:, :hidden] = up_grad
    packs[0][:, hidden:] = down_grad


def attend_back_kernel(spread_pack, place, upstream, middle, mine, other, gain, attended, query, key, value,
                       log_total, visible, wide, weights, *refs):
    if spread_pack:
        pack, middle_out, wide_mine, wide_other, sums_out, heads_out, wide_query, wide_both, near = refs
    else:
        _, pack, middle_out, wide_mine, wide_other, sums_out, heads_out, wide_query, wide_both, near = refs
    tokens, width = upstream.shape
    rows, block, keys = visible.shape
    cols = query.shape[1]
    scale = HEAD ** (-0.5)
    feed_back = mine[...].astype(FULL) + other[...].astype(FULL)
    normed, spread = norm_stats(middle[...])
    middle_back = upstream[...] + norm_backward(feed_back, normed, spread, gain[...])
    middle_out[...] = middle_back
    sums_out[...] = jnp.concatenate(
        [jnp.sum(feed_back * normed, axis=0, keepdims=True), jnp.sum(feed_back, axis=0, keepdims=True),
         jnp.sum(middle_back, axis=0, keepdims=True)], axis=0)
    middle_half = middle_back.astype(HALF)
    mix_grad = dot(middle_half, attended[...], 0, 0).astype(HALF)
    near[...] = dot(middle_half, weights[:, 3 * cols:4 * cols], 1, 0).astype(HALF)
    pairs = cols // 128
    low_lane = lax.broadcasted_iota(jnp.int32, (block, 128), 1) < HEAD
    low_key = lax.broadcasted_iota(jnp.int32, (keys, 128), 1) < HEAD
    lane = lax.broadcasted_iota(jnp.int32, (block, 128), 1)
    heads_out[...] = jnp.zeros(heads_out.shape, FULL)

    def one(step, carry):
        row, pair = step // pairs, step % pairs
        at_rows = pl.ds(pl.multiple_of(row * block, block), block)
        at_cols = pl.ds(pl.multiple_of(pair * 128, 128), 128)
        at_values = pl.ds(pl.multiple_of(cols + pair * 128, 128), 128)
        query_two = query[at_rows, at_cols]
        key_two, value_two = key[row, :, at_cols], value[row, :, at_cols]
        back_two = near[at_rows, at_cols]
        product = back_two.astype(FULL) * attended[at_rows, at_cols].astype(FULL)
        shown = visible[row] > 0
        logs = log_total[at_rows, :]
        query_parts, key_parts, value_parts = [], [], []
        for which in range(2):
            lanes = low_lane if which == 0 else ~low_lane
            picked = jnp.where(lanes, query_two, jnp.zeros_like(query_two))
            picked_back = jnp.where(lanes, back_two, jnp.zeros_like(back_two))
            delta = jnp.sum(jnp.where(lanes, product, 0.0), axis=-1, keepdims=True)
            own_log = jnp.sum(jnp.where(lane == 2 * pair + which, logs, 0.0), axis=-1, keepdims=True)
            scores = jnp.where(shown, dot(picked, key_two, 1, 1) * scale, MASKED)
            soft = jnp.exp(scores - own_log)
            score_back = (soft * (dot(picked_back, value_two, 1, 1) - delta) * scale).astype(HALF)
            query_parts.append(dot(score_back, key_two, 1, 0))
            key_parts.append(dot(score_back, query_two, 0, 0))
            value_parts.append(dot(soft.astype(HALF), back_two, 0, 0))
        query_back = jnp.where(low_lane, query_parts[0], query_parts[1])
        key_back = jnp.where(low_key, key_parts[0], key_parts[1])
        value_back = jnp.where(low_key, value_parts[0], value_parts[1])
        heads_out[0:1, at_cols] += jnp.sum(query_back, axis=0, keepdims=True)
        heads_out[1:2, at_cols] += jnp.sum(value_back, axis=0, keepdims=True)
        wide_query[at_rows, at_cols] = query_back.astype(HALF)
        wide_both[row, :, at_cols] = key_back.astype(HALF)
        wide_both[row, :, at_values] = value_back.astype(HALF)
        return carry

    lax.fori_loop(0, rows * pairs, one, 0)
    both = wide_both[...].reshape(rows * keys, 2 * cols)
    own = wide[:, keys - block:, :].reshape(tokens, width)
    query_grad = dot(own, wide_query[...], 0, 0).astype(HALF)
    both_grad = dot(wide[...].reshape(rows * keys, width), both, 0, 0).astype(HALF)
    grads = (query_grad, both_grad[:, :cols], both_grad[:, cols:], mix_grad)
    for index, grad in enumerate(grads):
        if spread_pack:
            pack[index] = grad
        else:
            pack[:, index * cols:(index + 1) * cols] = grad
    wide_back = dot(both, weights[:, cols:3 * cols], 1, 1).reshape(rows, keys, width)
    own_back = dot(wide_query[...], weights[:, :cols], 1, 1).reshape(rows, block, width)
    half = width // 2
    low = place[0] == 0

    def put(first, count, values):
        wide_mine[:, first:first + count, :] = jnp.where(low, values[..., :half], values[..., half:])
        wide_other[:, first:first + count, :] = jnp.where(low, values[..., half:], values[..., :half]).astype(HALF)

    put(0, keys - block, wide_back[:, :keys - block])
    put(keys - block, block, wide_back[:, keys - block:] + own_back)


def per_device(
    inputs,
    segment_ids,
    projection,
    head_bias,
    mixing,
    expansion,
    hidden_bias,
    contraction,
    norm_gains,
    offsets,
    cotangent,
):
    layers = projection.shape[0]
    rows, block, width = inputs.shape
    shards = lax.axis_size("shard")
    contexts = lax.axis_size("context")
    own = projection.shape[2]
    heads = head_bias.shape[2]
    head_cols = projection.shape[3]
    hidden = expansion.shape[2]
    tokens = rows * block
    head_scale = HEAD ** (-0.5)
    back_steps = 2

    def attend_block(layer):
        return [projection[layer, 0], projection[layer, 1], projection[layer, 2], mixing[layer].T]

    others = [expansion[0], contraction[0].T]
    for layer in range(1, layers):
        others += attend_block(layer) + [expansion[layer], contraction[layer].T]
    gathered = lax.all_gather(jnp.concatenate(others, axis=1), "shard", axis=0, tiled=True)
    small_parts = [norm_gains, offsets, head_bias, hidden_bias]
    small_sizes = [part.size for part in small_parts]
    small_total = sum(small_sizes)
    small_padded = -(-small_total // 1024) * 1024
    small_rows = small_padded // 128
    small = jnp.concatenate([part.reshape(-1) for part in small_parts] + [jnp.zeros((own * 128 - small_total,), HALF)])
    turn = lax.axis_index("context")
    quarter_cols = 4 * head_cols // contexts
    first = jnp.concatenate([
        lax.dynamic_slice_in_dim(jnp.concatenate(attend_block(0), axis=1), turn * quarter_cols, quarter_cols, 1),
        small.reshape(own, 128)], axis=1)
    first = lax.all_to_all(jnp.broadcast_to(first[None], (shards,) + first.shape), "shard", 0, 0)
    small = first[:, :small_rows, first.shape[2] - 128:].reshape(shards, small_padded)
    attend_pieces = context_spread(first.reshape(shards * own, -1)[:, :quarter_cols])

    def widen(index):
        start = sum(small_sizes[:index])
        shape = small_parts[index].shape
        piece = small[:, start:start + small_sizes[index]].astype(FULL).reshape((shards,) + shape)
        piece = jnp.moveaxis(piece, 0, -2)
        return piece.reshape(shape[:-1] + (shards * shape[-1],))

    gains_all, offsets_all = widen(0), widen(1)
    head_all = widen(2).reshape(layers, 2, head_cols)
    hidden_all = widen(3).reshape(layers, hidden)

    seg_before = [from_before(segment_ids, steps) for steps in range(back_steps, 0, -1)]
    segments_all = jnp.concatenate(seg_before + [segment_ids], axis=1)
    query_pos = jnp.arange(block, dtype=jnp.int32) + back_steps * block
    key_pos = jnp.arange((back_steps + 1) * block, dtype=jnp.int32)
    first_key = (back_steps - lax.axis_index("context")) * block
    visible = (segments_all[:, None, :] == segment_ids[:, :, None]) & (
        key_pos[None, None, :] <= query_pos[None, :, None]
    ) & (key_pos >= first_key)[None, None, :]

    mask = visible.astype(FULL)
    keys = (back_steps + 1) * block
    half = width // 2
    place = jnp.stack([lax.axis_index("tensor"), turn]).astype(jnp.int32)
    side_cols = 4 * head_cols

    def row_of(table, layer, index):
        return table[layer, index].reshape(1, -1)

    def gathered_spec(layer, member):
        at = member if layer == 0 else 2 + 3 * (layer - 1) + member
        return weight_spec(width, side_cols, at)

    vmem = whole()
    stream = inputs.reshape(tokens, width)
    kept = []
    parts = ()
    middle = None
    for layer in range(layers):
        outs = [shape((tokens, width), HALF), shape((tokens, half), HALF)]
        gain_row, offset_row = row_of(gains_all, layer, 0), row_of(offsets_all, layer, 0)
        if layer == 0:
            attend_input, sent = call(
                functools.partial(enter_kernel, False), outs, (place, stream, gain_row, offset_row),
                in_specs=[scalars()] + [vmem] * 3, out_specs=[vmem] * 2, name="enter_first")
        else:
            stream, attend_input, sent = call(
                functools.partial(enter_kernel, True), [shape((tokens, width), FULL)] + outs,
                (place, middle) + parts + (row_of(offsets_all, layer - 1, 3), gain_row, offset_row),
                in_specs=[scalars()] + [vmem] * 6, out_specs=[vmem] * 3, name="enter")
        sent = sent.reshape(rows, block, half)
        far, near = from_before(sent, 2), from_before(sent, 1)
        far_other, near_other = pair_other(far), pair_other(near)
        attend_outs = [
            shape((tokens, head_cols), HALF), shape((rows, keys, head_cols), HALF), shape((rows, keys, head_cols), HALF),
            shape((tokens, head_cols), HALF), shape((tokens, 128), FULL), shape((rows, keys, width), HALF),
            shape((tokens, width), FULL)]
        attend_args = (attend_input, far, near, far_other, near_other)
        if layer == 0:
            query, key, value, attended, log_total, wide, part, weights = call(
                functools.partial(attend_first_kernel, contexts), attend_outs + [shape((width, side_cols), HALF)],
                (place,) + tuple(attend_pieces) + attend_args + (head_all[layer], mask),
                in_specs=[scalars()] + [vmem] * (contexts + 7), out_specs=[vmem] * 8, name="attend_first")
            held = (weights, gathered, gathered)
            specs = (vmem, gathered_spec(0, 0), gathered_spec(0, 1))
        else:
            held = (gathered,) * 3
            specs = tuple(gathered_spec(layer, member) for member in range(3))
            query, key, value, attended, log_total, wide, part = call(
                attend_kernel, attend_outs, (place,) + attend_args + (held[0], head_all[layer], mask),
                in_specs=[scalars()] + [vmem] * 5 + [specs[0]] + [vmem] * 2, out_specs=[vmem] * 7, name="attend")
        before = stream
        middle, preact, part = call(
            feed_kernel,
            [shape((tokens, width), FULL), shape((tokens, hidden), FULL), shape((tokens, width), FULL)],
            (stream, part, pair_other(part), row_of(offsets_all, layer, 2), row_of(gains_all, layer, 1),
             row_of(offsets_all, layer, 1), held[1], hidden_all[layer].reshape(1, -1), held[2]),
            scratch=[pltpu.VMEM((tokens, hidden), HALF)],
            in_specs=[vmem] * 6 + [specs[1], vmem, specs[2]], out_specs=[vmem] * 3, name="feed")
        parts = (part, pair_other(part))
        kept.append((before, query, key, value, attended, log_total, wide, middle, preact, held, specs))
    stream = middle + (parts[0] + parts[1]) + offsets_all[layers - 1, 3]

    vectors = [None] * layers
    leave = None
    shares = [None] * layers
    unread = pl.BlockSpec(memory_space=pl.ANY)
    for layer in reversed(range(layers)):
        before, query, key, value, attended, log_total, wide, middle, preact, held, specs = kept[layer]
        last = layer == layers - 1
        if layer == 0:
            feed_packs = [shape((width, 2 * hidden), HALF)]
            feed_pack_specs = [vmem]
            attend_pack = shape((contexts, width, side_cols // contexts), HALF)
            attend_pack_spec = vmem
        else:
            attend_pack = shape((width, 2 * hidden + side_cols), HALF)
            feed_packs = [attend_pack]
            feed_pack_specs = [pl.BlockSpec((width, 2 * hidden), lambda *_: (0, 0))]
            attend_pack_spec = pl.BlockSpec((width, side_cols), lambda *_: (0, 2 * hidden // side_cols))
        shared = (middle, preact, row_of(gains_all, layer, 1), row_of(offsets_all, layer, 1), held[1], held[2])
        shared_specs = [vmem] * 4 + [specs[1], specs[2]]
        outs = feed_packs + [shape((1, hidden), FULL), shape((1, width), FULL), shape((tokens, width), HALF)]
        outs_specs = feed_pack_specs + [vmem] * 3
        scratch = [pltpu.VMEM((tokens, hidden), HALF)] * 2
        if last:
            upstream = cotangent.reshape(tokens, width)
            packed, hidden_sum, down_sum, part = call(
                functools.partial(feed_back_kernel, False), outs, (upstream,) + shared, scratch=scratch,
                in_specs=[vmem] + shared_specs, out_specs=outs_specs, name="feed_back_last")
        else:
            upstream, leave_sums, packed, hidden_sum, down_sum, part = call(
                functools.partial(feed_back_kernel, True),
                [shape((tokens, width), FULL), shape((2, width), FULL)] + outs, leave + shared, scratch=scratch,
                in_specs=[scalars()] + [vmem] * 5 + shared_specs, out_specs=[vmem] * 2 + outs_specs, name="feed_back")
            vectors[layer + 1] = (leave_sums,) + vectors[layer + 1]
        if layer == 0:
            feed_moved = lax.all_to_all(packed.reshape(shards, own, 2 * hidden), "shard", 0, 0)
        operands = (place, upstream, middle, part, pair_other(part), row_of(gains_all, layer, 1), attended,
                    query, key, value, log_total, mask, wide, held[0])
        attend_packed, middle_back, wide_mine, wide_other, sums, head_sums = call(
            functools.partial(attend_back_kernel, layer == 0),
            [attend_pack, shape((tokens, width), FULL), shape((rows, keys, half), FULL), shape((rows, keys, half), HALF),
             shape((3, width), FULL), shape((2, head_cols), FULL)],
            operands + (() if layer == 0 else (packed,)),
            scratch=[pltpu.VMEM((tokens, head_cols), HALF), pltpu.VMEM((rows, keys, 2 * head_cols), HALF),
                     pltpu.VMEM((tokens, head_cols), HALF)],
            aliases=None if layer == 0 else {len(operands): 0},
            in_specs=[scalars()] + [vmem] * 12 + [specs[0]] + ([] if layer == 0 else [unread]),
            out_specs=[attend_pack_spec] + [vmem] * 5, name="attend_back")
        if layer == 0:
            first_quarter = context_share(attend_packed).astype(HALF)
        else:
            shares[layer] = lax.psum_scatter(attend_packed, "shard", scatter_dimension=0, tiled=True)
        wide_sum = wide_mine + pair_other(wide_other).astype(FULL)
        half_back = wide_sum[:, back_steps * block:]
        for steps in range(1, back_steps + 1):
            start = (back_steps - steps) * block
            half_back = half_back + from_after(wide_sum[:, start:start + block].astype(HALF), steps).astype(FULL)
        half_back = half_back.reshape(tokens, half)
        leave = (place, middle_back, before, half_back, pair_other(half_back), row_of(gains_all, layer, 0))
        vectors[layer] = (sums, down_sum, head_sums, hidden_sum)
    upstream, leave_sums = call(
        leave_kernel, [shape((tokens, width), FULL), shape((2, width), FULL)], leave,
        in_specs=[scalars()] + [vmem] * 5, out_specs=[vmem] * 2, name="leave")
    vectors[0] = (leave_sums,) + vectors[0]

    def spread_out(values, shape):
        lead = shape[:-1]
        values = values.reshape(lead + (shards, shape[-1]))
        return jnp.moveaxis(values, -2, 0).reshape(shards, -1)

    gain_sums = jnp.stack([jnp.stack([entry[0][0], entry[1][0]]) for entry in vectors])
    offset_sums = jnp.stack([jnp.concatenate([entry[0][1:2], entry[1][1:], entry[2]]) for entry in vectors])
    head_sums = jnp.stack([entry[3] for entry in vectors])
    hidden_sums = jnp.stack([entry[4] for entry in vectors])
    vector_pack = jnp.concatenate(
        [spread_out(values, part.shape) for values, part in zip((gain_sums, offset_sums, head_sums, hidden_sums), small_parts)]
        + [jnp.zeros((shards, small_padded - small_total), FULL)], axis=1)
    vector_pack = context_sum(vector_pack.reshape(shards * small_rows, 128)).astype(HALF)
    vector_pack = jnp.pad(vector_pack.reshape(shards, small_rows, 128), ((0, 0), (0, own - small_rows), (0, 0)))
    final = jnp.concatenate([first_quarter.reshape(shards, own, -1), vector_pack], axis=2)
    final, feed_moved, shares[1] = lax.optimization_barrier((final, feed_moved, shares[1]))
    final = jnp.sum(lax.all_to_all(final, "shard", 0, 0).astype(FULL), axis=0)
    first_cols = final.shape[1] - 128
    vector_own = final[:small_rows, first_cols:].reshape(-1)
    vector_out = []
    for index, part in enumerate(small_parts):
        start = sum(small_sizes[:index])
        vector_out.append(vector_own[start:start + small_sizes[index]].reshape(part.shape))
    gains_grad, offsets_grad, head_grad, hidden_grad = vector_out

    feed_first = jnp.sum(feed_moved.astype(FULL), axis=0).astype(HALF)
    pieces = [feed_first.reshape(own, contexts, -1)] + [shares[layer].reshape(own, contexts, -1) for layer in range(1, layers)]
    later = context_share(jnp.concatenate(pieces, axis=2).transpose(1, 0, 2)).astype(HALF)
    sizes = [first_cols] + [piece.shape[2] for piece in pieces]
    quarters = jnp.concatenate([final[:, :first_cols].astype(HALF), later], axis=1)
    quarters = lax.all_gather(quarters, "context", axis=0, tiled=False).astype(FULL)
    joined, start = [], 0
    for size in sizes:
        joined.append(jnp.moveaxis(quarters[:, :, start:start + size], 0, 1).reshape(own, -1))
        start += size
    feed_own = joined[1:]
    attend_own = [joined[0]] + [share[:, 2 * hidden:] for share in joined[2:]]
    projection_grad = jnp.stack(
        [jnp.stack([share[:, k * head_cols:(k + 1) * head_cols] for k in range(3)]) for share in attend_own])
    mixing_grad = jnp.stack([share[:, 3 * head_cols:].T for share in attend_own])
    expansion_grad = jnp.stack([share[:, :hidden] for share in feed_own])
    contraction_grad = jnp.stack([share[:, hidden:2 * hidden].T for share in feed_own])
    return (
        stream.reshape(rows, block, width),
        upstream.reshape(rows, block, width),
        projection_grad,
        head_grad,
        mixing_grad,
        expansion_grad,
        hidden_grad,
        contraction_grad,
        gains_grad,
        offsets_grad,
    )


def solution(mesh):
    in_specs = (
        P("shard", "context", None),
        P("shard", "context"),
        P(None, None, "shard", "tensor"),
        P(None, None, "tensor", "shard"),
        P(None, "tensor", "shard"),
        P(None, "shard", "tensor"),
        P(None, "tensor", "shard"),
        P(None, "tensor", "shard"),
        P(None, None, "shard"),
        P(None, None, "shard"),
        P("shard", "context", None),
    )
    out_specs = (
        P("shard", "context", None),
        P("shard", "context", None),
        P(None, None, "shard", "tensor"),
        P(None, None, "tensor", "shard"),
        P(None, "tensor", "shard"),
        P(None, "shard", "tensor"),
        P(None, "tensor", "shard"),
        P(None, "tensor", "shard"),
        P(None, None, "shard"),
        P(None, None, "shard"),
    )
    return jax.shard_map(
        per_device, mesh=mesh, in_specs=in_specs, out_specs=out_specs, check_vma=False
    )
```

```python
import functools

import jax
import jax.numpy as jnp
from jax import lax
from jax.experimental import pallas as pl
from jax.experimental.pallas import tpu as pltpu
from jax.sharding import PartitionSpec as P

HEAD = 64

EPS = 1e-05
GELU_COEF = 0.7978845608028654
GELU_CUBE = 0.044715
MASKED = -1e30
HALF = jnp.bfloat16
FULL = jnp.float32


def gelu_value(preact):
    inner_arg = GELU_COEF * (preact + GELU_CUBE * preact * preact * preact)
    return 0.5 * preact * (1.0 + jnp.tanh(inner_arg))


def norm_backward(upstream, normed, spread, gain_row):
    scaled = upstream * gain_row
    first_mean = jnp.mean(scaled, axis=-1, keepdims=True)
    second_mean = jnp.mean(scaled * normed, axis=-1, keepdims=True)
    return spread * (scaled - first_mean - normed * second_mean)


def dot(left, right, left_dim, right_dim):
    return lax.dot_general(
        left, right, (((left_dim,), (right_dim,)), ((), ())), preferred_element_type=FULL
    )


def from_before(block, steps):
    size = lax.axis_size("context")
    return lax.ppermute(block, "context", [(i, i + steps) for i in range(size - steps)])


def from_after(block, steps):
    size = lax.axis_size("context")
    return lax.ppermute(block, "context", [(i + steps, i) for i in range(size - steps)])


def context_share(parts):
    size = lax.axis_size("context")
    place = lax.axis_index("context")
    total = lax.dynamic_index_in_dim(parts, place, 0, keepdims=False).astype(FULL)
    for steps in range(1, size):
        piece = lax.dynamic_index_in_dim(parts, (place + steps) % size, 0, keepdims=False)
        total = total + lax.ppermute(piece, "context", [(i, (i + steps) % size) for i in range(size)]).astype(FULL)
    return total


def context_spread(part):
    size = lax.axis_size("context")
    return [part] + [
        lax.ppermute(part, "context", [(i, (i + steps) % size) for i in range(size)]) for steps in range(1, size)]


def context_sum(part):
    size = lax.axis_size("context")
    total = part.astype(FULL)
    for steps in range(1, size):
        moved = lax.ppermute(part, "context", [(i, (i + steps) % size) for i in range(size)])
        total = total + moved.astype(FULL)
    return total


def pair_other(part):
    size = lax.axis_size("tensor")
    return lax.ppermute(part, "tensor", [(i, (i + 1) % size) for i in range(size)])


def call(body, outs, ins, scratch=(), aliases=None, in_specs=None, out_specs=None, name=None, steps=1):
    return pl.pallas_call(
        body,
        out_shape=outs,
        grid=(steps,),
        in_specs=in_specs,
        out_specs=out_specs,
        scratch_shapes=list(scratch),
        input_output_aliases=aliases or {},
        compiler_params=pltpu.CompilerParams(vmem_limit_bytes=58 * 2**20),
        name=name,
    )(*ins)


def whole():
    return pl.BlockSpec(memory_space=pltpu.VMEM)


def scalars():
    return pl.BlockSpec(memory_space=pltpu.SMEM)


def shape(dims, dtype):
    return jax.ShapeDtypeStruct(dims, dtype)


def weight_spec(depth, cols, index):
    return pl.BlockSpec((depth, cols), lambda *_: (0, index))


def norm_stats(stream):
    center = stream - jnp.mean(stream, axis=-1, keepdims=True)
    spread = lax.rsqrt(jnp.mean(center * center, axis=-1, keepdims=True) + EPS)
    return center * spread, spread


def enter_kernel(has_parts, place, *refs):
    if has_parts:
        middle, mine, other, offset_last, gain, offset, stream_out, attend_out, half_out = refs
        stream = middle[...] + (mine[...] + other[...]) + offset_last[...]
        stream_out[...] = stream
    else:
        stream_in, gain, offset, attend_out, half_out = refs
        stream = stream_in[...]
    normed, _ = norm_stats(stream)
    attend = (normed * gain[...] + offset[...]).astype(HALF)
    attend_out[...] = attend
    cols = half_out.shape[1]
    half_out[...] = jnp.where(place[0] == 0, attend[:, :cols], attend[:, cols:])


def assemble(place, pieces, out):
    count, cols = len(pieces), pieces[0].shape[1]
    for index, piece in enumerate(pieces):
        source = lax.rem(place[1] + count - index, count)
        out[:, pl.ds(pl.multiple_of(source * cols, cols), cols)] = piece[...]


def attend_first_kernel(count, place, *refs):
    pieces, rest, weights = refs[:count], refs[count:-1], refs[-1]
    assemble(place, pieces, weights)
    attend_kernel(place, *rest[:5], weights, *rest[5:])


def attend_kernel(place, own, far_mine, near_mine, far_other, near_other, weights, bias, visible,
                  query_out, key_out, value_out, attended_out, log_out, wide_out, part_out):
    tokens, width = own.shape
    rows, block, keys = visible.shape
    cols = query_out.shape[1]
    half = far_mine.shape[2]
    wide_out[:, keys - block:, :] = own[...].reshape(rows, block, width)

    def put(first, mine, other):
        mine, other = mine[...], other[...]
        low = place[0] == 0
        wide_out[:, first:first + block, :half] = jnp.where(low, mine, other)
        wide_out[:, first:first + block, half:] = jnp.where(low, other, mine)

    put(0, far_mine, far_other)
    put(block, near_mine, near_other)
    query_out[...] = (dot(own[...], weights[:, :cols], 1, 0) + bias[0:1, :]).astype(HALF)
    wide = wide_out[...].reshape(rows * keys, width)
    key_out[...] = dot(wide, weights[:, cols:2 * cols], 1, 0).astype(HALF).reshape(rows, keys, cols)
    value_out[...] = (dot(wide, weights[:, 2 * cols:3 * cols], 1, 0) + bias[1:2, :]).astype(HALF).reshape(rows, keys, cols)
    scale = HEAD ** (-0.5)
    pairs = cols // 128
    low_lane = lax.broadcasted_iota(jnp.int32, (block, 128), 1) < HEAD
    lane = lax.broadcasted_iota(jnp.int32, (block, 128), 1)
    log_out[...] = jnp.zeros(log_out.shape, FULL)

    def one(step, carry):
        row, pair = step // pairs, step % pairs
        at_rows = pl.ds(pl.multiple_of(row * block, block), block)
        at_cols = pl.ds(pl.multiple_of(pair * 128, 128), 128)
        query = query_out[at_rows, at_cols]
        key = key_out[row, :, at_cols]
        value = value_out[row, :, at_cols]
        shown = visible[row] > 0
        outs = []
        logs = log_out[at_rows, :]
        for which in range(2):
            picked = jnp.where(low_lane if which == 0 else ~low_lane, query, jnp.zeros_like(query))
            scores = jnp.where(shown, dot(picked, key, 1, 1) * scale, MASKED)
            top = jnp.max(scores, axis=-1, keepdims=True)
            grown = jnp.exp(scores - top)
            total = jnp.sum(grown, axis=-1, keepdims=True)
            logs = jnp.where(lane == 2 * pair + which, top + jnp.log(total), logs)
            soft = (grown * (1.0 / total)).astype(HALF)
            outs.append(dot(soft, value, 1, 0))
        log_out[at_rows, :] = logs
        attended_out[at_rows, at_cols] = jnp.where(low_lane, outs[0], outs[1]).astype(HALF)
        return carry

    lax.fori_loop(0, rows * pairs, one, 0)
    part_out[...] = dot(attended_out[...], weights[:, 3 * cols:4 * cols], 1, 1)


def feed_kernel(stream, mine, other, offset_mid, gain, offset, up, hidden_bias, down,
                middle_out, preact_out, part_out, active):
    middle = stream[...] + (mine[...] + other[...]) + offset_mid[...]
    middle_out[...] = middle
    normed, _ = norm_stats(middle)
    feed = (normed * gain[...] + offset[...]).astype(HALF)
    preact_out[...] = dot(feed, up[...], 1, 0) + hidden_bias[...]
    step_rows = 32

    def one(step, carry):
        at = pl.ds(pl.multiple_of(step * step_rows, step_rows), step_rows)
        active[at, :] = gelu_value(preact_out[at, :]).astype(HALF)
        return carry

    lax.fori_loop(0, preact_out.shape[0] // step_rows, one, 0)
    part_out[...] = dot(active[...], down[...], 1, 1)


def leave_norm(place, middle_back, stream, mine, other, gain):
    low = place[0] == 0
    mine, other = mine[...], other[...]
    back = jnp.concatenate([jnp.where(low, mine, other), jnp.where(low, other, mine)], axis=1)
    normed, spread = norm_stats(stream[...])
    upstream = middle_back[...] + norm_backward(back, normed, spread, gain[...])
    sums = jnp.concatenate(
        [jnp.sum(back * normed, axis=0, keepdims=True), jnp.sum(back, axis=0, keepdims=True)], axis=0)
    return upstream, sums


def leave_kernel(place, middle_back, stream, mine, other, gain, upstream_out, sums_out):
    upstream, sums = leave_norm(place, middle_back, stream, mine, other, gain)
    upstream_out[...] = upstream
    sums_out[...] = sums


def feed_back_kernel(has_leave, *refs):
    if has_leave:
        place, middle_back, stream, mine, other, gain_one = refs[:6]
        middle, preact, gain, offset, up, down, _ = refs[6:13]
        upstream_out, sums_out, pack, hidden_sum, down_sum, part_out, active, hidden_half = refs[13:]
        upstream, sums = leave_norm(place, middle_back, stream, mine, other, gain_one)
        upstream_out[...] = upstream
        sums_out[...] = sums
    else:
        upstream_in, middle, preact, gain, offset, up, down = refs[:7]
        feed_out, hidden_sum, down_sum, part_out, active, hidden_half = refs[7:]
        upstream = upstream_in[...]
    hidden = up.shape[1]
    step_rows = 32
    upstream_half = upstream.astype(HALF)
    down_sum[...] = jnp.sum(upstream, axis=0, keepdims=True)
    normed, _ = norm_stats(middle[...])
    feed = (normed * gain[...] + offset[...]).astype(HALF)
    back = dot(upstream_half, down[...], 1, 0)
    hidden_sum[...] = jnp.zeros(hidden_sum.shape, FULL)
    for first in range(0, upstream.shape[0], step_rows):
        inner = slice(first, first + step_rows)
        pre = preact[inner, :]
        square = pre * pre
        tanh_value = jnp.tanh(GELU_COEF * (pre + GELU_CUBE * square * pre))
        active[inner, :] = (0.5 * pre * (1.0 + tanh_value)).astype(HALF)
        slope = 0.5 * (1.0 + tanh_value) + 0.5 * pre * (1.0 - tanh_value * tanh_value) * GELU_COEF * (
            1.0 + 3.0 * GELU_CUBE * square)
        hidden_back = back[inner, :] * slope
        hidden_sum[...] += jnp.sum(hidden_back, axis=0, keepdims=True)
        hidden_half[inner, :] = hidden_back.astype(HALF)
    part_out[...] = dot(hidden_half[...], up[...], 1, 1).astype(HALF)
    if has_leave:
        pack[:, :hidden] = dot(feed, hidden_half[...], 0, 0).astype(HALF)
        pack[:, hidden:2 * hidden] = dot(upstream_half, active[...], 0, 0).astype(HALF)
    else:
        feed_out[...] = feed


def attend_grads(middle_half, attended, wide, wide_query, wide_both):
    tokens, cols = wide_query.shape
    rows, keys, width = wide.shape
    own = wide[:, keys - tokens // rows:, :].reshape(tokens, width)
    both = wide_both[...].reshape(rows * keys, 2 * cols)
    query_grad = dot(own, wide_query[...], 0, 0).astype(HALF)
    both_grad = dot(wide[...].reshape(rows * keys, width), both, 0, 0).astype(HALF)
    mix_grad = dot(middle_half, attended[...], 0, 0).astype(HALF)
    return query_grad, both_grad[:, :cols], both_grad[:, cols:], mix_grad


def grads_kernel(upstream, feed, hidden_half, active, middle_back, attended, wide, wide_query, wide_both, pack):
    step = pl.program_id(0)

    @pl.when(step == 0)
    def _():
        pack[...] = dot(feed[...], hidden_half[...], 0, 0).astype(HALF)

    @pl.when(step == 1)
    def _():
        pack[...] = dot(upstream[...].astype(HALF), active[...], 0, 0).astype(HALF)

    @pl.when(step == 2)
    def _():
        cols = wide_query.shape[1]
        middle_half = middle_back[...].astype(HALF)
        for index, grad in enumerate(attend_grads(middle_half, attended, wide, wide_query, wide_both)):
            pack[:, index * cols:(index + 1) * cols] = grad


def attend_back_kernel(spread_pack, place, upstream, middle, mine, other, gain, attended, query, key, value,
                       log_total, visible, wide, weights, *refs):
    if spread_pack:
        pack, middle_out, wide_mine, wide_other, sums_out, heads_out, wide_query, wide_both, near = refs
    else:
        middle_out, wide_mine, wide_other, sums_out, heads_out, wide_query, wide_both, near = refs
    tokens, width = upstream.shape
    rows, block, keys = visible.shape
    cols = query.shape[1]
    scale = HEAD ** (-0.5)
    feed_back = mine[...].astype(FULL) + other[...].astype(FULL)
    normed, spread = norm_stats(middle[...])
    middle_back = upstream[...] + norm_backward(feed_back, normed, spread, gain[...])
    middle_out[...] = middle_back
    sums_out[...] = jnp.concatenate(
        [jnp.sum(feed_back * normed, axis=0, keepdims=True), jnp.sum(feed_back, axis=0, keepdims=True),
         jnp.sum(middle_back, axis=0, keepdims=True)], axis=0)
    middle_half = middle_back.astype(HALF)
    near[...] = dot(middle_half, weights[:, 3 * cols:4 * cols], 1, 0).astype(HALF)
    pairs = cols // 128
    low_lane = lax.broadcasted_iota(jnp.int32, (block, 128), 1) < HEAD
    low_key = lax.broadcasted_iota(jnp.int32, (keys, 128), 1) < HEAD
    lane = lax.broadcasted_iota(jnp.int32, (block, 128), 1)
    heads_out[...] = jnp.zeros(heads_out.shape, FULL)

    def one(step, carry):
        row, pair = step // pairs, step % pairs
        at_rows = pl.ds(pl.multiple_of(row * block, block), block)
        at_cols = pl.ds(pl.multiple_of(pair * 128, 128), 128)
        at_values = pl.ds(pl.multiple_of(cols + pair * 128, 128), 128)
        query_two = query[at_rows, at_cols]
        key_two, value_two = key[row, :, at_cols], value[row, :, at_cols]
        back_two = near[at_rows, at_cols]
        product = back_two.astype(FULL) * attended[at_rows, at_cols].astype(FULL)
        shown = visible[row] > 0
        logs = log_total[at_rows, :]
        query_parts, key_parts, value_parts = [], [], []
        for which in range(2):
            lanes = low_lane if which == 0 else ~low_lane
            picked = jnp.where(lanes, query_two, jnp.zeros_like(query_two))
            picked_back = jnp.where(lanes, back_two, jnp.zeros_like(back_two))
            delta = jnp.sum(jnp.where(lanes, product, 0.0), axis=-1, keepdims=True)
            own_log = jnp.sum(jnp.where(lane == 2 * pair + which, logs, 0.0), axis=-1, keepdims=True)
            scores = jnp.where(shown, dot(picked, key_two, 1, 1) * scale, MASKED)
            soft = jnp.exp(scores - own_log)
            score_back = (soft * (dot(picked_back, value_two, 1, 1) - delta) * scale).astype(HALF)
            query_parts.append(dot(score_back, key_two, 1, 0))
            key_parts.append(dot(score_back, query_two, 0, 0))
            value_parts.append(dot(soft.astype(HALF), back_two, 0, 0))
        query_back = jnp.where(low_lane, query_parts[0], query_parts[1])
        key_back = jnp.where(low_key, key_parts[0], key_parts[1])
        value_back = jnp.where(low_key, value_parts[0], value_parts[1])
        heads_out[0:1, at_cols] += jnp.sum(query_back, axis=0, keepdims=True)
        heads_out[1:2, at_cols] += jnp.sum(value_back, axis=0, keepdims=True)
        wide_query[at_rows, at_cols] = query_back.astype(HALF)
        wide_both[row, :, at_cols] = key_back.astype(HALF)
        wide_both[row, :, at_values] = value_back.astype(HALF)
        return carry

    lax.fori_loop(0, rows * pairs, one, 0)
    both = wide_both[...].reshape(rows * keys, 2 * cols)
    if spread_pack:
        for index, grad in enumerate(attend_grads(middle_half, attended, wide, wide_query, wide_both)):
            pack[index] = grad
    wide_back = dot(both, weights[:, cols:3 * cols], 1, 1).reshape(rows, keys, width)
    own_back = dot(wide_query[...], weights[:, :cols], 1, 1).reshape(rows, block, width)
    half = width // 2
    low = place[0] == 0

    def put(first, count, values):
        wide_mine[:, first:first + count, :] = jnp.where(low, values[..., :half], values[..., half:])
        wide_other[:, first:first + count, :] = jnp.where(low, values[..., half:], values[..., :half]).astype(HALF)

    put(0, keys - block, wide_back[:, :keys - block])
    put(keys - block, block, wide_back[:, keys - block:] + own_back)


def per_device(
    inputs,
    segment_ids,
    projection,
    head_bias,
    mixing,
    expansion,
    hidden_bias,
    contraction,
    norm_gains,
    offsets,
    cotangent,
):
    layers = projection.shape[0]
    rows, block, width = inputs.shape
    shards = lax.axis_size("shard")
    contexts = lax.axis_size("context")
    own = projection.shape[2]
    heads = head_bias.shape[2]
    head_cols = projection.shape[3]
    hidden = expansion.shape[2]
    tokens = rows * block
    head_scale = HEAD ** (-0.5)
    back_steps = 2

    def attend_block(layer):
        return [projection[layer, 0], projection[layer, 1], projection[layer, 2], mixing[layer].T]

    others = [expansion[0], contraction[0].T]
    for layer in range(1, layers):
        others += attend_block(layer) + [expansion[layer], contraction[layer].T]
    gathered = lax.all_gather(jnp.concatenate(others, axis=1), "shard", axis=0, tiled=True)
    small_parts = [norm_gains, offsets, head_bias, hidden_bias]
    small_sizes = [part.size for part in small_parts]
    small_total = sum(small_sizes)
    small_padded = -(-small_total // 1024) * 1024
    small_rows = small_padded // 128
    small = jnp.concatenate([part.reshape(-1) for part in small_parts] + [jnp.zeros((own * 128 - small_total,), HALF)])
    turn = lax.axis_index("context")
    quarter_cols = 4 * head_cols // contexts
    first = jnp.concatenate([
        lax.dynamic_slice_in_dim(jnp.concatenate(attend_block(0), axis=1), turn * quarter_cols, quarter_cols, 1),
        small.reshape(own, 128)], axis=1)
    first = lax.all_to_all(jnp.broadcast_to(first[None], (shards,) + first.shape), "shard", 0, 0)
    small = first[:, :small_rows, first.shape[2] - 128:].reshape(shards, small_padded)
    attend_pieces = context_spread(first.reshape(shards * own, -1)[:, :quarter_cols])

    def widen(index):
        start = sum(small_sizes[:index])
        shape = small_parts[index].shape
        piece = small[:, start:start + small_sizes[index]].astype(FULL).reshape((shards,) + shape)
        piece = jnp.moveaxis(piece, 0, -2)
        return piece.reshape(shape[:-1] + (shards * shape[-1],))

    gains_all, offsets_all = widen(0), widen(1)
    head_all = widen(2).reshape(layers, 2, head_cols)
    hidden_all = widen(3).reshape(layers, hidden)

    seg_before = [from_before(segment_ids, steps) for steps in range(back_steps, 0, -1)]
    segments_all = jnp.concatenate(seg_before + [segment_ids], axis=1)
    query_pos = jnp.arange(block, dtype=jnp.int32) + back_steps * block
    key_pos = jnp.arange((back_steps + 1) * block, dtype=jnp.int32)
    first_key = (back_steps - lax.axis_index("context")) * block
    visible = (segments_all[:, None, :] == segment_ids[:, :, None]) & (
        key_pos[None, None, :] <= query_pos[None, :, None]
    ) & (key_pos >= first_key)[None, None, :]

    mask = visible.astype(FULL)
    keys = (back_steps + 1) * block
    half = width // 2
    place = jnp.stack([lax.axis_index("tensor"), turn]).astype(jnp.int32)
    side_cols = 4 * head_cols

    def row_of(table, layer, index):
        return table[layer, index].reshape(1, -1)

    def gathered_spec(layer, member):
        at = member if layer == 0 else 2 + 3 * (layer - 1) + member
        return weight_spec(width, side_cols, at)

    vmem = whole()
    stream = inputs.reshape(tokens, width)
    kept = []
    parts = ()
    middle = None
    for layer in range(layers):
        outs = [shape((tokens, width), HALF), shape((tokens, half), HALF)]
        gain_row, offset_row = row_of(gains_all, layer, 0), row_of(offsets_all, layer, 0)
        if layer == 0:
            attend_input, sent = call(
                functools.partial(enter_kernel, False), outs, (place, stream, gain_row, offset_row),
                in_specs=[scalars()] + [vmem] * 3, out_specs=[vmem] * 2, name="enter_first")
        else:
            stream, attend_input, sent = call(
                functools.partial(enter_kernel, True), [shape((tokens, width), FULL)] + outs,
                (place, middle) + parts + (row_of(offsets_all, layer - 1, 3), gain_row, offset_row),
                in_specs=[scalars()] + [vmem] * 6, out_specs=[vmem] * 3, name="enter")
        sent = sent.reshape(rows, block, half)
        far, near = from_before(sent, 2), from_before(sent, 1)
        far_other, near_other = pair_other(far), pair_other(near)
        attend_outs = [
            shape((tokens, head_cols), HALF), shape((rows, keys, head_cols), HALF), shape((rows, keys, head_cols), HALF),
            shape((tokens, head_cols), HALF), shape((tokens, 128), FULL), shape((rows, keys, width), HALF),
            shape((tokens, width), FULL)]
        attend_args = (attend_input, far, near, far_other, near_other)
        if layer == 0:
            query, key, value, attended, log_total, wide, part, weights = call(
                functools.partial(attend_first_kernel, contexts), attend_outs + [shape((width, side_cols), HALF)],
                (place,) + tuple(attend_pieces) + attend_args + (head_all[layer], mask),
                in_specs=[scalars()] + [vmem] * (contexts + 7), out_specs=[vmem] * 8, name="attend_first")
            held = (weights, gathered, gathered)
            specs = (vmem, gathered_spec(0, 0), gathered_spec(0, 1))
        else:
            held = (gathered,) * 3
            specs = tuple(gathered_spec(layer, member) for member in range(3))
            query, key, value, attended, log_total, wide, part = call(
                attend_kernel, attend_outs, (place,) + attend_args + (held[0], head_all[layer], mask),
                in_specs=[scalars()] + [vmem] * 5 + [specs[0]] + [vmem] * 2, out_specs=[vmem] * 7, name="attend")
        before = stream
        middle, preact, part = call(
            feed_kernel,
            [shape((tokens, width), FULL), shape((tokens, hidden), FULL), shape((tokens, width), FULL)],
            (stream, part, pair_other(part), row_of(offsets_all, layer, 2), row_of(gains_all, layer, 1),
             row_of(offsets_all, layer, 1), held[1], hidden_all[layer].reshape(1, -1), held[2]),
            scratch=[pltpu.VMEM((tokens, hidden), HALF)],
            in_specs=[vmem] * 6 + [specs[1], vmem, specs[2]], out_specs=[vmem] * 3, name="feed")
        parts = (part, pair_other(part))
        kept.append((before, query, key, value, attended, log_total, wide, middle, preact, held, specs))
    stream = middle + (parts[0] + parts[1]) + offsets_all[layers - 1, 3]

    pack_shape = shape((width, layers * 2 * hidden + (layers - 1) * side_cols), HALF)
    vectors = [None] * layers
    leave = None
    packed = None
    unread = pl.BlockSpec(memory_space=pl.ANY)
    for layer in reversed(range(layers)):
        before, query, key, value, attended, log_total, wide, middle, preact, held, specs = kept[layer]
        last = layer == layers - 1
        feed_pack_spec = pl.BlockSpec((width, 2 * hidden), functools.partial(lambda at, *_: (0, at), layer))
        shared = (middle, preact, row_of(gains_all, layer, 1), row_of(offsets_all, layer, 1), held[1], held[2])
        shared_specs = [vmem] * 4 + [specs[1], specs[2]]
        outs = [pack_shape, shape((1, hidden), FULL), shape((1, width), FULL), shape((tokens, width), HALF)]
        outs_specs = [feed_pack_spec] + [vmem] * 3
        scratch = [pltpu.VMEM((tokens, hidden), HALF)] * 2
        if last:
            upstream = cotangent.reshape(tokens, width)
            feed_held, hidden_sum, down_sum, part, active, hidden_half = call(
                functools.partial(feed_back_kernel, False),
                [shape((tokens, width), HALF)] + outs[1:] + [shape((tokens, hidden), HALF)] * 2, (upstream,) + shared,
                in_specs=[vmem] + shared_specs, out_specs=[vmem] * 6, name="feed_back_last")
        else:
            operands = leave + shared
            upstream, leave_sums, packed, hidden_sum, down_sum, part = call(
                functools.partial(feed_back_kernel, True),
                [shape((tokens, width), FULL), shape((2, width), FULL)] + outs, operands + (packed,), scratch=scratch,
                aliases={len(operands): 2},
                in_specs=[scalars()] + [vmem] * 5 + shared_specs + [unread], out_specs=[vmem] * 2 + outs_specs, name="feed_back")
            vectors[layer + 1] = (leave_sums,) + vectors[layer + 1]
        if layer == 0:
            share = lax.psum_scatter(packed, "shard", scatter_dimension=0, tiled=True)
            attend_pack = shape((contexts, width, side_cols // contexts), HALF)
            attend_pack_spec = vmem
        operands = (place, upstream, middle, part, pair_other(part), row_of(gains_all, layer, 1), attended,
                    query, key, value, log_total, mask, wide, held[0])
        attend_outs = [
            shape((tokens, width), FULL), shape((rows, keys, half), FULL), shape((rows, keys, half), HALF),
            shape((3, width), FULL), shape((2, head_cols), FULL)]
        spare = [((tokens, head_cols), HALF), ((rows, keys, 2 * head_cols), HALF), ((tokens, head_cols), HALF)]
        attend_specs = [scalars()] + [vmem] * 12 + [specs[0]]
        if layer == 0:
            attend_packed, middle_back, wide_mine, wide_other, sums, head_sums = call(
                functools.partial(attend_back_kernel, True), [attend_pack] + attend_outs, operands,
                scratch=[pltpu.VMEM(*entry) for entry in spare], in_specs=attend_specs,
                out_specs=[attend_pack_spec] + [vmem] * 5, name="attend_back")
            attend_quarter = context_share(attend_packed).astype(HALF)
        else:
            middle_back, wide_mine, wide_other, sums, head_sums, wide_query, wide_both = call(
                functools.partial(attend_back_kernel, False), attend_outs + [shape(*entry) for entry in spare[:2]], operands,
                scratch=[pltpu.VMEM(*spare[2])], in_specs=attend_specs, out_specs=[vmem] * 7, name="attend_back_last")
            packed = call(
                grads_kernel, pack_shape,
                (upstream, feed_held, hidden_half, active, middle_back, attended, wide, wide_query, wide_both),
                in_specs=[vmem] * 9, out_specs=pl.BlockSpec((width, side_cols), lambda step: (0, 2 * (layers - 1) + step)),
                name="grads_last", steps=3)
        wide_sum = wide_mine + pair_other(wide_other).astype(FULL)
        half_back = wide_sum[:, back_steps * block:]
        returned = []
        for steps in range(1, back_steps + 1):
            start = (back_steps - steps) * block
            returned.append(from_after(wide_sum[:, start:start + block].astype(HALF), steps))
        if last:
            returned, packed = lax.optimization_barrier((returned, packed))
        for piece in returned:
            half_back = half_back + piece.astype(FULL)
        half_back = half_back.reshape(tokens, half)
        leave = (place, middle_back, before, half_back, pair_other(half_back), row_of(gains_all, layer, 0))
        vectors[layer] = (sums, down_sum, head_sums, hidden_sum)
    upstream, leave_sums = call(
        leave_kernel, [shape((tokens, width), FULL), shape((2, width), FULL)], leave,
        in_specs=[scalars()] + [vmem] * 5, out_specs=[vmem] * 2, name="leave")
    vectors[0] = (leave_sums,) + vectors[0]

    def spread_out(values, shape):
        lead = shape[:-1]
        values = values.reshape(lead + (shards, shape[-1]))
        return jnp.moveaxis(values, -2, 0).reshape(shards, -1)

    gain_sums = jnp.stack([jnp.stack([entry[0][0], entry[1][0]]) for entry in vectors])
    offset_sums = jnp.stack([jnp.concatenate([entry[0][1:2], entry[1][1:], entry[2]]) for entry in vectors])
    head_sums = jnp.stack([entry[3] for entry in vectors])
    hidden_sums = jnp.stack([entry[4] for entry in vectors])
    vector_pack = jnp.concatenate(
        [spread_out(values, part.shape) for values, part in zip((gain_sums, offset_sums, head_sums, hidden_sums), small_parts)]
        + [jnp.zeros((shards, small_padded - small_total), FULL)], axis=1)
    vector_pack = context_sum(vector_pack.reshape(shards * small_rows, 128)).astype(HALF)
    vector_pack = jnp.pad(vector_pack.reshape(shards, small_rows, 128), ((0, 0), (0, own - small_rows), (0, 0)))
    final = jnp.concatenate([attend_quarter.reshape(shards, own, -1), vector_pack], axis=2)
    final = jnp.sum(lax.all_to_all(final, "shard", 0, 0).astype(FULL), axis=0)
    attend_sum = final[:, :side_cols // contexts].astype(HALF)
    vector_own = final[:small_rows, side_cols // contexts:].reshape(-1)
    vector_out = []
    for index, part in enumerate(small_parts):
        start = sum(small_sizes[:index])
        vector_out.append(vector_own[start:start + small_sizes[index]].reshape(part.shape))
    gains_grad, offsets_grad, head_grad, hidden_grad = vector_out

    share = share.reshape(own, contexts, -1).transpose(1, 0, 2)
    share = jnp.sum(lax.all_to_all(share, "context", 0, 0).astype(FULL), axis=0).astype(HALF)
    quarters = lax.all_gather(jnp.concatenate([share, attend_sum], axis=1), "context", axis=0, tiled=False).astype(FULL)
    share_cols = share.shape[1]

    def join(piece):
        return jnp.moveaxis(piece, 0, 1).reshape(own, -1)

    attend_own, share = [join(quarters[:, :, share_cols:])], join(quarters[:, :, :share_cols])
    feed_own = [share[:, 2 * hidden * layer:2 * hidden * (layer + 1)] for layer in range(layers)]
    for layer in range(1, layers):
        start = 2 * hidden * layers + side_cols * (layer - 1)
        attend_own.append(share[:, start:start + side_cols])
    projection_grad = jnp.stack(
        [jnp.stack([share[:, k * head_cols:(k + 1) * head_cols] for k in range(3)]) for share in attend_own])
    mixing_grad = jnp.stack([share[:, 3 * head_cols:].T for share in attend_own])
    expansion_grad = jnp.stack([share[:, :hidden] for share in feed_own])
    contraction_grad = jnp.stack([share[:, hidden:].T for share in feed_own])
    return (
        stream.reshape(rows, block, width),
        upstream.reshape(rows, block, width),
        projection_grad,
        head_grad,
        mixing_grad,
        expansion_grad,
        hidden_grad,
        contraction_grad,
        gains_grad,
        offsets_grad,
    )


def solution(mesh):
    in_specs = (
        P("shard", "context", None),
        P("shard", "context"),
        P(None, None, "shard", "tensor"),
        P(None, None, "tensor", "shard"),
        P(None, "tensor", "shard"),
        P(None, "shard", "tensor"),
        P(None, "tensor", "shard"),
        P(None, "tensor", "shard"),
        P(None, None, "shard"),
        P(None, None, "shard"),
        P("shard", "context", None),
    )
    out_specs = (
        P("shard", "context", None),
        P("shard", "context", None),
        P(None, None, "shard", "tensor"),
        P(None, None, "tensor", "shard"),
        P(None, "tensor", "shard"),
        P(None, "shard", "tensor"),
        P(None, "tensor", "shard"),
        P(None, "tensor", "shard"),
        P(None, None, "shard"),
        P(None, None, "shard"),
    )
    return jax.shard_map(
        per_device, mesh=mesh, in_specs=in_specs, out_specs=out_specs, check_vma=False
    )
```

```python
import functools

import jax
import jax.numpy as jnp
from jax import lax
from jax.experimental import pallas as pl
from jax.experimental.pallas import tpu as pltpu
from jax.sharding import PartitionSpec as P

HEAD = 64

EPS = 1e-05
GELU_COEF = 0.7978845608028654
GELU_CUBE = 0.044715
MASKED = -1e30
HALF = jnp.bfloat16
FULL = jnp.float32


def gelu_value(preact):
    inner_arg = GELU_COEF * (preact + GELU_CUBE * preact * preact * preact)
    return 0.5 * preact * (1.0 + jnp.tanh(inner_arg))


def norm_backward(upstream, normed, spread, gain_row):
    scaled = upstream * gain_row
    first_mean = jnp.mean(scaled, axis=-1, keepdims=True)
    second_mean = jnp.mean(scaled * normed, axis=-1, keepdims=True)
    return spread * (scaled - first_mean - normed * second_mean)


def dot(left, right, left_dim, right_dim):
    return lax.dot_general(
        left, right, (((left_dim,), (right_dim,)), ((), ())), preferred_element_type=FULL
    )


def from_before(block, steps):
    size = lax.axis_size("context")
    return lax.ppermute(block, "context", [(i, i + steps) for i in range(size - steps)])


def from_after(block, steps):
    size = lax.axis_size("context")
    return lax.ppermute(block, "context", [(i + steps, i) for i in range(size - steps)])


def context_share(parts):
    size = lax.axis_size("context")
    place = lax.axis_index("context")
    total = lax.dynamic_index_in_dim(parts, place, 0, keepdims=False).astype(FULL)
    for steps in range(1, size):
        piece = lax.dynamic_index_in_dim(parts, (place + steps) % size, 0, keepdims=False)
        total = total + lax.ppermute(piece, "context", [(i, (i + steps) % size) for i in range(size)]).astype(FULL)
    return total


def context_spread(part):
    size = lax.axis_size("context")
    return [part] + [
        lax.ppermute(part, "context", [(i, (i + steps) % size) for i in range(size)]) for steps in range(1, size)]


def context_sum(part):
    size = lax.axis_size("context")
    total = part.astype(FULL)
    for steps in range(1, size):
        moved = lax.ppermute(part, "context", [(i, (i + steps) % size) for i in range(size)])
        total = total + moved.astype(FULL)
    return total


def pair_other(part):
    size = lax.axis_size("tensor")
    return lax.ppermute(part, "tensor", [(i, (i + 1) % size) for i in range(size)])


def call(body, outs, ins, scratch=(), aliases=None, in_specs=None, out_specs=None, name=None, steps=1):
    return pl.pallas_call(
        body,
        out_shape=outs,
        grid=(steps,),
        in_specs=in_specs,
        out_specs=out_specs,
        scratch_shapes=list(scratch),
        input_output_aliases=aliases or {},
        compiler_params=pltpu.CompilerParams(vmem_limit_bytes=58 * 2**20),
        name=name,
    )(*ins)


def whole():
    return pl.BlockSpec(memory_space=pltpu.VMEM)


def scalars():
    return pl.BlockSpec(memory_space=pltpu.SMEM)


def shape(dims, dtype):
    return jax.ShapeDtypeStruct(dims, dtype)


def weight_spec(depth, cols, index):
    return pl.BlockSpec((depth, cols), lambda *_: (0, index))


def norm_stats(stream):
    center = stream - jnp.mean(stream, axis=-1, keepdims=True)
    spread = lax.rsqrt(jnp.mean(center * center, axis=-1, keepdims=True) + EPS)
    return center * spread, spread


def enter_kernel(has_parts, place, *refs):
    if has_parts:
        middle, mine, other, offset_last, gain, offset, stream_out, attend_out, half_out = refs
        stream = middle[...] + (mine[...] + other[...]) + offset_last[...]
        stream_out[...] = stream
    else:
        stream_in, gain, offset, attend_out, half_out = refs
        stream = stream_in[...]
    normed, _ = norm_stats(stream)
    attend = (normed * gain[...] + offset[...]).astype(HALF)
    attend_out[...] = attend
    cols = half_out.shape[1]
    half_out[...] = jnp.where(place[0] == 0, attend[:, :cols], attend[:, cols:])


def assemble(place, pieces, out):
    count, cols = len(pieces), pieces[0].shape[1]
    for index, piece in enumerate(pieces):
        source = lax.rem(place[1] + count - index, count)
        out[:, pl.ds(pl.multiple_of(source * cols, cols), cols)] = piece[...]


def attend_first_kernel(count, place, *refs):
    pieces, rest, weights = refs[:count], refs[count:-1], refs[-1]
    assemble(place, pieces, weights)
    attend_kernel(place, *rest[:5], weights, *rest[5:])


def attend_kernel(place, own, far_mine, near_mine, far_other, near_other, weights, bias, visible,
                  query_out, key_out, value_out, attended_out, log_out, wide_out, part_out):
    tokens, width = own.shape
    rows, block, keys = visible.shape
    cols = query_out.shape[1]
    half = far_mine.shape[2]
    wide_out[:, keys - block:, :] = own[...].reshape(rows, block, width)

    def put(first, mine, other):
        mine, other = mine[...], other[...]
        low = place[0] == 0
        wide_out[:, first:first + block, :half] = jnp.where(low, mine, other)
        wide_out[:, first:first + block, half:] = jnp.where(low, other, mine)

    put(0, far_mine, far_other)
    put(block, near_mine, near_other)
    query_out[...] = (dot(own[...], weights[:, :cols], 1, 0) + bias[0:1, :]).astype(HALF)
    wide = wide_out[...].reshape(rows * keys, width)
    key_out[...] = dot(wide, weights[:, cols:2 * cols], 1, 0).astype(HALF).reshape(rows, keys, cols)
    value_out[...] = (dot(wide, weights[:, 2 * cols:3 * cols], 1, 0) + bias[1:2, :]).astype(HALF).reshape(rows, keys, cols)
    scale = HEAD ** (-0.5)
    pairs = cols // 128
    low_lane = lax.broadcasted_iota(jnp.int32, (block, 128), 1) < HEAD
    lane = lax.broadcasted_iota(jnp.int32, (block, 128), 1)
    log_out[...] = jnp.zeros(log_out.shape, FULL)

    def one(step, carry):
        row, pair = step // pairs, step % pairs
        at_rows = pl.ds(pl.multiple_of(row * block, block), block)
        at_cols = pl.ds(pl.multiple_of(pair * 128, 128), 128)
        query = query_out[at_rows, at_cols]
        key = key_out[row, :, at_cols]
        value = value_out[row, :, at_cols]
        shown = visible[row] > 0
        outs = []
        logs = log_out[at_rows, :]
        for which in range(2):
            picked = jnp.where(low_lane if which == 0 else ~low_lane, query, jnp.zeros_like(query))
            scores = jnp.where(shown, dot(picked, key, 1, 1) * scale, MASKED)
            top = jnp.max(scores, axis=-1, keepdims=True)
            grown = jnp.exp(scores - top)
            total = jnp.sum(grown, axis=-1, keepdims=True)
            logs = jnp.where(lane == 2 * pair + which, top + jnp.log(total), logs)
            soft = (grown * (1.0 / total)).astype(HALF)
            outs.append(dot(soft, value, 1, 0))
        log_out[at_rows, :] = logs
        attended_out[at_rows, at_cols] = jnp.where(low_lane, outs[0], outs[1]).astype(HALF)
        return carry

    lax.fori_loop(0, rows * pairs, one, 0)
    part_out[...] = dot(attended_out[...], weights[:, 3 * cols:4 * cols], 1, 1)


def feed_kernel(stream, mine, other, offset_mid, gain, offset, up, hidden_bias, down,
                middle_out, preact_out, part_out, active):
    middle = stream[...] + (mine[...] + other[...]) + offset_mid[...]
    middle_out[...] = middle
    normed, _ = norm_stats(middle)
    feed = (normed * gain[...] + offset[...]).astype(HALF)
    preact_out[...] = dot(feed, up[...], 1, 0) + hidden_bias[...]
    step_rows = 32

    def one(step, carry):
        at = pl.ds(pl.multiple_of(step * step_rows, step_rows), step_rows)
        active[at, :] = gelu_value(preact_out[at, :]).astype(HALF)
        return carry

    lax.fori_loop(0, preact_out.shape[0] // step_rows, one, 0)
    part_out[...] = dot(active[...], down[...], 1, 1)


def leave_norm(place, middle_back, stream, mine, other, gain):
    low = place[0] == 0
    mine, other = mine[...], other[...]
    back = jnp.concatenate([jnp.where(low, mine, other), jnp.where(low, other, mine)], axis=1)
    normed, spread = norm_stats(stream[...])
    upstream = middle_back[...] + norm_backward(back, normed, spread, gain[...])
    sums = jnp.concatenate(
        [jnp.sum(back * normed, axis=0, keepdims=True), jnp.sum(back, axis=0, keepdims=True)], axis=0)
    return upstream, sums


def leave_kernel(place, middle_back, stream, mine, other, gain, upstream_out, sums_out):
    upstream, sums = leave_norm(place, middle_back, stream, mine, other, gain)
    upstream_out[...] = upstream
    sums_out[...] = sums


def feed_back_kernel(has_leave, *refs):
    if has_leave:
        place, middle_back, stream, mine, other, gain_one = refs[:6]
        middle, preact, gain, offset, up, down, _ = refs[6:13]
        upstream_out, sums_out, pack, hidden_sum, down_sum, part_out, active, hidden_half = refs[13:]
        upstream, sums = leave_norm(place, middle_back, stream, mine, other, gain_one)
        upstream_out[...] = upstream
        sums_out[...] = sums
    else:
        upstream_in, middle, preact, gain, offset, up, down = refs[:7]
        feed_out, hidden_sum, down_sum, part_out, active, hidden_half = refs[7:]
        upstream = upstream_in[...]
    hidden = up.shape[1]
    step_rows = 32
    upstream_half = upstream.astype(HALF)
    down_sum[...] = jnp.sum(upstream, axis=0, keepdims=True)
    normed, _ = norm_stats(middle[...])
    feed = (normed * gain[...] + offset[...]).astype(HALF)
    back = dot(upstream_half, down[...], 1, 0)
    hidden_sum[...] = jnp.zeros(hidden_sum.shape, FULL)
    for first in range(0, upstream.shape[0], step_rows):
        inner = slice(first, first + step_rows)
        pre = preact[inner, :]
        square = pre * pre
        tanh_value = jnp.tanh(GELU_COEF * (pre + GELU_CUBE * square * pre))
        active[inner, :] = (0.5 * pre * (1.0 + tanh_value)).astype(HALF)
        slope = 0.5 * (1.0 + tanh_value) + 0.5 * pre * (1.0 - tanh_value * tanh_value) * GELU_COEF * (
            1.0 + 3.0 * GELU_CUBE * square)
        hidden_back = back[inner, :] * slope
        hidden_sum[...] += jnp.sum(hidden_back, axis=0, keepdims=True)
        hidden_half[inner, :] = hidden_back.astype(HALF)
    part_out[...] = dot(hidden_half[...], up[...], 1, 1).astype(HALF)
    if has_leave:
        grads = (dot(feed, hidden_half[...], 0, 0).astype(HALF), dot(upstream_half, active[...], 0, 0).astype(HALF))
        count, cols = pack.shape[0], pack.shape[2] // 2
        for index, grad in enumerate(grads):
            for side in range(count):
                pack[side, :, index * cols:(index + 1) * cols] = grad[:, side * cols:(side + 1) * cols]
    else:
        feed_out[...] = feed


def attend_grads(middle_half, attended, wide, wide_query, wide_both):
    tokens, cols = wide_query.shape
    rows, keys, width = wide.shape
    own = wide[:, keys - tokens // rows:, :].reshape(tokens, width)
    both = wide_both[...].reshape(rows * keys, 2 * cols)
    query_grad = dot(own, wide_query[...], 0, 0).astype(HALF)
    both_grad = dot(wide[...].reshape(rows * keys, width), both, 0, 0).astype(HALF)
    mix_grad = dot(middle_half, attended[...], 0, 0).astype(HALF)
    return query_grad, both_grad[:, :cols], both_grad[:, cols:], mix_grad


def grads_kernel(upstream, feed, hidden_half, active, middle_back, attended, wide, wide_query, wide_both, pack):
    step = pl.program_id(0)

    def put(grad):
        cols = pack.shape[2]
        for side in range(pack.shape[0]):
            pack[side] = grad[:, side * cols:(side + 1) * cols]

    @pl.when(step == 0)
    def _():
        put(dot(feed[...], hidden_half[...], 0, 0).astype(HALF))

    @pl.when(step == 1)
    def _():
        put(dot(upstream[...].astype(HALF), active[...], 0, 0).astype(HALF))

    @pl.when(step == 2)
    def _():
        middle_half = middle_back[...].astype(HALF)
        for index, grad in enumerate(attend_grads(middle_half, attended, wide, wide_query, wide_both)):
            pack[index] = grad


def attend_back_kernel(spread_pack, place, upstream, middle, mine, other, gain, attended, query, key, value,
                       log_total, visible, wide, weights, *refs):
    if spread_pack:
        pack, middle_out, wide_mine, wide_other, sums_out, heads_out, wide_query, wide_both, near = refs
    else:
        middle_out, wide_mine, wide_other, sums_out, heads_out, wide_query, wide_both, near = refs
    tokens, width = upstream.shape
    rows, block, keys = visible.shape
    cols = query.shape[1]
    scale = HEAD ** (-0.5)
    feed_back = mine[...].astype(FULL) + other[...].astype(FULL)
    normed, spread = norm_stats(middle[...])
    middle_back = upstream[...] + norm_backward(feed_back, normed, spread, gain[...])
    middle_out[...] = middle_back
    sums_out[...] = jnp.concatenate(
        [jnp.sum(feed_back * normed, axis=0, keepdims=True), jnp.sum(feed_back, axis=0, keepdims=True),
         jnp.sum(middle_back, axis=0, keepdims=True)], axis=0)
    middle_half = middle_back.astype(HALF)
    near[...] = dot(middle_half, weights[:, 3 * cols:4 * cols], 1, 0).astype(HALF)
    pairs = cols // 128
    low_lane = lax.broadcasted_iota(jnp.int32, (block, 128), 1) < HEAD
    low_key = lax.broadcasted_iota(jnp.int32, (keys, 128), 1) < HEAD
    lane = lax.broadcasted_iota(jnp.int32, (block, 128), 1)
    heads_out[...] = jnp.zeros(heads_out.shape, FULL)

    def one(step, carry):
        row, pair = step // pairs, step % pairs
        at_rows = pl.ds(pl.multiple_of(row * block, block), block)
        at_cols = pl.ds(pl.multiple_of(pair * 128, 128), 128)
        at_values = pl.ds(pl.multiple_of(cols + pair * 128, 128), 128)
        query_two = query[at_rows, at_cols]
        key_two, value_two = key[row, :, at_cols], value[row, :, at_cols]
        back_two = near[at_rows, at_cols]
        product = back_two.astype(FULL) * attended[at_rows, at_cols].astype(FULL)
        shown = visible[row] > 0
        logs = log_total[at_rows, :]
        query_parts, key_parts, value_parts = [], [], []
        for which in range(2):
            lanes = low_lane if which == 0 else ~low_lane
            picked = jnp.where(lanes, query_two, jnp.zeros_like(query_two))
            picked_back = jnp.where(lanes, back_two, jnp.zeros_like(back_two))
            delta = jnp.sum(jnp.where(lanes, product, 0.0), axis=-1, keepdims=True)
            own_log = jnp.sum(jnp.where(lane == 2 * pair + which, logs, 0.0), axis=-1, keepdims=True)
            scores = jnp.where(shown, dot(picked, key_two, 1, 1) * scale, MASKED)
            soft = jnp.exp(scores - own_log)
            score_back = (soft * (dot(picked_back, value_two, 1, 1) - delta) * scale).astype(HALF)
            query_parts.append(dot(score_back, key_two, 1, 0))
            key_parts.append(dot(score_back, query_two, 0, 0))
            value_parts.append(dot(soft.astype(HALF), back_two, 0, 0))
        query_back = jnp.where(low_lane, query_parts[0], query_parts[1])
        key_back = jnp.where(low_key, key_parts[0], key_parts[1])
        value_back = jnp.where(low_key, value_parts[0], value_parts[1])
        heads_out[0:1, at_cols] += jnp.sum(query_back, axis=0, keepdims=True)
        heads_out[1:2, at_cols] += jnp.sum(value_back, axis=0, keepdims=True)
        wide_query[at_rows, at_cols] = query_back.astype(HALF)
        wide_both[row, :, at_cols] = key_back.astype(HALF)
        wide_both[row, :, at_values] = value_back.astype(HALF)
        return carry

    lax.fori_loop(0, rows * pairs, one, 0)
    both = wide_both[...].reshape(rows * keys, 2 * cols)
    if spread_pack:
        for index, grad in enumerate(attend_grads(middle_half, attended, wide, wide_query, wide_both)):
            pack[index] = grad
    wide_back = dot(both, weights[:, cols:3 * cols], 1, 1).reshape(rows, keys, width)
    own_back = dot(wide_query[...], weights[:, :cols], 1, 1).reshape(rows, block, width)
    half = width // 2
    low = place[0] == 0

    def put(first, count, values):
        wide_mine[:, first:first + count, :] = jnp.where(low, values[..., :half], values[..., half:])
        wide_other[:, first:first + count, :] = jnp.where(low, values[..., half:], values[..., :half]).astype(HALF)

    put(0, keys - block, wide_back[:, :keys - block])
    put(keys - block, block, wide_back[:, keys - block:] + own_back)


def per_device(
    inputs,
    segment_ids,
    projection,
    head_bias,
    mixing,
    expansion,
    hidden_bias,
    contraction,
    norm_gains,
    offsets,
    cotangent,
):
    layers = projection.shape[0]
    rows, block, width = inputs.shape
    shards = lax.axis_size("shard")
    contexts = lax.axis_size("context")
    own = projection.shape[2]
    heads = head_bias.shape[2]
    head_cols = projection.shape[3]
    hidden = expansion.shape[2]
    tokens = rows * block
    head_scale = HEAD ** (-0.5)
    back_steps = 2

    def attend_block(layer):
        return [projection[layer, 0], projection[layer, 1], projection[layer, 2], mixing[layer].T]

    others = [expansion[0], contraction[0].T]
    for layer in range(1, layers):
        others += attend_block(layer) + [expansion[layer], contraction[layer].T]
    gathered = lax.all_gather(jnp.concatenate(others, axis=1), "shard", axis=0, tiled=True)
    small_parts = [norm_gains, offsets, head_bias, hidden_bias]
    small_sizes = [part.size for part in small_parts]
    small_total = sum(small_sizes)
    small_padded = -(-small_total // 1024) * 1024
    small_rows = small_padded // 128
    small = jnp.concatenate([part.reshape(-1) for part in small_parts] + [jnp.zeros((own * 128 - small_total,), HALF)])
    turn = lax.axis_index("context")
    quarter_cols = 4 * head_cols // contexts
    first = jnp.concatenate([
        lax.dynamic_slice_in_dim(jnp.concatenate(attend_block(0), axis=1), turn * quarter_cols, quarter_cols, 1),
        small.reshape(own, 128)], axis=1)
    first = lax.all_to_all(jnp.broadcast_to(first[None], (shards,) + first.shape), "shard", 0, 0)
    small = first[:, :small_rows, first.shape[2] - 128:].reshape(shards, small_padded)
    attend_pieces = context_spread(first.reshape(shards * own, -1)[:, :quarter_cols])

    def widen(index):
        start = sum(small_sizes[:index])
        shape = small_parts[index].shape
        piece = small[:, start:start + small_sizes[index]].astype(FULL).reshape((shards,) + shape)
        piece = jnp.moveaxis(piece, 0, -2)
        return piece.reshape(shape[:-1] + (shards * shape[-1],))

    gains_all, offsets_all = widen(0), widen(1)
    head_all = widen(2).reshape(layers, 2, head_cols)
    hidden_all = widen(3).reshape(layers, hidden)

    seg_before = [from_before(segment_ids, steps) for steps in range(back_steps, 0, -1)]
    segments_all = jnp.concatenate(seg_before + [segment_ids], axis=1)
    query_pos = jnp.arange(block, dtype=jnp.int32) + back_steps * block
    key_pos = jnp.arange((back_steps + 1) * block, dtype=jnp.int32)
    first_key = (back_steps - lax.axis_index("context")) * block
    visible = (segments_all[:, None, :] == segment_ids[:, :, None]) & (
        key_pos[None, None, :] <= query_pos[None, :, None]
    ) & (key_pos >= first_key)[None, None, :]

    mask = visible.astype(FULL)
    keys = (back_steps + 1) * block
    half = width // 2
    place = jnp.stack([lax.axis_index("tensor"), turn]).astype(jnp.int32)
    side_cols = 4 * head_cols

    def row_of(table, layer, index):
        return table[layer, index].reshape(1, -1)

    def gathered_spec(layer, member):
        at = member if layer == 0 else 2 + 3 * (layer - 1) + member
        return weight_spec(width, side_cols, at)

    vmem = whole()
    stream = inputs.reshape(tokens, width)
    kept = []
    parts = ()
    middle = None
    for layer in range(layers):
        outs = [shape((tokens, width), HALF), shape((tokens, half), HALF)]
        gain_row, offset_row = row_of(gains_all, layer, 0), row_of(offsets_all, layer, 0)
        if layer == 0:
            attend_input, sent = call(
                functools.partial(enter_kernel, False), outs, (place, stream, gain_row, offset_row),
                in_specs=[scalars()] + [vmem] * 3, out_specs=[vmem] * 2, name="enter_first")
        else:
            stream, attend_input, sent = call(
                functools.partial(enter_kernel, True), [shape((tokens, width), FULL)] + outs,
                (place, middle) + parts + (row_of(offsets_all, layer - 1, 3), gain_row, offset_row),
                in_specs=[scalars()] + [vmem] * 6, out_specs=[vmem] * 3, name="enter")
        sent = sent.reshape(rows, block, half)
        far, near = from_before(sent, 2), from_before(sent, 1)
        far_other, near_other = pair_other(far), pair_other(near)
        attend_outs = [
            shape((tokens, head_cols), HALF), shape((rows, keys, head_cols), HALF), shape((rows, keys, head_cols), HALF),
            shape((tokens, head_cols), HALF), shape((tokens, 128), FULL), shape((rows, keys, width), HALF),
            shape((tokens, width), FULL)]
        attend_args = (attend_input, far, near, far_other, near_other)
        if layer == 0:
            query, key, value, attended, log_total, wide, part, weights = call(
                functools.partial(attend_first_kernel, contexts), attend_outs + [shape((width, side_cols), HALF)],
                (place,) + tuple(attend_pieces) + attend_args + (head_all[layer], mask),
                in_specs=[scalars()] + [vmem] * (contexts + 7), out_specs=[vmem] * 8, name="attend_first")
            held = (weights, gathered, gathered)
            specs = (vmem, gathered_spec(0, 0), gathered_spec(0, 1))
        else:
            held = (gathered,) * 3
            specs = tuple(gathered_spec(layer, member) for member in range(3))
            query, key, value, attended, log_total, wide, part = call(
                attend_kernel, attend_outs, (place,) + attend_args + (held[0], head_all[layer], mask),
                in_specs=[scalars()] + [vmem] * 5 + [specs[0]] + [vmem] * 2, out_specs=[vmem] * 7, name="attend")
        before = stream
        middle, preact, part = call(
            feed_kernel,
            [shape((tokens, width), FULL), shape((tokens, hidden), FULL), shape((tokens, width), FULL)],
            (stream, part, pair_other(part), row_of(offsets_all, layer, 2), row_of(gains_all, layer, 1),
             row_of(offsets_all, layer, 1), held[1], hidden_all[layer].reshape(1, -1), held[2]),
            scratch=[pltpu.VMEM((tokens, hidden), HALF)],
            in_specs=[vmem] * 6 + [specs[1], vmem, specs[2]], out_specs=[vmem] * 3, name="feed")
        parts = (part, pair_other(part))
        kept.append((before, query, key, value, attended, log_total, wide, middle, preact, held, specs))
    stream = middle + (parts[0] + parts[1]) + offsets_all[layers - 1, 3]

    quarter_hidden = hidden // contexts
    pack_shape = shape((contexts, width, layers * 2 * quarter_hidden + (layers - 1) * quarter_cols), HALF)
    vectors = [None] * layers
    leave = None
    packed = None
    unread = pl.BlockSpec(memory_space=pl.ANY)
    for layer in reversed(range(layers)):
        before, query, key, value, attended, log_total, wide, middle, preact, held, specs = kept[layer]
        last = layer == layers - 1
        feed_pack_spec = pl.BlockSpec((contexts, width, 2 * quarter_hidden), functools.partial(lambda at, *_: (0, 0, at), layer))
        shared = (middle, preact, row_of(gains_all, layer, 1), row_of(offsets_all, layer, 1), held[1], held[2])
        shared_specs = [vmem] * 4 + [specs[1], specs[2]]
        outs = [pack_shape, shape((1, hidden), FULL), shape((1, width), FULL), shape((tokens, width), HALF)]
        outs_specs = [feed_pack_spec] + [vmem] * 3
        scratch = [pltpu.VMEM((tokens, hidden), HALF)] * 2
        if last:
            upstream = cotangent.reshape(tokens, width)
            feed_held, hidden_sum, down_sum, part, active, hidden_half = call(
                functools.partial(feed_back_kernel, False),
                [shape((tokens, width), HALF)] + outs[1:] + [shape((tokens, hidden), HALF)] * 2, (upstream,) + shared,
                in_specs=[vmem] + shared_specs, out_specs=[vmem] * 6, name="feed_back_last")
        else:
            operands = leave + shared
            upstream, leave_sums, packed, hidden_sum, down_sum, part = call(
                functools.partial(feed_back_kernel, True),
                [shape((tokens, width), FULL), shape((2, width), FULL)] + outs, operands + (packed,), scratch=scratch,
                aliases={len(operands): 2},
                in_specs=[scalars()] + [vmem] * 5 + shared_specs + [unread], out_specs=[vmem] * 2 + outs_specs, name="feed_back")
            vectors[layer + 1] = (leave_sums,) + vectors[layer + 1]
        if layer == 0:
            share = lax.psum_scatter(packed, "shard", scatter_dimension=1, tiled=True)
            attend_pack = shape((contexts, width, side_cols // contexts), HALF)
            attend_pack_spec = vmem
        operands = (place, upstream, middle, part, pair_other(part), row_of(gains_all, layer, 1), attended,
                    query, key, value, log_total, mask, wide, held[0])
        attend_outs = [
            shape((tokens, width), FULL), shape((rows, keys, half), FULL), shape((rows, keys, half), HALF),
            shape((3, width), FULL), shape((2, head_cols), FULL)]
        spare = [((tokens, head_cols), HALF), ((rows, keys, 2 * head_cols), HALF), ((tokens, head_cols), HALF)]
        attend_specs = [scalars()] + [vmem] * 12 + [specs[0]]
        if layer == 0:
            attend_packed, middle_back, wide_mine, wide_other, sums, head_sums = call(
                functools.partial(attend_back_kernel, True), [attend_pack] + attend_outs, operands,
                scratch=[pltpu.VMEM(*entry) for entry in spare], in_specs=attend_specs,
                out_specs=[attend_pack_spec] + [vmem] * 5, name="attend_back")
            attend_quarter = context_share(attend_packed).astype(HALF)
        else:
            middle_back, wide_mine, wide_other, sums, head_sums, wide_query, wide_both = call(
                functools.partial(attend_back_kernel, False), attend_outs + [shape(*entry) for entry in spare[:2]], operands,
                scratch=[pltpu.VMEM(*spare[2])], in_specs=attend_specs, out_specs=[vmem] * 7, name="attend_back_last")
            packed = call(
                grads_kernel, pack_shape,
                (upstream, feed_held, hidden_half, active, middle_back, attended, wide, wide_query, wide_both),
                in_specs=[vmem] * 9, out_specs=pl.BlockSpec((contexts, width, quarter_cols), lambda step: (0, 0, 2 * (layers - 1) + step)),
                name="grads_last", steps=3)
        wide_sum = wide_mine + pair_other(wide_other).astype(FULL)
        half_back = wide_sum[:, back_steps * block:]
        returned = []
        for steps in range(1, back_steps + 1):
            start = (back_steps - steps) * block
            returned.append(from_after(wide_sum[:, start:start + block].astype(HALF), steps))
        if last:
            returned, packed = lax.optimization_barrier((returned, packed))
        for piece in returned:
            half_back = half_back + piece.astype(FULL)
        half_back = half_back.reshape(tokens, half)
        leave = (place, middle_back, before, half_back, pair_other(half_back), row_of(gains_all, layer, 0))
        vectors[layer] = (sums, down_sum, head_sums, hidden_sum)
    upstream, leave_sums = call(
        leave_kernel, [shape((tokens, width), FULL), shape((2, width), FULL)], leave,
        in_specs=[scalars()] + [vmem] * 5, out_specs=[vmem] * 2, name="leave")
    vectors[0] = (leave_sums,) + vectors[0]

    def spread_out(values, shape):
        lead = shape[:-1]
        values = values.reshape(lead + (shards, shape[-1]))
        return jnp.moveaxis(values, -2, 0).reshape(shards, -1)

    gain_sums = jnp.stack([jnp.stack([entry[0][0], entry[1][0]]) for entry in vectors])
    offset_sums = jnp.stack([jnp.concatenate([entry[0][1:2], entry[1][1:], entry[2]]) for entry in vectors])
    head_sums = jnp.stack([entry[3] for entry in vectors])
    hidden_sums = jnp.stack([entry[4] for entry in vectors])
    vector_pack = jnp.concatenate(
        [spread_out(values, part.shape) for values, part in zip((gain_sums, offset_sums, head_sums, hidden_sums), small_parts)]
        + [jnp.zeros((shards, small_padded - small_total), FULL)], axis=1)
    vector_pack = context_sum(vector_pack.reshape(shards * small_rows, 128)).astype(HALF)
    vector_pack = jnp.pad(vector_pack.reshape(shards, small_rows, 128), ((0, 0), (0, own - small_rows), (0, 0)))
    final = jnp.concatenate([attend_quarter.reshape(shards, own, -1), vector_pack], axis=2)
    final = jnp.sum(lax.all_to_all(final, "shard", 0, 0).astype(FULL), axis=0)
    attend_sum = final[:, :side_cols // contexts].astype(HALF)
    vector_own = final[:small_rows, side_cols // contexts:].reshape(-1)
    vector_out = []
    for index, part in enumerate(small_parts):
        start = sum(small_sizes[:index])
        vector_out.append(vector_own[start:start + small_sizes[index]].reshape(part.shape))
    gains_grad, offsets_grad, head_grad, hidden_grad = vector_out

    share = jnp.sum(lax.all_to_all(share, "context", 0, 0).astype(FULL), axis=0).astype(HALF)
    quarters = lax.all_gather(jnp.concatenate([share, attend_sum], axis=1), "context", axis=0, tiled=False).astype(FULL)
    share_cols = share.shape[1]

    def join(piece):
        return jnp.moveaxis(piece, 0, 1).reshape(own, -1)

    attend_own = [join(quarters[:, :, share_cols:])]
    up_own, down_own = [], []
    for layer in range(layers):
        start = 2 * quarter_hidden * layer
        up_own.append(join(quarters[:, :, start:start + quarter_hidden]))
        down_own.append(join(quarters[:, :, start + quarter_hidden:start + 2 * quarter_hidden]))
    for layer in range(1, layers):
        start = 2 * quarter_hidden * layers + quarter_cols * (layer - 1)
        attend_own.append(join(quarters[:, :, start:start + quarter_cols]))
    projection_grad = jnp.stack(
        [jnp.stack([share[:, k * head_cols:(k + 1) * head_cols] for k in range(3)]) for share in attend_own])
    mixing_grad = jnp.stack([share[:, 3 * head_cols:].T for share in attend_own])
    expansion_grad = jnp.stack(up_own)
    contraction_grad = jnp.stack([share.T for share in down_own])
    return (
        stream.reshape(rows, block, width),
        upstream.reshape(rows, block, width),
        projection_grad,
        head_grad,
        mixing_grad,
        expansion_grad,
        hidden_grad,
        contraction_grad,
        gains_grad,
        offsets_grad,
    )


def solution(mesh):
    in_specs = (
        P("shard", "context", None),
        P("shard", "context"),
        P(None, None, "shard", "tensor"),
        P(None, None, "tensor", "shard"),
        P(None, "tensor", "shard"),
        P(None, "shard", "tensor"),
        P(None, "tensor", "shard"),
        P(None, "tensor", "shard"),
        P(None, None, "shard"),
        P(None, None, "shard"),
        P("shard", "context", None),
    )
    out_specs = (
        P("shard", "context", None),
        P("shard", "context", None),
        P(None, None, "shard", "tensor"),
        P(None, None, "tensor", "shard"),
        P(None, "tensor", "shard"),
        P(None, "shard", "tensor"),
        P(None, "tensor", "shard"),
        P(None, "tensor", "shard"),
        P(None, None, "shard"),
        P(None, None, "shard"),
    )
    return jax.shard_map(
        per_device, mesh=mesh, in_specs=in_specs, out_specs=out_specs, check_vma=False
    )
```

```python
import functools

import jax
import jax.numpy as jnp
from jax import lax
from jax.experimental import pallas as pl
from jax.experimental.pallas import tpu as pltpu
from jax.sharding import PartitionSpec as P

HEAD = 64

EPS = 1e-05
GELU_COEF = 0.7978845608028654
GELU_CUBE = 0.044715
MASKED = -1e30
HALF = jnp.bfloat16
FULL = jnp.float32


def gelu_value(preact):
    inner_arg = GELU_COEF * (preact + GELU_CUBE * preact * preact * preact)
    return 0.5 * preact * (1.0 + jnp.tanh(inner_arg))


def norm_backward(upstream, normed, spread, gain_row):
    scaled = upstream * gain_row
    first_mean = jnp.mean(scaled, axis=-1, keepdims=True)
    second_mean = jnp.mean(scaled * normed, axis=-1, keepdims=True)
    return spread * (scaled - first_mean - normed * second_mean)


def dot(left, right, left_dim, right_dim):
    return lax.dot_general(
        left, right, (((left_dim,), (right_dim,)), ((), ())), preferred_element_type=FULL
    )


def from_before(block, steps):
    size = lax.axis_size("context")
    return lax.ppermute(block, "context", [(i, i + steps) for i in range(size - steps)])


def from_after(block, steps):
    size = lax.axis_size("context")
    return lax.ppermute(block, "context", [(i + steps, i) for i in range(size - steps)])


def context_share(parts):
    size = lax.axis_size("context")
    place = lax.axis_index("context")
    total = lax.dynamic_index_in_dim(parts, place, 0, keepdims=False).astype(FULL)
    for steps in range(1, size):
        piece = lax.dynamic_index_in_dim(parts, (place + steps) % size, 0, keepdims=False)
        total = total + lax.ppermute(piece, "context", [(i, (i + steps) % size) for i in range(size)]).astype(FULL)
    return total


def context_spread(part):
    size = lax.axis_size("context")
    return [part] + [
        lax.ppermute(part, "context", [(i, (i + steps) % size) for i in range(size)]) for steps in range(1, size)]


def context_sum(part):
    size = lax.axis_size("context")
    total = part.astype(FULL)
    for steps in range(1, size):
        moved = lax.ppermute(part, "context", [(i, (i + steps) % size) for i in range(size)])
        total = total + moved.astype(FULL)
    return total


def pair_other(part):
    size = lax.axis_size("tensor")
    return lax.ppermute(part, "tensor", [(i, (i + 1) % size) for i in range(size)])


def call(body, outs, ins, scratch=(), aliases=None, in_specs=None, out_specs=None, name=None, steps=1):
    return pl.pallas_call(
        body,
        out_shape=outs,
        grid=(steps,),
        in_specs=in_specs,
        out_specs=out_specs,
        scratch_shapes=list(scratch),
        input_output_aliases=aliases or {},
        compiler_params=pltpu.CompilerParams(vmem_limit_bytes=58 * 2**20),
        name=name,
    )(*ins)


def whole():
    return pl.BlockSpec(memory_space=pltpu.VMEM)


def scalars():
    return pl.BlockSpec(memory_space=pltpu.SMEM)


def shape(dims, dtype):
    return jax.ShapeDtypeStruct(dims, dtype)


def weight_spec(depth, cols, index):
    return pl.BlockSpec((depth, cols), lambda *_: (0, index))


def norm_stats(stream):
    center = stream - jnp.mean(stream, axis=-1, keepdims=True)
    spread = lax.rsqrt(jnp.mean(center * center, axis=-1, keepdims=True) + EPS)
    return center * spread, spread


def pack_kernel(projection, mixing, expansion, contraction, out):
    layers, hidden, cols = expansion.shape[0], expansion.shape[2], mixing.shape[2]
    start = 0
    for layer in range(layers):
        if layer:
            for index in range(3):
                out[:, start + index * cols:start + (index + 1) * cols] = projection[layer, index]
            out[:, start + 3 * cols:start + 4 * cols] = mixing[layer]
            start += 4 * cols
        out[:, start:start + hidden] = expansion[layer]
        out[:, start + hidden:start + 2 * hidden] = contraction[layer]
        start += 2 * hidden


def enter_kernel(has_parts, place, *refs):
    if has_parts:
        middle, mine, other, offset_last, gain, offset, stream_out, attend_out, half_out = refs
        stream = middle[...] + (mine[...] + other[...]) + offset_last[...]
        stream_out[...] = stream
    else:
        stream_in, gain, offset, attend_out, half_out = refs
        stream = stream_in[...]
    normed, _ = norm_stats(stream)
    attend = (normed * gain[...] + offset[...]).astype(HALF)
    attend_out[...] = attend
    cols = half_out.shape[1]
    half_out[...] = jnp.where(place[0] == 0, attend[:, :cols], attend[:, cols:])


def assemble(place, pieces, out):
    count, cols = len(pieces), pieces[0].shape[1]
    for index, piece in enumerate(pieces):
        source = lax.rem(place[1] + count - index, count)
        out[:, pl.ds(pl.multiple_of(source * cols, cols), cols)] = piece[...]


def attend_first_kernel(count, place, *refs):
    pieces, rest, weights = refs[:count], refs[count:-1], refs[-1]
    assemble(place, pieces, weights)
    attend_kernel(place, *rest[:5], weights, *rest[5:])


def attend_kernel(place, own, far_mine, near_mine, far_other, near_other, weights, bias, visible,
                  query_out, key_out, value_out, attended_out, log_out, wide_out, part_out):
    tokens, width = own.shape
    rows, block, keys = visible.shape
    cols = query_out.shape[1]
    half = far_mine.shape[2]
    wide_out[:, keys - block:, :] = own[...].reshape(rows, block, width)

    def put(first, mine, other):
        mine, other = mine[...], other[...]
        low = place[0] == 0
        wide_out[:, first:first + block, :half] = jnp.where(low, mine, other)
        wide_out[:, first:first + block, half:] = jnp.where(low, other, mine)

    put(0, far_mine, far_other)
    put(block, near_mine, near_other)
    query_out[...] = (dot(own[...], weights[:, :cols], 1, 0) + bias[0:1, :]).astype(HALF)
    wide = wide_out[...].reshape(rows * keys, width)
    key_out[...] = dot(wide, weights[:, cols:2 * cols], 1, 0).astype(HALF).reshape(rows, keys, cols)
    value_out[...] = (dot(wide, weights[:, 2 * cols:3 * cols], 1, 0) + bias[1:2, :]).astype(HALF).reshape(rows, keys, cols)
    scale = HEAD ** (-0.5)
    pairs = cols // 128
    low_lane = lax.broadcasted_iota(jnp.int32, (block, 128), 1) < HEAD
    lane = lax.broadcasted_iota(jnp.int32, (block, 128), 1)
    log_out[...] = jnp.zeros(log_out.shape, FULL)

    def one(step, carry):
        row, pair = step // pairs, step % pairs
        at_rows = pl.ds(pl.multiple_of(row * block, block), block)
        at_cols = pl.ds(pl.multiple_of(pair * 128, 128), 128)
        query = query_out[at_rows, at_cols]
        key = key_out[row, :, at_cols]
        value = value_out[row, :, at_cols]
        shown = visible[row] > 0
        outs = []
        logs = log_out[at_rows, :]
        for which in range(2):
            picked = jnp.where(low_lane if which == 0 else ~low_lane, query, jnp.zeros_like(query))
            scores = jnp.where(shown, dot(picked, key, 1, 1) * scale, MASKED)
            top = jnp.max(scores, axis=-1, keepdims=True)
            grown = jnp.exp(scores - top)
            total = jnp.sum(grown, axis=-1, keepdims=True)
            logs = jnp.where(lane == 2 * pair + which, top + jnp.log(total), logs)
            soft = (grown * (1.0 / total)).astype(HALF)
            outs.append(dot(soft, value, 1, 0))
        log_out[at_rows, :] = logs
        attended_out[at_rows, at_cols] = jnp.where(low_lane, outs[0], outs[1]).astype(HALF)
        return carry

    lax.fori_loop(0, rows * pairs, one, 0)
    part_out[...] = dot(attended_out[...], weights[:, 3 * cols:4 * cols], 1, 1)


def feed_kernel(stream, mine, other, offset_mid, gain, offset, up, hidden_bias, down,
                middle_out, preact_out, part_out, active):
    middle = stream[...] + (mine[...] + other[...]) + offset_mid[...]
    middle_out[...] = middle
    normed, _ = norm_stats(middle)
    feed = (normed * gain[...] + offset[...]).astype(HALF)
    preact_out[...] = dot(feed, up[...], 1, 0) + hidden_bias[...]
    step_rows = 32

    def one(step, carry):
        at = pl.ds(pl.multiple_of(step * step_rows, step_rows), step_rows)
        active[at, :] = gelu_value(preact_out[at, :]).astype(HALF)
        return carry

    lax.fori_loop(0, preact_out.shape[0] // step_rows, one, 0)
    part_out[...] = dot(active[...], down[...], 1, 1)


def leave_norm(place, middle_back, stream, mine, other, gain):
    low = place[0] == 0
    mine, other = mine[...], other[...]
    back = jnp.concatenate([jnp.where(low, mine, other), jnp.where(low, other, mine)], axis=1)
    normed, spread = norm_stats(stream[...])
    upstream = middle_back[...] + norm_backward(back, normed, spread, gain[...])
    sums = jnp.concatenate(
        [jnp.sum(back * normed, axis=0, keepdims=True), jnp.sum(back, axis=0, keepdims=True)], axis=0)
    return upstream, sums


def leave_kernel(place, middle_back, stream, mine, other, gain, upstream_out, sums_out):
    upstream, sums = leave_norm(place, middle_back, stream, mine, other, gain)
    upstream_out[...] = upstream
    sums_out[...] = sums


def feed_back_kernel(has_leave, *refs):
    if has_leave:
        place, middle_back, stream, mine, other, gain_one = refs[:6]
        middle, preact, gain, offset, up, down, _ = refs[6:13]
        upstream_out, sums_out, pack, hidden_sum, down_sum, part_out, active, hidden_half = refs[13:]
        upstream, sums = leave_norm(place, middle_back, stream, mine, other, gain_one)
        upstream_out[...] = upstream
        sums_out[...] = sums
    else:
        upstream_in, middle, preact, gain, offset, up, down = refs[:7]
        feed_out, hidden_sum, down_sum, part_out, active, hidden_half = refs[7:]
        upstream = upstream_in[...]
    hidden = up.shape[1]
    step_rows = 32
    upstream_half = upstream.astype(HALF)
    down_sum[...] = jnp.sum(upstream, axis=0, keepdims=True)
    normed, _ = norm_stats(middle[...])
    feed = (normed * gain[...] + offset[...]).astype(HALF)
    back = dot(upstream_half, down[...], 1, 0)
    hidden_sum[...] = jnp.zeros(hidden_sum.shape, FULL)
    for first in range(0, upstream.shape[0], step_rows):
        inner = slice(first, first + step_rows)
        pre = preact[inner, :]
        square = pre * pre
        tanh_value = jnp.tanh(GELU_COEF * (pre + GELU_CUBE * square * pre))
        active[inner, :] = (0.5 * pre * (1.0 + tanh_value)).astype(HALF)
        slope = 0.5 * (1.0 + tanh_value) + 0.5 * pre * (1.0 - tanh_value * tanh_value) * GELU_COEF * (
            1.0 + 3.0 * GELU_CUBE * square)
        hidden_back = back[inner, :] * slope
        hidden_sum[...] += jnp.sum(hidden_back, axis=0, keepdims=True)
        hidden_half[inner, :] = hidden_back.astype(HALF)
    part_out[...] = dot(hidden_half[...], up[...], 1, 1).astype(HALF)
    if has_leave:
        grads = (dot(feed, hidden_half[...], 0, 0).astype(HALF), dot(upstream_half, active[...], 0, 0).astype(HALF))
        count, cols = pack.shape[0], pack.shape[2] // 2
        for index, grad in enumerate(grads):
            for side in range(count):
                pack[side, :, index * cols:(index + 1) * cols] = grad[:, side * cols:(side + 1) * cols]
    else:
        feed_out[...] = feed


def attend_grads(middle_half, attended, wide, wide_query, wide_both):
    tokens, cols = wide_query.shape
    rows, keys, width = wide.shape
    own = wide[:, keys - tokens // rows:, :].reshape(tokens, width)
    both = wide_both[...].reshape(rows * keys, 2 * cols)
    query_grad = dot(own, wide_query[...], 0, 0).astype(HALF)
    both_grad = dot(wide[...].reshape(rows * keys, width), both, 0, 0).astype(HALF)
    mix_grad = dot(middle_half, attended[...], 0, 0).astype(HALF)
    return query_grad, both_grad[:, :cols], both_grad[:, cols:], mix_grad


def grads_kernel(upstream, feed, hidden_half, active, middle_back, attended, wide, wide_query, wide_both, pack):
    step = pl.program_id(0)

    def put(grad):
        cols = pack.shape[2]
        for side in range(pack.shape[0]):
            pack[side] = grad[:, side * cols:(side + 1) * cols]

    @pl.when(step == 0)
    def _():
        put(dot(feed[...], hidden_half[...], 0, 0).astype(HALF))

    @pl.when(step == 1)
    def _():
        put(dot(upstream[...].astype(HALF), active[...], 0, 0).astype(HALF))

    @pl.when(step == 2)
    def _():
        middle_half = middle_back[...].astype(HALF)
        for index, grad in enumerate(attend_grads(middle_half, attended, wide, wide_query, wide_both)):
            pack[index] = grad


def attend_back_kernel(spread_pack, place, upstream, middle, mine, other, gain, attended, query, key, value,
                       log_total, visible, wide, weights, *refs):
    if spread_pack:
        pack, middle_out, wide_mine, wide_other, sums_out, heads_out, wide_query, wide_both, near = refs
    else:
        middle_out, wide_mine, wide_other, sums_out, heads_out, wide_query, wide_both, near = refs
    tokens, width = upstream.shape
    rows, block, keys = visible.shape
    cols = query.shape[1]
    scale = HEAD ** (-0.5)
    feed_back = mine[...].astype(FULL) + other[...].astype(FULL)
    normed, spread = norm_stats(middle[...])
    middle_back = upstream[...] + norm_backward(feed_back, normed, spread, gain[...])
    middle_out[...] = middle_back
    sums_out[...] = jnp.concatenate(
        [jnp.sum(feed_back * normed, axis=0, keepdims=True), jnp.sum(feed_back, axis=0, keepdims=True),
         jnp.sum(middle_back, axis=0, keepdims=True)], axis=0)
    middle_half = middle_back.astype(HALF)
    near[...] = dot(middle_half, weights[:, 3 * cols:4 * cols], 1, 0).astype(HALF)
    pairs = cols // 128
    low_lane = lax.broadcasted_iota(jnp.int32, (block, 128), 1) < HEAD
    low_key = lax.broadcasted_iota(jnp.int32, (keys, 128), 1) < HEAD
    lane = lax.broadcasted_iota(jnp.int32, (block, 128), 1)
    heads_out[...] = jnp.zeros(heads_out.shape, FULL)

    def one(step, carry):
        row, pair = step // pairs, step % pairs
        at_rows = pl.ds(pl.multiple_of(row * block, block), block)
        at_cols = pl.ds(pl.multiple_of(pair * 128, 128), 128)
        at_values = pl.ds(pl.multiple_of(cols + pair * 128, 128), 128)
        query_two = query[at_rows, at_cols]
        key_two, value_two = key[row, :, at_cols], value[row, :, at_cols]
        back_two = near[at_rows, at_cols]
        product = back_two.astype(FULL) * attended[at_rows, at_cols].astype(FULL)
        shown = visible[row] > 0
        logs = log_total[at_rows, :]
        query_parts, key_parts, value_parts = [], [], []
        for which in range(2):
            lanes = low_lane if which == 0 else ~low_lane
            picked = jnp.where(lanes, query_two, jnp.zeros_like(query_two))
            picked_back = jnp.where(lanes, back_two, jnp.zeros_like(back_two))
            delta = jnp.sum(jnp.where(lanes, product, 0.0), axis=-1, keepdims=True)
            own_log = jnp.sum(jnp.where(lane == 2 * pair + which, logs, 0.0), axis=-1, keepdims=True)
            scores = jnp.where(shown, dot(picked, key_two, 1, 1) * scale, MASKED)
            soft = jnp.exp(scores - own_log)
            score_back = (soft * (dot(picked_back, value_two, 1, 1) - delta) * scale).astype(HALF)
            query_parts.append(dot(score_back, key_two, 1, 0))
            key_parts.append(dot(score_back, query_two, 0, 0))
            value_parts.append(dot(soft.astype(HALF), back_two, 0, 0))
        query_back = jnp.where(low_lane, query_parts[0], query_parts[1])
        key_back = jnp.where(low_key, key_parts[0], key_parts[1])
        value_back = jnp.where(low_key, value_parts[0], value_parts[1])
        heads_out[0:1, at_cols] += jnp.sum(query_back, axis=0, keepdims=True)
        heads_out[1:2, at_cols] += jnp.sum(value_back, axis=0, keepdims=True)
        wide_query[at_rows, at_cols] = query_back.astype(HALF)
        wide_both[row, :, at_cols] = key_back.astype(HALF)
        wide_both[row, :, at_values] = value_back.astype(HALF)
        return carry

    lax.fori_loop(0, rows * pairs, one, 0)
    both = wide_both[...].reshape(rows * keys, 2 * cols)
    if spread_pack:
        for index, grad in enumerate(attend_grads(middle_half, attended, wide, wide_query, wide_both)):
            pack[index] = grad
    wide_back = dot(both, weights[:, cols:3 * cols], 1, 1).reshape(rows, keys, width)
    own_back = dot(wide_query[...], weights[:, :cols], 1, 1).reshape(rows, block, width)
    half = width // 2
    low = place[0] == 0

    def put(first, count, values):
        wide_mine[:, first:first + count, :] = jnp.where(low, values[..., :half], values[..., half:])
        wide_other[:, first:first + count, :] = jnp.where(low, values[..., half:], values[..., :half]).astype(HALF)

    put(0, keys - block, wide_back[:, :keys - block])
    put(keys - block, block, wide_back[:, keys - block:] + own_back)


def per_device(
    inputs,
    segment_ids,
    projection,
    head_bias,
    mixing,
    expansion,
    hidden_bias,
    contraction,
    norm_gains,
    offsets,
    cotangent,
):
    layers = projection.shape[0]
    rows, block, width = inputs.shape
    shards = lax.axis_size("shard")
    contexts = lax.axis_size("context")
    own = projection.shape[2]
    heads = head_bias.shape[2]
    head_cols = projection.shape[3]
    hidden = expansion.shape[2]
    tokens = rows * block
    head_scale = HEAD ** (-0.5)
    back_steps = 2

    def attend_block(layer):
        return [projection[layer, 0], projection[layer, 1], projection[layer, 2], mixing[layer].T]

    others = call(
        pack_kernel, shape((own, layers * 2 * hidden + (layers - 1) * 4 * head_cols), HALF),
        (projection, mixing.transpose(0, 2, 1), expansion, contraction.transpose(0, 2, 1)),
        in_specs=[whole()] * 4, out_specs=whole(), name="pack")
    gathered = lax.all_gather(others, "shard", axis=0, tiled=True)
    small_parts = [norm_gains, offsets, head_bias, hidden_bias]
    small_sizes = [part.size for part in small_parts]
    small_total = sum(small_sizes)
    small_padded = -(-small_total // 1024) * 1024
    small_rows = small_padded // 128
    small = jnp.concatenate([part.reshape(-1) for part in small_parts] + [jnp.zeros((own * 128 - small_total,), HALF)])
    turn = lax.axis_index("context")
    quarter_cols = 4 * head_cols // contexts
    first = jnp.concatenate([
        lax.dynamic_slice_in_dim(jnp.concatenate(attend_block(0), axis=1), turn * quarter_cols, quarter_cols, 1),
        small.reshape(own, 128)], axis=1)
    first = lax.all_to_all(jnp.broadcast_to(first[None], (shards,) + first.shape), "shard", 0, 0)
    small = first[:, :small_rows, first.shape[2] - 128:].reshape(shards, small_padded)
    attend_pieces = context_spread(first.reshape(shards * own, -1)[:, :quarter_cols])

    def widen(index):
        start = sum(small_sizes[:index])
        shape = small_parts[index].shape
        piece = small[:, start:start + small_sizes[index]].astype(FULL).reshape((shards,) + shape)
        piece = jnp.moveaxis(piece, 0, -2)
        return piece.reshape(shape[:-1] + (shards * shape[-1],))

    gains_all, offsets_all = widen(0), widen(1)
    head_all = widen(2).reshape(layers, 2, head_cols)
    hidden_all = widen(3).reshape(layers, hidden)

    seg_before = [from_before(segment_ids, steps) for steps in range(back_steps, 0, -1)]
    segments_all = jnp.concatenate(seg_before + [segment_ids], axis=1)
    query_pos = jnp.arange(block, dtype=jnp.int32) + back_steps * block
    key_pos = jnp.arange((back_steps + 1) * block, dtype=jnp.int32)
    first_key = (back_steps - lax.axis_index("context")) * block
    visible = (segments_all[:, None, :] == segment_ids[:, :, None]) & (
        key_pos[None, None, :] <= query_pos[None, :, None]
    ) & (key_pos >= first_key)[None, None, :]

    mask = visible.astype(FULL)
    keys = (back_steps + 1) * block
    half = width // 2
    place = jnp.stack([lax.axis_index("tensor"), turn]).astype(jnp.int32)
    side_cols = 4 * head_cols

    def row_of(table, layer, index):
        return table[layer, index].reshape(1, -1)

    def gathered_spec(layer, member):
        at = member if layer == 0 else 2 + 3 * (layer - 1) + member
        return weight_spec(width, side_cols, at)

    vmem = whole()
    stream = inputs.reshape(tokens, width)
    kept = []
    parts = ()
    middle = None
    for layer in range(layers):
        outs = [shape((tokens, width), HALF), shape((tokens, half), HALF)]
        gain_row, offset_row = row_of(gains_all, layer, 0), row_of(offsets_all, layer, 0)
        if layer == 0:
            attend_input, sent = call(
                functools.partial(enter_kernel, False), outs, (place, stream, gain_row, offset_row),
                in_specs=[scalars()] + [vmem] * 3, out_specs=[vmem] * 2, name="enter_first")
        else:
            stream, attend_input, sent = call(
                functools.partial(enter_kernel, True), [shape((tokens, width), FULL)] + outs,
                (place, middle) + parts + (row_of(offsets_all, layer - 1, 3), gain_row, offset_row),
                in_specs=[scalars()] + [vmem] * 6, out_specs=[vmem] * 3, name="enter")
        sent = sent.reshape(rows, block, half)
        far, near = from_before(sent, 2), from_before(sent, 1)
        far_other, near_other = pair_other(far), pair_other(near)
        attend_outs = [
            shape((tokens, head_cols), HALF), shape((rows, keys, head_cols), HALF), shape((rows, keys, head_cols), HALF),
            shape((tokens, head_cols), HALF), shape((tokens, 128), FULL), shape((rows, keys, width), HALF),
            shape((tokens, width), FULL)]
        attend_args = (attend_input, far, near, far_other, near_other)
        if layer == 0:
            query, key, value, attended, log_total, wide, part, weights = call(
                functools.partial(attend_first_kernel, contexts), attend_outs + [shape((width, side_cols), HALF)],
                (place,) + tuple(attend_pieces) + attend_args + (head_all[layer], mask),
                in_specs=[scalars()] + [vmem] * (contexts + 7), out_specs=[vmem] * 8, name="attend_first")
            held = (weights, gathered, gathered)
            specs = (vmem, gathered_spec(0, 0), gathered_spec(0, 1))
        else:
            held = (gathered,) * 3
            specs = tuple(gathered_spec(layer, member) for member in range(3))
            query, key, value, attended, log_total, wide, part = call(
                attend_kernel, attend_outs, (place,) + attend_args + (held[0], head_all[layer], mask),
                in_specs=[scalars()] + [vmem] * 5 + [specs[0]] + [vmem] * 2, out_specs=[vmem] * 7, name="attend")
        before = stream
        middle, preact, part = call(
            feed_kernel,
            [shape((tokens, width), FULL), shape((tokens, hidden), FULL), shape((tokens, width), FULL)],
            (stream, part, pair_other(part), row_of(offsets_all, layer, 2), row_of(gains_all, layer, 1),
             row_of(offsets_all, layer, 1), held[1], hidden_all[layer].reshape(1, -1), held[2]),
            scratch=[pltpu.VMEM((tokens, hidden), HALF)],
            in_specs=[vmem] * 6 + [specs[1], vmem, specs[2]], out_specs=[vmem] * 3, name="feed")
        parts = (part, pair_other(part))
        kept.append((before, query, key, value, attended, log_total, wide, middle, preact, held, specs))
    stream = middle + (parts[0] + parts[1]) + offsets_all[layers - 1, 3]

    quarter_hidden = hidden // contexts
    pack_shape = shape((contexts, width, layers * 2 * quarter_hidden + (layers - 1) * quarter_cols), HALF)
    vectors = [None] * layers
    leave = None
    packed = None
    unread = pl.BlockSpec(memory_space=pl.ANY)
    for layer in reversed(range(layers)):
        before, query, key, value, attended, log_total, wide, middle, preact, held, specs = kept[layer]
        last = layer == layers - 1
        feed_pack_spec = pl.BlockSpec((contexts, width, 2 * quarter_hidden), functools.partial(lambda at, *_: (0, 0, at), layer))
        shared = (middle, preact, row_of(gains_all, layer, 1), row_of(offsets_all, layer, 1), held[1], held[2])
        shared_specs = [vmem] * 4 + [specs[1], specs[2]]
        outs = [pack_shape, shape((1, hidden), FULL), shape((1, width), FULL), shape((tokens, width), HALF)]
        outs_specs = [feed_pack_spec] + [vmem] * 3
        scratch = [pltpu.VMEM((tokens, hidden), HALF)] * 2
        if last:
            upstream = cotangent.reshape(tokens, width)
            feed_held, hidden_sum, down_sum, part, active, hidden_half = call(
                functools.partial(feed_back_kernel, False),
                [shape((tokens, width), HALF)] + outs[1:] + [shape((tokens, hidden), HALF)] * 2, (upstream,) + shared,
                in_specs=[vmem] + shared_specs, out_specs=[vmem] * 6, name="feed_back_last")
        else:
            operands = leave + shared
            upstream, leave_sums, packed, hidden_sum, down_sum, part = call(
                functools.partial(feed_back_kernel, True),
                [shape((tokens, width), FULL), shape((2, width), FULL)] + outs, operands + (packed,), scratch=scratch,
                aliases={len(operands): 2},
                in_specs=[scalars()] + [vmem] * 5 + shared_specs + [unread], out_specs=[vmem] * 2 + outs_specs, name="feed_back")
            vectors[layer + 1] = (leave_sums,) + vectors[layer + 1]
        if layer == 0:
            share = lax.psum_scatter(packed, "shard", scatter_dimension=1, tiled=True)
            attend_pack = shape((contexts, width, side_cols // contexts), HALF)
            attend_pack_spec = vmem
        operands = (place, upstream, middle, part, pair_other(part), row_of(gains_all, layer, 1), attended,
                    query, key, value, log_total, mask, wide, held[0])
        attend_outs = [
            shape((tokens, width), FULL), shape((rows, keys, half), FULL), shape((rows, keys, half), HALF),
            shape((3, width), FULL), shape((2, head_cols), FULL)]
        spare = [((tokens, head_cols), HALF), ((rows, keys, 2 * head_cols), HALF), ((tokens, head_cols), HALF)]
        attend_specs = [scalars()] + [vmem] * 12 + [specs[0]]
        if layer == 0:
            attend_packed, middle_back, wide_mine, wide_other, sums, head_sums = call(
                functools.partial(attend_back_kernel, True), [attend_pack] + attend_outs, operands,
                scratch=[pltpu.VMEM(*entry) for entry in spare], in_specs=attend_specs,
                out_specs=[attend_pack_spec] + [vmem] * 5, name="attend_back")
            attend_quarter = context_share(attend_packed).astype(HALF)
        else:
            middle_back, wide_mine, wide_other, sums, head_sums, wide_query, wide_both = call(
                functools.partial(attend_back_kernel, False), attend_outs + [shape(*entry) for entry in spare[:2]], operands,
                scratch=[pltpu.VMEM(*spare[2])], in_specs=attend_specs, out_specs=[vmem] * 7, name="attend_back_last")
            packed = call(
                grads_kernel, pack_shape,
                (upstream, feed_held, hidden_half, active, middle_back, attended, wide, wide_query, wide_both),
                in_specs=[vmem] * 9, out_specs=pl.BlockSpec((contexts, width, quarter_cols), lambda step: (0, 0, 2 * (layers - 1) + step)),
                name="grads_last", steps=3)
        wide_sum = wide_mine + pair_other(wide_other).astype(FULL)
        half_back = wide_sum[:, back_steps * block:]
        returned = []
        for steps in range(1, back_steps + 1):
            start = (back_steps - steps) * block
            returned.append(from_after(wide_sum[:, start:start + block].astype(HALF), steps))
        if last:
            returned, packed = lax.optimization_barrier((returned, packed))
        for piece in returned:
            half_back = half_back + piece.astype(FULL)
        half_back = half_back.reshape(tokens, half)
        leave = (place, middle_back, before, half_back, pair_other(half_back), row_of(gains_all, layer, 0))
        vectors[layer] = (sums, down_sum, head_sums, hidden_sum)
    upstream, leave_sums = call(
        leave_kernel, [shape((tokens, width), FULL), shape((2, width), FULL)], leave,
        in_specs=[scalars()] + [vmem] * 5, out_specs=[vmem] * 2, name="leave")
    vectors[0] = (leave_sums,) + vectors[0]

    def spread_out(values, shape):
        lead = shape[:-1]
        values = values.reshape(lead + (shards, shape[-1]))
        return jnp.moveaxis(values, -2, 0).reshape(shards, -1)

    gain_sums = jnp.stack([jnp.stack([entry[0][0], entry[1][0]]) for entry in vectors])
    offset_sums = jnp.stack([jnp.concatenate([entry[0][1:2], entry[1][1:], entry[2]]) for entry in vectors])
    head_sums = jnp.stack([entry[3] for entry in vectors])
    hidden_sums = jnp.stack([entry[4] for entry in vectors])
    vector_pack = jnp.concatenate(
        [spread_out(values, part.shape) for values, part in zip((gain_sums, offset_sums, head_sums, hidden_sums), small_parts)]
        + [jnp.zeros((shards, small_padded - small_total), FULL)], axis=1)
    vector_pack = context_sum(vector_pack.reshape(shards * small_rows, 128)).astype(HALF)
    vector_pack = jnp.pad(vector_pack.reshape(shards, small_rows, 128), ((0, 0), (0, own - small_rows), (0, 0)))
    final = jnp.concatenate([attend_quarter.reshape(shards, own, -1), vector_pack], axis=2)
    final = jnp.sum(lax.all_to_all(final, "shard", 0, 0).astype(FULL), axis=0)
    attend_sum = final[:, :side_cols // contexts].astype(HALF)
    vector_own = final[:small_rows, side_cols // contexts:].reshape(-1)
    vector_out = []
    for index, part in enumerate(small_parts):
        start = sum(small_sizes[:index])
        vector_out.append(vector_own[start:start + small_sizes[index]].reshape(part.shape))
    gains_grad, offsets_grad, head_grad, hidden_grad = vector_out

    share = jnp.sum(lax.all_to_all(share, "context", 0, 0).astype(FULL), axis=0).astype(HALF)
    quarters = lax.all_gather(jnp.concatenate([share, attend_sum], axis=1), "context", axis=0, tiled=False).astype(FULL)
    share_cols = share.shape[1]

    def join(piece):
        return jnp.moveaxis(piece, 0, 1).reshape(own, -1)

    attend_own = [join(quarters[:, :, share_cols:])]
    up_own, down_own = [], []
    for layer in range(layers):
        start = 2 * quarter_hidden * layer
        up_own.append(join(quarters[:, :, start:start + quarter_hidden]))
        down_own.append(join(quarters[:, :, start + quarter_hidden:start + 2 * quarter_hidden]))
    for layer in range(1, layers):
        start = 2 * quarter_hidden * layers + quarter_cols * (layer - 1)
        attend_own.append(join(quarters[:, :, start:start + quarter_cols]))
    projection_grad = jnp.stack(
        [jnp.stack([share[:, k * head_cols:(k + 1) * head_cols] for k in range(3)]) for share in attend_own])
    mixing_grad = jnp.stack([share[:, 3 * head_cols:].T for share in attend_own])
    expansion_grad = jnp.stack(up_own)
    contraction_grad = jnp.stack([share.T for share in down_own])
    return (
        stream.reshape(rows, block, width),
        upstream.reshape(rows, block, width),
        projection_grad,
        head_grad,
        mixing_grad,
        expansion_grad,
        hidden_grad,
        contraction_grad,
        gains_grad,
        offsets_grad,
    )


def solution(mesh):
    in_specs = (
        P("shard", "context", None),
        P("shard", "context"),
        P(None, None, "shard", "tensor"),
        P(None, None, "tensor", "shard"),
        P(None, "tensor", "shard"),
        P(None, "shard", "tensor"),
        P(None, "tensor", "shard"),
        P(None, "tensor", "shard"),
        P(None, None, "shard"),
        P(None, None, "shard"),
        P("shard", "context", None),
    )
    out_specs = (
        P("shard", "context", None),
        P("shard", "context", None),
        P(None, None, "shard", "tensor"),
        P(None, None, "tensor", "shard"),
        P(None, "tensor", "shard"),
        P(None, "shard", "tensor"),
        P(None, "tensor", "shard"),
        P(None, "tensor", "shard"),
        P(None, None, "shard"),
        P(None, None, "shard"),
    )
    return jax.shard_map(
        per_device, mesh=mesh, in_specs=in_specs, out_specs=out_specs, check_vma=False
    )
```
